32 devices in a mesh: runs: 2 (over y), tile: 4 (over z), layer: 2 (over x), star: 2 (over core).
Axes of the slice: x: 2, y: 2, z: 4, core: 2. Of those that a mesh axis runs over, the one named last changes fastest.
Arguments:
- screens: float32 [12, 384, 1536], P(('runs', 'layer'), 'tile'), parts along dimension 0, may hold values from -6 to 6
- layer_weight: float32 [12], P(('runs', 'layer')), parts along dimension 0, may hold values from 0.3 to 1
- wind_row: int32 [12], P('runs'), parts along dimension 0, may hold values from -4 to 4, as said below
- wind_col: int32 [12], P('runs'), parts along dimension 0, may hold values from -4 to 4, as said below
- foot_row: int32 [6, 6], replicated, may hold values from -80 to 79, as said below
- foot_col: int32 [6, 6], replicated, may hold values from -80 to 79, as said below
- frac_row: float32 [6, 6], replicated, may hold values from 0 to 1
- frac_col: float32 [6, 6], replicated, may hold values from 0 to 1
- amplitude: float32 [384, 1536], P('tile', 'layer'), may hold values from 0.5 to 2
- valid: int32 [24, 96], P('tile', 'layer'), may hold values 0 or 1
- recon_matrix: bfloat16 [6, 2, 24, 96, 2688], P('star', None, 'tile', 'layer'), may hold values from -0.0390625 to 0.0390625
- prev_recon: float32 [5376], P('runs'), parts along dimension 0, may hold values from -6 to 6
Outputs:
- shifted: float32 [12, 384, 1536], P(('runs', 'layer'), 'tile'), parts along dimension 0
- slopes: float32 [12, 2, 24, 96], P(('runs', 'star'), None, 'tile', 'layer'), parts along dimension 0
- commands: float32 [5376], P('runs'), parts along dimension 0
The draws below stay inside these ranges and needn't reach their ends.
There are 2 independent parts, one for each index of `runs`. The reference program is written for one: setup_inputs(seed, part) draws one part's arguments, and reference() takes and returns one part's arrays. A program takes and returns all parts, laid end to end along the dimension named above; an argument that names none is the same for every part. Nothing has to cross between parts.
Inputs may be any that keep to these rules, and one draw needn't show every extreme that they name: `wind_row`: some layer takes 4 and another takes -4. `wind_col`: some layer takes 4 and another takes -4. `foot_row`: some star and layer take -80 and another takes 80 - 1. `foot_col`: some star and layer take -80 and another takes 80 - 1.
All inputs are finite; a program needn't handle non-finite values. No bound on the sum of `valid` on one device may be relied on, other than what follows from the above.
Results may differ from the reference program's by a relative error of at most 0.0019.
Values sent between devices are 32-bit elements; how exact they have to be, the bound alone decides.
A program may use at most 64 MiB of HBM per device.

```python
import math
import jax
import jax.numpy as jnp

PIX = 16
PAD = 32
SUB_COLS = 96
NACT = 2688
WIND = 4
FOOT = 80
LAYERS = 6
STARS = 6
SUBROWS = 24
ROWS = 384
COLS = 1536


def with_ends(key, count, lowest_value, highest_value):
    first_key, second_key, third_key = jax.random.split(key, 3)
    values = jax.random.randint(first_key, (count,), lowest_value, highest_value + 1)
    top_place = jax.random.randint(second_key, (), 0, count)
    stride = jax.random.randint(third_key, (), 1, count)
    low_place = jnp.mod(top_place + stride, count)
    places = jnp.arange(count)
    values = jnp.where(places == top_place, highest_value, values)
    values = jnp.where(places == low_place, lowest_value, values)
    return values.astype(jnp.int32)


def draw_wind_row(key, part):
    return with_ends(jax.random.fold_in(key, 7), LAYERS, -WIND, WIND)


def draw_wind_col(key, part):
    return with_ends(jax.random.fold_in(key, 11), LAYERS, -WIND, WIND)


def draw_foot_row(key, part):
    return with_ends(jax.random.fold_in(key, 13), STARS * LAYERS, -FOOT, FOOT - 1).reshape(STARS, LAYERS)


def draw_foot_col(key, part):
    return with_ends(jax.random.fold_in(key, 17), STARS * LAYERS, -FOOT, FOOT - 1).reshape(STARS, LAYERS)


def touch_ends(result, rng, low, high):
    longest = result.shape.index(max(result.shape))
    spots = []
    for shift in (0, 1):
        where = [jax.random.randint(jax.random.fold_in(rng, axis), (), 0, length) for axis, length in enumerate(result.shape)]
        where[longest] = (where[longest] + shift) % result.shape[longest]
        spots.append(tuple(where))
    return result.at[spots[0]].set(low).at[spots[1]].set(high)


def shard_levels(stream_key, extent, pieces, low, high):
    gain, own = 1.0, jax.random.fold_in(stream_key, 6)
    for position, blocks in pieces:
        heights = jnp.exp(jax.random.uniform(jax.random.fold_in(own, position), (blocks,), jnp.float32, low / len(pieces), high / len(pieces)))
        gain = gain * jnp.repeat(heights, extent[position] // blocks).reshape([-1 if axis == position else 1 for axis in range(len(extent))])
    return gain


def scatter_about(own_key, extent, scale, most, cuts=(), dtype=jnp.bfloat16):
    values = scale * jax.random.normal(own_key, extent, jnp.float32)
    if cuts:
        values = values * shard_levels(own_key, extent, cuts, -0.22, 0.18)
    return jnp.clip(values, -most, most).astype(dtype)


def setup_inputs(seed: int = 0, part: int = 0) -> dict:
    key_list = jax.random.split(jax.random.key(seed), 13)
    part_splits = jax.random.split(jax.random.fold_in(key_list[12], part), 13)
    screens = scatter_about(part_splits[0], (LAYERS, ROWS, COLS), 1.0, 6.0, ((0, 2), (1, 4)), jnp.float32)
    layer_weight = jnp.clip(jnp.exp(math.log(1.0) - 1.2039728 * jax.random.uniform(part_splits[1], (LAYERS,), jnp.float32) ** shard_levels(part_splits[1], (LAYERS,), ((0, 2),), -0.2, 0.2)), 0.3, 1.0)
    wind_row = draw_wind_row(jax.random.fold_in(jax.random.fold_in(key_list[12], part), 71), part)
    wind_col = draw_wind_col(jax.random.fold_in(jax.random.fold_in(key_list[12], part), 71), part)
    foot_row = draw_foot_row(jax.random.fold_in(key_list[12], 71), part)
    foot_col = draw_foot_col(jax.random.fold_in(key_list[12], 71), part)
    frac_row = jnp.clip(jax.random.uniform(key_list[6], (STARS, LAYERS), jnp.float32, 0.0, 1.0), 0.0, 1.0)
    frac_col = jnp.clip(jax.random.uniform(key_list[7], (STARS, LAYERS), jnp.float32, 0.0, 1.0), 0.0, 1.0)
    amplitude = jnp.clip(jnp.exp(math.log(2.0) - 1.3862944 * jax.random.uniform(key_list[8], (ROWS, COLS), jnp.float32) ** shard_levels(key_list[8], (ROWS, COLS), ((0, 4), (1, 2)), -0.2, 0.2)), 0.5, 2.0)
    valid = touch_ends((jax.random.randint(key_list[9], (SUBROWS, SUB_COLS), 0, 4) < 3).astype(jnp.int32), jax.random.fold_in(key_list[9], 1), 0, 1)
    recon_matrix = scatter_about(key_list[10], (STARS, 2, SUBROWS, SUB_COLS, NACT), (STARS * 2 * SUBROWS * SUB_COLS) ** -0.5, 0.0390625, ((0, 2), (2, 4), (3, 2)))
    prev_recon = scatter_about(part_splits[11], (NACT,), 1.0, 6.0, (), jnp.float32)
    return {"screens": screens, "layer_weight": layer_weight, "wind_row": wind_row, "wind_col": wind_col, "foot_row": foot_row, "foot_col": foot_col, "frac_row": frac_row, "frac_col": frac_col, "amplitude": amplitude, "valid": valid, "recon_matrix": recon_matrix, "prev_recon": prev_recon}


def star_images(phase, amplitude, valid):
    field = amplitude * jnp.cos(phase) + 1j * (amplitude * jnp.sin(phase))
    blocks = field.reshape(SUBROWS, PIX, SUB_COLS, PIX).transpose(0, 2, 1, 3)
    spectrum = jnp.fft.fft2(blocks, s=(PAD, PAD))
    intensity = jnp.real(spectrum) ** 2 + jnp.imag(spectrum) ** 2
    centred = (jnp.mod(jnp.arange(PAD) + PAD // 2, PAD) - PAD // 2).astype(jnp.float32)
    summed = jnp.sum(intensity, axis=(2, 3))
    along_rows = jnp.sum(intensity * centred[:, None], axis=(2, 3)) / summed
    along_cols = jnp.sum(intensity * centred[None, :], axis=(2, 3)) / summed
    return jnp.stack([along_rows, along_cols]) * valid.astype(jnp.float32)


def reference(screens, layer_weight, wind_row, wind_col, foot_row, foot_col, frac_row, frac_col, amplitude, valid, recon_matrix, prev_recon):
    shifted = jnp.stack([jnp.roll(screens[l], (wind_row[l], wind_col[l]), axis=(0, 1)) for l in range(LAYERS)])
    results = []
    for g in range(STARS):
        pupil = jnp.zeros((ROWS, COLS), jnp.float32)
        for l in range(LAYERS):
            row_frac = frac_row[g, l]
            col_frac = frac_col[g, l]
            anchor = jnp.roll(shifted[l], (-foot_row[g, l], -foot_col[g, l]), axis=(0, 1))
            lower = jnp.roll(anchor, -1, axis=0)
            beside = jnp.roll(anchor, -1, axis=1)
            corner = jnp.roll(lower, -1, axis=1)
            sampled = ((1.0 - row_frac) * (1.0 - col_frac) * anchor + row_frac * (1.0 - col_frac) * lower
                       + (1.0 - row_frac) * col_frac * beside + row_frac * col_frac * corner)
            pupil = pupil + layer_weight[l] * sampled
        results.append(star_images(pupil, amplitude, valid))
    slopes = jnp.stack(results)
    recon = jnp.dot(slopes.astype(jnp.bfloat16).reshape(1, -1), recon_matrix.reshape(-1, NACT), preferred_element_type=jnp.float32)[0]
    commands = 2.0 * recon - prev_recon
    return shifted, slopes, commands
```

```python
import functools
import math

import jax
import jax.numpy as jnp
import numpy as np
from jax import lax
from jax.experimental import pallas as pl
from jax.experimental.pallas import tpu as pltpu
from jax.sharding import PartitionSpec as P

PIX = 16
PAD = 32
WIND = 4
FOOT = 80
LANES = 128
HALO = -(-(WIND + FOOT + 1) // 8) * 8
MESH = pl.DeviceIdType.MESH
ANY = pl.BlockSpec(memory_space=pl.ANY)
SMEM = pl.BlockSpec(memory_space=pltpu.SMEM)
VMEM = pl.BlockSpec(memory_space=pltpu.VMEM)


def greet(peers):
    barrier = pltpu.get_barrier_semaphore()
    for peer in peers:
        pl.semaphore_signal(barrier, inc=1, device_id=peer, device_id_type=MESH)
    pl.semaphore_wait(barrier, len(peers))


def plan(rows, cols, blocks):
    strips = cols // LANES
    per_block = strips // blocks
    unit = 2 if per_block % 2 == 0 else 1
    units = per_block // unit
    group = 1 if (unit * LANES // PIX) % 16 == 0 else units
    return strips, per_block, unit, units, group


def frame_kernel(
    tiles, cores, blocks, stars, weights, wind_row, wind_col, foot_row, foot_col,
    frac_row, frac_col, screens, amplitude, valid, matrix, row_table, col_table, gather, spread,
    shifted, slopes, recon,
    field, land, outbox, inbox, share, moved, amp, mask, weight, row_tab, col_tab, gath, spre,
    scale, real, real_high, real_low, imag_high, imag_low, sums, total_terms, near, far,
    zsend, zrecv, csend, crecv, xsend, xrecv, local, load, store, nsend, nrecv, fsend, frecv,
):
    tile, core, layer = (lax.axis_index(n) for n in ("tile", "star", "layer"))
    up, down = lax.rem(tile + 1, tiles), lax.rem(tile + tiles - 1, tiles)
    partners = [lax.rem(core + k, cores) for k in range(1, cores)]
    peers = [lax.rem(layer + k, blocks) for k in range(1, blocks)]
    count = blocks * cores
    me = layer * cores + core
    near_peers = []
    for k in range(1, count):
        rank = lax.rem(me + k, count)
        near_peers.append({"layer": rank // cores, "star": lax.rem(rank, cores)})
    far_peers = [{"tile": lax.rem(tile + k, tiles)} for k in range(1, tiles)]
    lays, rows, cols = screens.shape
    strips, per_block, unit, units, group = plan(rows, cols, blocks)
    chunks = units // group
    width = group * unit * LANES
    subs = rows // PIX
    groups = rows // 8
    first = (layer + 1) * per_block + strips - 1
    star_start, layer_start = core * stars, layer * lays
    many = math.gcd(groups, 6)
    pairs = 2 * stars
    taps = matrix.shape[3] // chunks

    def column(n, size=1):
        start = pl.multiple_of(lax.rem(first + n, strips) * LANES, LANES)
        return pl.ds(start, size * LANES)

    copies = []
    for n in range(strips + 2):
        copy = pltpu.make_async_copy(
            screens.at[:, :, column(n % strips)],
            field.at[:, n, pl.ds(HALO, rows), :],
            local.at[n],
        )
        copy.start()
        copies.append(copy)
    greet(near_peers + far_peers)
    sends = []
    for m in range(strips // cores):
        n = m * cores + core
        pair = []
        for d, (start, peer) in enumerate(((rows - HALO, up), (0, down))):
            copy = pltpu.make_async_remote_copy(
                src_ref=screens.at[:, pl.ds(start, HALO), column(n)],
                dst_ref=land.at[d, n],
                send_sem=zsend.at[m, d],
                recv_sem=zrecv.at[m, d],
                device_id={"tile": peer},
                device_id_type=MESH,
            )
            copy.start()
            pair.append(copy)
        sends.append(pair)
    loads = []
    for n, (source, target) in enumerate(
        ((amplitude, amp), (valid, mask), (row_table, row_tab), (col_table, col_tab),
         (gather, gath), (spread, spre))
    ):
        copy = pltpu.make_async_copy(source, target, load.at[n])
        copy.start()
        loads.append(copy)
    matrix_copies = []
    for w in range(chunks):
        copy = pltpu.make_async_copy(
            matrix.at[:, :, :, w * taps : (w + 1) * taps, :],
            weight.at[w, :, :, 0:subs, 0:taps, :],
            load.at[len(loads) + w],
        )
        copy.start()
        matrix_copies.append(copy)
    high_rows = weight.shape[3]
    if high_rows > subs:
        for w in range(chunks):
            for g in range(stars):
                for d in range(2):
                    weight[w, g, d, subs:, :, :] = jnp.zeros(
                        (high_rows - subs,) + weight.shape[4:], weight.dtype
                    )
    if weight.shape[4] > taps:
        for w in range(chunks):
            for g in range(stars):
                for d in range(2):
                    weight[w, g, d, 0:subs, taps:, :] = jnp.zeros(
                        (subs, weight.shape[4] - taps, weight.shape[5]), weight.dtype
                    )
    sums[...] = jnp.zeros_like(sums)
    scale[...] = jnp.zeros_like(scale)

    def per_sub(values):
        return jnp.sum(values.reshape(subs, PIX, values.shape[1]), axis=1)

    def collect(values):
        high, low = halves(values)
        return product(high, gath[...]) + product(low, gath[...])

    for copy in loads:
        copy.wait()
    for w in range(chunks):
        power = amp[:, w * width : (w + 1) * width]
        sums[0:subs, :] = per_sub(power * power)
        lit = product(mask[...].astype(jnp.float32).astype(jnp.bfloat16), spre[w])
        scale[w, 0:subs, :] = lit / (collect(sums[0:8, :])[0:subs] * PAD)
    for copy in copies:
        copy.wait()
    lane = lax.broadcasted_iota(jnp.int32, (8, LANES), 1)

    def window(j, row, base, n):
        return [field[j, base + n + k, pl.ds(row, 8), :] for k in range(unit + 1)]

    def place(start):
        base = start // LANES
        turn = start - base * LANES
        return base, turn

    moves = []

    def move(u):
        low = u * unit

        def move_step(i, carry):
            for j in range(lays):
                base, turn = place(LANES - wind_col[layer_start + j])
                values = window(j, HALO + i * 8 - wind_row[layer_start + j], base, low)
                rolled = [pltpu.roll(v, (LANES - turn) & (LANES - 1), 1) for v in values]
                keep = lane < LANES - turn
                for k in range(unit):
                    moved[u, j, pl.ds(pl.multiple_of(i * 8, 8), 8), k * LANES : (k + 1) * LANES] = (
                        jnp.where(keep, rolled[k], rolled[k + 1])
                    )
            return carry

        lax.fori_loop(0, groups, move_step, 0, unroll=math.gcd(groups, 3))
        copy = pltpu.make_async_copy(
            moved.at[u], shifted.at[:, :, column(low + 1, unit)], store.at[u]
        )
        copy.start()
        moves.append(copy)

    def compute(u, put):
        low = u * unit

        def pupil_step(n, carry):
            g = n // (groups // many)
            i = (n - g * (groups // many)) * many
            star = star_start + g
            total = [[None] * unit for _ in range(many)]
            for j in range(lays):
                lay = layer_start + j
                top_row = HALO + i * 8 + foot_row[star, lay] - wind_row[lay]
                base, turn = place(LANES + foot_col[star, lay] - wind_col[lay])
                gain = weights[j]
                a, b = frac_row[star, lay], frac_col[star, lay]
                top, bottom = gain * (1.0 - a), gain * a
                keep_near = lane < LANES - turn
                keep_far = lane < LANES - 1 - turn
                near_turn, far_turn = (LANES - turn) & (LANES - 1), LANES - 1 - turn
                for r in range(many):
                    row = top_row + r * 8
                    values = [
                        top * x + bottom * y
                        for x, y in zip(window(j, row, base, low), window(j, row + 1, base, low))
                    ]
                    close = [pltpu.roll(v, near_turn, 1) for v in values]
                    beside = [pltpu.roll(v, far_turn, 1) for v in values]
                    for k in range(unit):
                        term = (1.0 - b) * jnp.where(
                            keep_near, close[k], close[k + 1]
                        ) + b * jnp.where(keep_far, beside[k], beside[k + 1])
                        total[r][k] = term if j == 0 else total[r][k] + term
            for r in range(many):
                for k in range(unit):
                    put(g, pl.ds(pl.multiple_of((i + r) * 8, 8), 8), k, total[r][k])
            return carry

        lax.fori_loop(0, stars * groups // many, pupil_step, 0)

    def to_outbox(u):
        def put(g, at, k, value):
            outbox[u, g, at, k * LANES : (k + 1) * LANES] = value

        return put

    def to_share(w):
        def put(g, at, k, value):
            share[w, g, at, k * LANES : (k + 1) * LANES] = value

        return put

    block = col_tab.shape[1]

    def slope_chunk(w):
        left = w * width

        def field_step(n, carry):
            g = n // subs
            i = n - g * subs
            at = pl.ds(pl.multiple_of(i * PIX, PIX), PIX)
            parts = []
            for v in range(w * group, (w + 1) * group):
                phase = share[v, g, at, :]
                for k in range(blocks - 1):
                    phase = phase + inbox[k, v, g, at, :]
                parts.append(phase)
            sine, cosine = sine_cosine(jnp.concatenate(parts, axis=1))
            power = amp[at, left : left + width]
            a, b = power * cosine, power * sine
            to = pl.ds(pl.multiple_of(n * PIX, PIX), PIX)
            real[to, :] = a
            real_high[to, :], real_low[to, :] = halves(a)
            imag_high[to, :], imag_low[to, :] = halves(b)
            return carry

        lax.fori_loop(0, stars * subs, field_step, 0)
        for g in range(stars):
            at = slice(g * rows, (g + 1) * rows)
            a = real[at, :]
            a_high, a_low = real_high[at, :], real_low[at, :]
            b_high, b_low = imag_high[at, :], imag_low[at, :]
            row_high, row_low, row_alt = (
                row_tab[0:rows, :], row_tab[rows : 2 * rows, :], row_tab[2 * rows :, :]
            )
            turned = product(row_high, b_high) + product(row_high, b_low) + product(row_low, b_high)
            alt_a = (product(row_alt, a_high) + product(row_alt, a_low))[:subs]
            alt_b = (product(row_alt, b_high) + product(row_alt, b_low))[:subs]
            along = 2.0 * per_sub(a * turned) - PIX * (alt_a * alt_a + alt_b * alt_b)
            sums[16 * g : 16 * g + subs, :] = along
            pieces = []
            for k in range(width // block):
                cut = slice(k * block, (k + 1) * block)
                turned = (
                    product(b_high[:, cut], col_tab[0])
                    + product(b_low[:, cut], col_tab[0])
                    + product(b_high[:, cut], col_tab[1])
                )
                alt_a = product(a_high[:, cut], col_tab[2]) + product(a_low[:, cut], col_tab[2])
                alt_b = product(b_high[:, cut], col_tab[2]) + product(b_low[:, cut], col_tab[2])
                pieces.append(2.0 * a[:, cut] * turned - (alt_a * alt_a + alt_b * alt_b))
            across = per_sub(jnp.concatenate(pieces, axis=1))
            sums[16 * g + 8 : 16 * g + 8 + subs, :] = across
        found = collect(sums[...])
        depth = weight.shape[4]
        mine = (
            lax.broadcasted_iota(jnp.int32, (8, found.shape[1]), 1) // depth
            == lax.broadcasted_iota(jnp.int32, (8, found.shape[1]), 0)
        )
        terms = []
        for n in range(pairs):
            part = found[8 * n : 8 * n + 8] * scale[w]
            g, d = divmod(n, 2)
            slopes[g, d, :, w * taps : (w + 1) * taps] = part[0:subs, 0:taps]
            terms.append(jnp.where(mine, part, 0.0).astype(jnp.bfloat16))
        matrix_copies[w].wait()
        left_side = jnp.concatenate(terms, axis=1)
        right_side = weight[w].reshape(left_side.shape[1], weight.shape[5])
        partial = jnp.dot(left_side, right_side, preferred_element_type=jnp.float32)
        partial = jnp.sum(partial, axis=0, keepdims=True)
        if w == 0:
            total_terms[...] = partial
        else:
            total_terms[...] = total_terms[...] + partial

    forwards, swaps = [], []
    done = 0
    late = []
    for m in range(strips // cores):
        n = m * cores + core
        current = []
        for d in range(2):
            sends[m][d].wait_recv()
            for k, p in enumerate(partners):
                forward = pltpu.make_async_remote_copy(
                    src_ref=land.at[d, n],
                    dst_ref=land.at[d, n],
                    send_sem=csend.at[m, d, k],
                    recv_sem=crecv.at[m, d, k],
                    device_id={"star": p},
                    device_id_type=MESH,
                )
                forward.start()
                current.append(forward)
        for forward in current:
            forward.wait_recv()
        forwards.extend(current)
        have = (m + 1) * cores
        for n in range(m * cores, have):
            for to in (n, n + strips):
                if to < strips + 2:
                    for j in range(lays):
                        field[j, to, 0:HALO, :] = land[0, n, j]
                        field[j, to, HALO + rows :, :] = land[1, n, j]
        while done < units * blocks and (
            have == strips or done * unit + unit + 2 <= have
        ):
            k, w = divmod(done, units)
            if k < blocks - 1:
                compute(done, to_outbox(done))
                copy = pltpu.make_async_remote_copy(
                    src_ref=outbox.at[done],
                    dst_ref=inbox.at[k, w],
                    send_sem=xsend.at[done],
                    recv_sem=xrecv.at[done],
                    device_id={"layer": peers[k]},
                    device_id_type=MESH,
                )
                copy.start()
                swaps.append(copy)
            else:
                compute(done, to_share(w))
                for q, copy in enumerate(swaps):
                    if q % units == w:
                        copy.wait_recv()
                if (w + 1) % group == 0:
                    slope_chunk(w // group)
            if have < strips:
                move(done)
            else:
                late.append(done)
            done += 1
    near_copies = []
    for k, peer in enumerate(near_peers):
        copy = pltpu.make_async_remote_copy(
            src_ref=total_terms,
            dst_ref=near.at[me],
            send_sem=nsend.at[k],
            recv_sem=nrecv.at[k],
            device_id=peer,
            device_id_type=MESH,
        )
        copy.start()
        near_copies.append(copy)
    near[me] = total_terms[...]
    for u in late:
        move(u)
    for copy in near_copies:
        copy.wait_recv()
    total = near[0]
    for k in range(1, count):
        total = total + near[k]
    far[tile] = total
    far_copies = []
    for k, peer in enumerate(far_peers):
        copy = pltpu.make_async_remote_copy(
            src_ref=far.at[tile],
            dst_ref=far.at[tile],
            send_sem=fsend.at[k],
            recv_sem=frecv.at[k],
            device_id=peer,
            device_id_type=MESH,
        )
        copy.start()
        far_copies.append(copy)
    for pair in sends:
        for copy in pair:
            copy.wait_send()
    for copy in forwards + swaps + near_copies:
        copy.wait_send()
    for copy in moves:
        copy.wait()
    for copy in far_copies:
        copy.wait()
    total = far[0]
    for k in range(1, tiles):
        total = total + far[k]
    recon[...] = total


def tables(rows, width, block, subs, taps, depth, chunks, high_rows):
    def block_diagonal(count, piece):
        return np.kron(np.eye(count), piece)

    index = np.arange(PIX)
    gap = index[:, None] - index[None, :]
    angle = np.where(gap == 0, 1, gap) * (math.pi / PAD)
    sign = np.where(gap % 2 == 0, 1.0, -1.0)
    table = np.where(gap == 0, 0.0, PIX * sign * np.cos(angle) / np.sin(angle))
    alternate = np.where(index % 2 == 0, 1.0, -1.0)
    row_part = block_diagonal(subs, table)
    row_alt = np.pad(block_diagonal(subs, alternate[None, :]), ((0, -subs % 16), (0, 0)))
    first = np.zeros((PIX, PIX))
    first[:, 0] = 4.0 * alternate
    col_part = block_diagonal(block // PIX, table.T)
    col_alt = block_diagonal(block // PIX, first)

    def split(t):
        high = np.asarray(t.astype(jnp.bfloat16), np.float64)
        return high, t - high

    row_all = np.concatenate([*split(row_part), row_alt], axis=0)
    col_all = np.stack([*split(col_part), col_alt])
    fold = np.zeros((taps, high_rows, depth))
    for k in range(taps):
        fold[k, :, k] = 1.0
    fold = fold.reshape(taps, high_rows * depth)
    gather = np.repeat(fold, PIX, axis=0)
    spread = np.zeros((chunks, chunks * taps, high_rows * depth))
    for w in range(chunks):
        spread[w, w * taps : (w + 1) * taps] = fold
    return tuple(jnp.asarray(t.astype(jnp.bfloat16)) for t in (row_all, col_all, gather, spread))


def frame(scalars, screens, amplitude, valid, matrix):
    tiles, blocks, cores = (lax.axis_size(n) for n in ("tile", "layer", "star"))
    lays, rows, cols = screens.shape
    stars, _, subs, sub_cols, commands = matrix.shape
    strips, per_block, unit, units, group = plan(rows, cols, blocks)
    chunks = units // group
    width = group * unit * LANES
    taps = sub_cols // chunks
    depth = -(-taps // 16) * 16
    high_rows = -(-subs // 8) * 8
    block = 2 * LANES if width % (2 * LANES) == 0 else LANES
    consts = tables(rows, width, block, subs, taps, depth, chunks, high_rows)
    count = blocks * cores
    steps = strips // cores
    dma = pltpu.SemaphoreType.DMA
    bf16, f32 = jnp.bfloat16, jnp.float32
    piece = (stars, rows, unit * LANES)
    return pl.pallas_call(
        functools.partial(frame_kernel, tiles, cores, blocks, stars),
        out_shape=(
            jax.ShapeDtypeStruct((lays, rows, cols), f32),
            jax.ShapeDtypeStruct((stars, 2, subs, sub_cols), f32),
            jax.ShapeDtypeStruct((1, commands), f32),
        ),
        in_specs=[SMEM] * len(scalars) + [ANY] * (4 + len(consts)),
        out_specs=(ANY, VMEM, VMEM),
        scratch_shapes=[
            pltpu.VMEM((lays, strips + 2, rows + 2 * HALO, LANES), f32),
            pltpu.VMEM((2, strips, lays, HALO, LANES), f32),
            pltpu.VMEM((units * (blocks - 1),) + piece, f32),
            pltpu.VMEM((blocks - 1, units) + piece, f32),
            pltpu.VMEM((units,) + piece, f32),
            pltpu.VMEM((units * blocks, lays, rows, unit * LANES), f32),
            pltpu.VMEM(amplitude.shape, f32),
            pltpu.VMEM(valid.shape, valid.dtype),
            pltpu.VMEM((chunks, stars, 2, high_rows, depth, commands), bf16),
        ]
        + [pltpu.VMEM(t.shape, bf16) for t in consts]
        + [
            pltpu.VMEM((chunks, 8, high_rows * depth), f32),
            pltpu.VMEM((stars * rows, width), f32),
            pltpu.VMEM((stars * rows, width), bf16),
            pltpu.VMEM((stars * rows, width), bf16),
            pltpu.VMEM((stars * rows, width), bf16),
            pltpu.VMEM((stars * rows, width), bf16),
            pltpu.VMEM((2 * stars * 8, width), f32),
            pltpu.VMEM((1, commands), f32),
            pltpu.VMEM((count, 1, commands), f32),
            pltpu.VMEM((tiles, 1, commands), f32),
            dma((steps, 2)),
            dma((steps, 2)),
            dma((steps, 2, cores - 1)),
            dma((steps, 2, cores - 1)),
            dma((units * (blocks - 1),)),
            dma((units * (blocks - 1),)),
            dma((strips + 2,)),
            dma((6 + chunks,)),
            dma((units * blocks,)),
            dma((count - 1,)),
            dma((count - 1,)),
            dma((tiles - 1,)),
            dma((tiles - 1,)),
        ],
        compiler_params=pltpu.CompilerParams(collective_id=0, has_side_effects=True),
        name="frame",
    )(*scalars, screens, amplitude, valid, matrix, *consts)


def sine_cosine(x):
    turns = jnp.floor(x * (2.0 / math.pi) + 0.5)
    r = x - turns * 1.5703125
    r = r - turns * 4.837512969970703125e-4
    r = r - turns * 7.54978995489188216e-8
    z = r * r
    s = r + r * z * (-1.6666654611e-1 + z * (8.3321608736e-3 - z * 1.9515295891e-4))
    c = 1.0 - 0.5 * z + z * z * (
        4.166664568298827e-2 + z * (-1.388731625493765e-3 + z * 2.443315711809948e-5)
    )
    quadrant = turns.astype(jnp.int32)
    odd = (quadrant & 1) == 1
    sine = jnp.where(odd, c, s)
    cosine = jnp.where(odd, s, c)
    sine = jnp.where((quadrant & 2) == 2, -sine, sine)
    cosine = jnp.where(((quadrant + 1) & 2) == 2, -cosine, cosine)
    return sine, cosine


def halves(x):
    high = x.astype(jnp.bfloat16)
    return high, (x - high.astype(jnp.float32)).astype(jnp.bfloat16)


def product(x, y):
    return jnp.dot(x, y, preferred_element_type=jnp.float32)


def body(
    screens,
    layer_weight,
    wind_row,
    wind_col,
    foot_row,
    foot_col,
    frac_row,
    frac_col,
    amplitude,
    valid,
    recon_matrix,
    prev_recon,
):
    scalars = (layer_weight, wind_row, wind_col, foot_row, foot_col, frac_row, frac_col)
    shifted, slopes, recon = frame(scalars, screens, amplitude, valid, recon_matrix)
    commands = 2.0 * recon[0] - prev_recon
    return (shifted, slopes, commands)


def solution(mesh):
    return jax.shard_map(
        body,
        mesh=mesh,
        in_specs=(
            P(("runs", "layer"), "tile", None),
            P(("runs", "layer")),
            P("runs"),
            P("runs"),
            P(),
            P(),
            P(),
            P(),
            P("tile", "layer"),
            P("tile", "layer"),
            P("star", None, "tile", "layer", None),
            P("runs"),
        ),
        out_specs=(
            P(("runs", "layer"), "tile", None),
            P(("runs", "star"), None, "tile", "layer"),
            P("runs"),
        ),
        check_vma=False,
    )
```

```python
import functools
import math

import jax
import jax.numpy as jnp
import numpy as np
from jax import lax
from jax.experimental import pallas as pl
from jax.experimental.pallas import tpu as pltpu
from jax.sharding import PartitionSpec as P

PIX = 16
PAD = 32
WIND = 4
FOOT = 80
LANES = 128
HALO = -(-(WIND + FOOT + 1) // 8) * 8
MESH = pl.DeviceIdType.MESH
ANY = pl.BlockSpec(memory_space=pl.ANY)
HBM = pl.BlockSpec(memory_space=pltpu.HBM)
SMEM = pl.BlockSpec(memory_space=pltpu.SMEM)
VMEM = pl.BlockSpec(memory_space=pltpu.VMEM)


def greet(peers):
    barrier = pltpu.get_barrier_semaphore()
    for peer in peers:
        pl.semaphore_signal(barrier, inc=1, device_id=peer, device_id_type=MESH)
    pl.semaphore_wait(barrier, len(peers))


def plan(rows, cols, blocks):
    strips = cols // LANES
    per_block = strips // blocks
    unit = 2 if per_block % 2 == 0 else 1
    units = per_block // unit
    group = 1 if (unit * LANES // PIX) % 16 == 0 else units
    return strips, per_block, unit, units, group


def frame_kernel(
    tiles, cores, blocks, stars, weights_in, wind_row_in, wind_col_in, foot_row_in, foot_col_in,
    frac_row_in, frac_col_in, screens, amplitude, valid, matrix, row_table, col_table, gather, spread,
    shifted, slopes, recon,
    weights, wind_row, wind_col, foot_row, foot_col, frac_row, frac_col,
    field, land, outbox, inbox, share, amp, mask, weight, row_tab, col_tab, gath, spre,
    scale, real, real_high, real_low, imag_high, imag_low, sums, total_terms, near, far,
    zsend, zrecv, csend, crecv, xsend, xrecv, local, load, nsend, nrecv, fsend, frecv,
):
    tile, core, layer = (lax.axis_index(n) for n in ("tile", "star", "layer"))
    up, down = lax.rem(tile + 1, tiles), lax.rem(tile + tiles - 1, tiles)
    partners = [lax.rem(core + k, cores) for k in range(1, cores)]
    peers = [lax.rem(layer + k, blocks) for k in range(1, blocks)]
    count = blocks * cores
    me = layer * cores + core
    near_peers = []
    for k in range(1, count):
        rank = lax.rem(me + k, count)
        near_peers.append({"layer": rank // cores, "star": lax.rem(rank, cores)})
    far_peers = [{"tile": lax.rem(tile + k, tiles)} for k in range(1, tiles)]
    lays, rows, cols = screens.shape
    strips, per_block, unit, units, group = plan(rows, cols, blocks)
    chunks = units // group
    width = group * unit * LANES
    subs = rows // PIX
    groups = rows // 8
    first = (layer + 1) * per_block + strips - 1
    star_start, layer_start = core * stars, layer * lays
    many = math.gcd(groups, 6)
    pairs = 2 * stars
    taps = matrix.shape[3] // chunks

    def column(n, size=1):
        start = pl.multiple_of(lax.rem(first + n, strips) * LANES, LANES)
        return pl.ds(start, size * LANES)

    copies = []
    for n in range(strips + 2):
        copy = pltpu.make_async_copy(
            screens.at[:, :, column(n % strips)],
            field.at[:, n, pl.ds(HALO, rows), :],
            local.at[n],
        )
        copy.start()
        copies.append(copy)
    greet(near_peers + far_peers)
    sends = []
    for m in range(strips // cores):
        n = m * cores + core
        pair = []
        for d, (start, peer) in enumerate(((rows - HALO, up), (0, down))):
            copy = pltpu.make_async_remote_copy(
                src_ref=screens.at[:, pl.ds(start, HALO), column(n)],
                dst_ref=land.at[d, n],
                send_sem=zsend.at[m, d],
                recv_sem=zrecv.at[m, d],
                device_id={"tile": peer},
                device_id_type=MESH,
            )
            copy.start()
            pair.append(copy)
        sends.append(pair)
    loads = []
    for n, (source, target) in enumerate(
        ((amplitude, amp), (valid, mask), (row_table, row_tab), (col_table, col_tab),
         (gather, gath), (spread, spre), (weights_in, weights), (wind_row_in, wind_row),
         (wind_col_in, wind_col), (foot_row_in, foot_row), (foot_col_in, foot_col),
         (frac_row_in, frac_row), (frac_col_in, frac_col))
    ):
        copy = pltpu.make_async_copy(source, target, load.at[n])
        copy.start()
        loads.append(copy)
    matrix_copies = []
    for w in range(chunks):
        copy = pltpu.make_async_copy(
            matrix.at[:, :, :, w * taps : (w + 1) * taps, :],
            weight.at[w, :, :, 0:subs, 0:taps, :],
            load.at[len(loads) + w],
        )
        copy.start()
        matrix_copies.append(copy)
    high_rows = weight.shape[3]
    if high_rows > subs:
        for w in range(chunks):
            for g in range(stars):
                for d in range(2):
                    weight[w, g, d, subs:, :, :] = jnp.zeros(
                        (high_rows - subs,) + weight.shape[4:], weight.dtype
                    )
    if weight.shape[4] > taps:
        for w in range(chunks):
            for g in range(stars):
                for d in range(2):
                    weight[w, g, d, 0:subs, taps:, :] = jnp.zeros(
                        (subs, weight.shape[4] - taps, weight.shape[5]), weight.dtype
                    )
    sums[...] = jnp.zeros_like(sums)
    scale[...] = jnp.zeros_like(scale)

    def per_sub(values):
        return jnp.sum(values.reshape(subs, PIX, values.shape[1]), axis=1)

    def collect(values):
        high, low = halves(values)
        return product(high, gath[...]) + product(low, gath[...])

    for copy in loads:
        copy.wait()
    for w in range(chunks):
        power = amp[:, w * width : (w + 1) * width]
        sums[0:subs, :] = per_sub(power * power)
        lit = product(mask[...].astype(jnp.float32).astype(jnp.bfloat16), spre[w])
        scale[w, 0:subs, :] = lit / (collect(sums[0:8, :])[0:subs] * PAD)
    for copy in copies:
        copy.wait()
    lane = lax.broadcasted_iota(jnp.int32, (8, LANES), 1)

    def window(j, row, base, n):
        return [field[j, base + n + k, pl.ds(row, 8), :] for k in range(unit + 1)]

    def place(start):
        base = start // LANES
        turn = start - base * LANES
        return base, turn

    def move(u):
        low = u * unit

        def move_step(i, carry):
            for j in range(lays):
                base, turn = place(LANES - wind_col[layer_start + j])
                values = window(j, HALO + i * 8 - wind_row[layer_start + j], base, low)
                rolled = [pltpu.roll(v, (LANES - turn) & (LANES - 1), 1) for v in values]
                keep = lane < LANES - turn
                for k in range(unit):
                    shifted[j, pl.ds(pl.multiple_of(i * 8, 8), 8), column(low + k + 1)] = jnp.where(
                        keep, rolled[k], rolled[k + 1]
                    )
            return carry

        lax.fori_loop(0, groups, move_step, 0, unroll=math.gcd(groups, 3))

    def compute(u, put):
        low = u * unit

        def pupil_step(n, carry):
            g = n // (groups // many)
            i = (n - g * (groups // many)) * many
            star = star_start + g
            total = [[None] * unit for _ in range(many)]
            for j in range(lays):
                lay = layer_start + j
                top_row = HALO + i * 8 + foot_row[star, lay] - wind_row[lay]
                base, turn = place(LANES + foot_col[star, lay] - wind_col[lay])
                gain = weights[j]
                a, b = frac_row[star, lay], frac_col[star, lay]
                top, bottom = gain * (1.0 - a), gain * a
                keep_near = lane < LANES - turn
                keep_far = lane < LANES - 1 - turn
                near_turn, far_turn = (LANES - turn) & (LANES - 1), LANES - 1 - turn
                for r in range(many):
                    row = top_row + r * 8
                    values = [
                        top * x + bottom * y
                        for x, y in zip(window(j, row, base, low), window(j, row + 1, base, low))
                    ]
                    close = [pltpu.roll(v, near_turn, 1) for v in values]
                    beside = [pltpu.roll(v, far_turn, 1) for v in values]
                    for k in range(unit):
                        term = (1.0 - b) * jnp.where(
                            keep_near, close[k], close[k + 1]
                        ) + b * jnp.where(keep_far, beside[k], beside[k + 1])
                        total[r][k] = term if j == 0 else total[r][k] + term
            for r in range(many):
                for k in range(unit):
                    put(g, pl.ds(pl.multiple_of((i + r) * 8, 8), 8), k, total[r][k])
            return carry

        lax.fori_loop(0, stars * groups // many, pupil_step, 0)

    def to_outbox(u):
        def put(g, at, k, value):
            outbox[u, g, at, k * LANES : (k + 1) * LANES] = value

        return put

    def to_share(w):
        def put(g, at, k, value):
            share[w, g, at, k * LANES : (k + 1) * LANES] = value

        return put

    block = col_tab.shape[1]

    def slope_chunk(w):
        left = w * width

        def field_step(n, carry):
            g = n // subs
            i = n - g * subs
            at = pl.ds(pl.multiple_of(i * PIX, PIX), PIX)
            parts = []
            for v in range(w * group, (w + 1) * group):
                phase = share[v, g, at, :]
                for k in range(blocks - 1):
                    phase = phase + inbox[k, v, g, at, :]
                parts.append(phase)
            sine, cosine = sine_cosine(jnp.concatenate(parts, axis=1))
            power = amp[at, left : left + width]
            a, b = power * cosine, power * sine
            to = pl.ds(pl.multiple_of(n * PIX, PIX), PIX)
            real[to, :] = a
            real_high[to, :], real_low[to, :] = halves(a)
            imag_high[to, :], imag_low[to, :] = halves(b)
            return carry

        lax.fori_loop(0, stars * subs, field_step, 0)
        for g in range(stars):
            at = slice(g * rows, (g + 1) * rows)
            a = real[at, :]
            a_high, a_low = real_high[at, :], real_low[at, :]
            b_high, b_low = imag_high[at, :], imag_low[at, :]
            row_high, row_low, row_alt = (
                row_tab[0:rows, :], row_tab[rows : 2 * rows, :], row_tab[2 * rows :, :]
            )
            turned = product(row_high, b_high) + product(row_high, b_low) + product(row_low, b_high)
            alt_a = (product(row_alt, a_high) + product(row_alt, a_low))[:subs]
            alt_b = (product(row_alt, b_high) + product(row_alt, b_low))[:subs]
            along = 2.0 * per_sub(a * turned) - PIX * (alt_a * alt_a + alt_b * alt_b)
            sums[16 * g : 16 * g + subs, :] = along
            pieces = []
            for k in range(width // block):
                cut = slice(k * block, (k + 1) * block)
                turned = (
                    product(b_high[:, cut], col_tab[0])
                    + product(b_low[:, cut], col_tab[0])
                    + product(b_high[:, cut], col_tab[1])
                )
                alt_a = product(a_high[:, cut], col_tab[2]) + product(a_low[:, cut], col_tab[2])
                alt_b = product(b_high[:, cut], col_tab[2]) + product(b_low[:, cut], col_tab[2])
                pieces.append(2.0 * a[:, cut] * turned - (alt_a * alt_a + alt_b * alt_b))
            across = per_sub(jnp.concatenate(pieces, axis=1))
            sums[16 * g + 8 : 16 * g + 8 + subs, :] = across
        found = collect(sums[...])
        depth = weight.shape[4]
        mine = (
            lax.broadcasted_iota(jnp.int32, (8, found.shape[1]), 1) // depth
            == lax.broadcasted_iota(jnp.int32, (8, found.shape[1]), 0)
        )
        terms = []
        for n in range(pairs):
            part = found[8 * n : 8 * n + 8] * scale[w]
            g, d = divmod(n, 2)
            slopes[g, :, d, w * taps : (w + 1) * taps] = part[0:subs, 0:taps]
            terms.append(jnp.where(mine, part, 0.0).astype(jnp.bfloat16))
        matrix_copies[w].wait()
        left_side = jnp.concatenate(terms, axis=1)
        right_side = weight[w].reshape(left_side.shape[1], weight.shape[5])
        partial = jnp.dot(left_side, right_side, preferred_element_type=jnp.float32)
        partial = jnp.sum(partial, axis=0, keepdims=True)
        if w == 0:
            total_terms[...] = partial
        else:
            total_terms[...] = total_terms[...] + partial

    forwards, swaps = [], []
    done = 0
    late = []
    for m in range(strips // cores):
        n = m * cores + core
        current = []
        for d in range(2):
            sends[m][d].wait_recv()
            for k, p in enumerate(partners):
                forward = pltpu.make_async_remote_copy(
                    src_ref=land.at[d, n],
                    dst_ref=land.at[d, n],
                    send_sem=csend.at[m, d, k],
                    recv_sem=crecv.at[m, d, k],
                    device_id={"star": p},
                    device_id_type=MESH,
                )
                forward.start()
                current.append(forward)
        for forward in current:
            forward.wait_recv()
        forwards.extend(current)
        have = (m + 1) * cores
        for n in range(m * cores, have):
            for to in (n, n + strips):
                if to < strips + 2:
                    for j in range(lays):
                        field[j, to, 0:HALO, :] = land[0, n, j]
                        field[j, to, HALO + rows :, :] = land[1, n, j]
        while done < units * blocks and (
            have == strips or done * unit + unit + 2 <= have
        ):
            k, w = divmod(done, units)
            if k < blocks - 1:
                compute(done, to_outbox(done))
                copy = pltpu.make_async_remote_copy(
                    src_ref=outbox.at[done],
                    dst_ref=inbox.at[k, w],
                    send_sem=xsend.at[done],
                    recv_sem=xrecv.at[done],
                    device_id={"layer": peers[k]},
                    device_id_type=MESH,
                )
                copy.start()
                swaps.append(copy)
            else:
                compute(done, to_share(w))
                for q, copy in enumerate(swaps):
                    if q % units == w:
                        copy.wait_recv()
                if (w + 1) % group == 0:
                    slope_chunk(w // group)
            if have < strips:
                move(done)
            else:
                late.append(done)
            done += 1
    near_copies = []
    for k, peer in enumerate(near_peers):
        copy = pltpu.make_async_remote_copy(
            src_ref=total_terms,
            dst_ref=near.at[me],
            send_sem=nsend.at[k],
            recv_sem=nrecv.at[k],
            device_id=peer,
            device_id_type=MESH,
        )
        copy.start()
        near_copies.append(copy)
    near[me] = total_terms[...]
    for u in late:
        move(u)
    for copy in near_copies:
        copy.wait_recv()
    total = near[0]
    for k in range(1, count):
        total = total + near[k]
    far[tile] = total
    far_copies = []
    for k, peer in enumerate(far_peers):
        copy = pltpu.make_async_remote_copy(
            src_ref=far.at[tile],
            dst_ref=far.at[tile],
            send_sem=fsend.at[k],
            recv_sem=frecv.at[k],
            device_id=peer,
            device_id_type=MESH,
        )
        copy.start()
        far_copies.append(copy)
    for pair in sends:
        for copy in pair:
            copy.wait_send()
    for copy in forwards + swaps + near_copies:
        copy.wait_send()
    for copy in far_copies:
        copy.wait()
    total = far[0]
    for k in range(1, tiles):
        total = total + far[k]
    recon[...] = total


def tables(rows, width, block, subs, taps, depth, chunks, high_rows):
    def block_diagonal(count, piece):
        return np.kron(np.eye(count), piece)

    index = np.arange(PIX)
    gap = index[:, None] - index[None, :]
    angle = np.where(gap == 0, 1, gap) * (math.pi / PAD)
    sign = np.where(gap % 2 == 0, 1.0, -1.0)
    table = np.where(gap == 0, 0.0, PIX * sign * np.cos(angle) / np.sin(angle))
    alternate = np.where(index % 2 == 0, 1.0, -1.0)
    row_part = block_diagonal(subs, table)
    row_alt = np.pad(block_diagonal(subs, alternate[None, :]), ((0, -subs % 16), (0, 0)))
    first = np.zeros((PIX, PIX))
    first[:, 0] = 4.0 * alternate
    col_part = block_diagonal(block // PIX, table.T)
    col_alt = block_diagonal(block // PIX, first)

    def split(t):
        high = np.asarray(t.astype(jnp.bfloat16), np.float64)
        return high, t - high

    row_all = np.concatenate([*split(row_part), row_alt], axis=0)
    col_all = np.stack([*split(col_part), col_alt])
    fold = np.zeros((taps, high_rows, depth))
    for k in range(taps):
        fold[k, :, k] = 1.0
    fold = fold.reshape(taps, high_rows * depth)
    gather = np.repeat(fold, PIX, axis=0)
    spread = np.zeros((chunks, chunks * taps, high_rows * depth))
    for w in range(chunks):
        spread[w, w * taps : (w + 1) * taps] = fold
    return tuple(jnp.asarray(t.astype(jnp.bfloat16)) for t in (row_all, col_all, gather, spread))


def stay(*arrays):
    return [pltpu.with_memory_space_constraint(x, pltpu.HBM) for x in arrays]


def frame(scalars, screens, amplitude, valid, matrix):
    tiles, blocks, cores = (lax.axis_size(n) for n in ("tile", "layer", "star"))
    lays, rows, cols = screens.shape
    stars, _, subs, sub_cols, commands = matrix.shape
    strips, per_block, unit, units, group = plan(rows, cols, blocks)
    chunks = units // group
    width = group * unit * LANES
    taps = sub_cols // chunks
    depth = -(-taps // 16) * 16
    high_rows = -(-subs // 8) * 8
    block = 2 * LANES if width % (2 * LANES) == 0 else LANES
    consts = tables(rows, width, block, subs, taps, depth, chunks, high_rows)
    count = blocks * cores
    steps = strips // cores
    dma = pltpu.SemaphoreType.DMA
    bf16, f32 = jnp.bfloat16, jnp.float32
    piece = (stars, rows, unit * LANES)
    return pl.pallas_call(
        functools.partial(frame_kernel, tiles, cores, blocks, stars),
        out_shape=(
            pltpu.VMEM((lays, rows, cols), f32),
            pltpu.VMEM((stars, subs, 2, sub_cols), f32),
            pltpu.VMEM((1, commands), f32),
        ),
        in_specs=[HBM] * (len(scalars) + 4 + len(consts)),
        out_specs=(VMEM, VMEM, VMEM),
        scratch_shapes=[pltpu.SMEM(t.shape, t.dtype) for t in scalars]
        + [
            pltpu.VMEM((lays, strips + 2, rows + 2 * HALO, LANES), f32),
            pltpu.VMEM((2, strips, lays, HALO, LANES), f32),
            pltpu.VMEM((units * (blocks - 1),) + piece, f32),
            pltpu.VMEM((blocks - 1, units) + piece, f32),
            pltpu.VMEM((units,) + piece, f32),
            pltpu.VMEM(amplitude.shape, f32),
            pltpu.VMEM(valid.shape, valid.dtype),
            pltpu.VMEM((chunks, stars, 2, high_rows, depth, commands), bf16),
        ]
        + [pltpu.VMEM(t.shape, bf16) for t in consts]
        + [
            pltpu.VMEM((chunks, 8, high_rows * depth), f32),
            pltpu.VMEM((stars * rows, width), f32),
            pltpu.VMEM((stars * rows, width), bf16),
            pltpu.VMEM((stars * rows, width), bf16),
            pltpu.VMEM((stars * rows, width), bf16),
            pltpu.VMEM((stars * rows, width), bf16),
            pltpu.VMEM((2 * stars * 8, width), f32),
            pltpu.VMEM((1, commands), f32),
            pltpu.VMEM((count, 1, commands), f32),
            pltpu.VMEM((tiles, 1, commands), f32),
            dma((steps, 2)),
            dma((steps, 2)),
            dma((steps, 2, cores - 1)),
            dma((steps, 2, cores - 1)),
            dma((units * (blocks - 1),)),
            dma((units * (blocks - 1),)),
            dma((strips + 2,)),
            dma((6 + len(scalars) + chunks,)),
            dma((count - 1,)),
            dma((count - 1,)),
            dma((tiles - 1,)),
            dma((tiles - 1,)),
        ],
        compiler_params=pltpu.CompilerParams(
            collective_id=0, has_side_effects=True, vmem_limit_bytes=48 * 2**20
        ),
        name="frame",
    )(*stay(*scalars, screens, amplitude, valid, matrix, *consts))


def sine_cosine(x):
    turns = jnp.floor(x * (2.0 / math.pi) + 0.5)
    r = x - turns * 1.5703125
    r = r - turns * 4.837512969970703125e-4
    r = r - turns * 7.54978995489188216e-8
    z = r * r
    s = r + r * z * (-1.6666654611e-1 + z * (8.3321608736e-3 - z * 1.9515295891e-4))
    c = 1.0 - 0.5 * z + z * z * (
        4.166664568298827e-2 + z * (-1.388731625493765e-3 + z * 2.443315711809948e-5)
    )
    quadrant = turns.astype(jnp.int32)
    odd = (quadrant & 1) == 1
    sine = jnp.where(odd, c, s)
    cosine = jnp.where(odd, s, c)
    sine = jnp.where((quadrant & 2) == 2, -sine, sine)
    cosine = jnp.where(((quadrant + 1) & 2) == 2, -cosine, cosine)
    return sine, cosine


def halves(x):
    high = x.astype(jnp.bfloat16)
    return high, (x - high.astype(jnp.float32)).astype(jnp.bfloat16)


def product(x, y):
    return jnp.dot(x, y, preferred_element_type=jnp.float32)

def finish_kernel(moved, found, recon, previous, shifted, slopes, commands, sems):
    copies = [
        pltpu.make_async_copy(moved.at[j], shifted.at[j], sems.at[j]) for j in range(moved.shape[0])
    ]
    copies.append(pltpu.make_async_copy(found, slopes, sems.at[moved.shape[0]]))
    for copy in copies:
        copy.start()
    commands[...] = 2.0 * recon[0, :] - previous[...]
    for copy in copies:
        copy.wait()


def finish(moved, found, recon, previous):
    shifted, slopes, commands = pl.pallas_call(
        finish_kernel,
        out_shape=tuple(
            jax.ShapeDtypeStruct(x.shape, jnp.float32) for x in (moved, found, previous)
        ),
        in_specs=[ANY, ANY, VMEM, VMEM],
        out_specs=(ANY, ANY, VMEM),
        scratch_shapes=[pltpu.SemaphoreType.DMA((moved.shape[0] + 1,))],
        compiler_params=pltpu.CompilerParams(vmem_limit_bytes=2**20),
        name="finish",
    )(moved, found, recon, previous)
    return shifted, jnp.transpose(slopes, (0, 2, 1, 3)), commands


def body(
    screens,
    layer_weight,
    wind_row,
    wind_col,
    foot_row,
    foot_col,
    frac_row,
    frac_col,
    amplitude,
    valid,
    recon_matrix,
    prev_recon,
):
    scalars = (layer_weight, wind_row, wind_col, foot_row, foot_col, frac_row, frac_col)
    moved, found, recon = frame(scalars, screens, amplitude, valid, recon_matrix)
    return finish(moved, found, recon, prev_recon)


def solution(mesh):
    return jax.shard_map(
        body,
        mesh=mesh,
        in_specs=(
            P(("runs", "layer"), "tile", None),
            P(("runs", "layer")),
            P("runs"),
            P("runs"),
            P(),
            P(),
            P(),
            P(),
            P("tile", "layer"),
            P("tile", "layer"),
            P("star", None, "tile", "layer", None),
            P("runs"),
        ),
        out_specs=(
            P(("runs", "layer"), "tile", None),
            P(("runs", "star"), None, "tile", "layer"),
            P("runs"),
        ),
        check_vma=False,
    )
```

```python
import functools
import math

import jax
import jax.numpy as jnp
import numpy as np
from jax import lax
from jax.experimental import pallas as pl
from jax.experimental.pallas import tpu as pltpu
from jax.sharding import PartitionSpec as P

PIX = 16
PAD = 32
WIND = 4
FOOT = 80
LANES = 128
HALO = -(-(WIND + FOOT + 1) // 8) * 8
MESH = pl.DeviceIdType.MESH
ANY = pl.BlockSpec(memory_space=pl.ANY)
HBM = pl.BlockSpec(memory_space=pltpu.HBM)
SMEM = pl.BlockSpec(memory_space=pltpu.SMEM)
VMEM = pl.BlockSpec(memory_space=pltpu.VMEM)


def greet(peers):
    barrier = pltpu.get_barrier_semaphore()
    for peer in peers:
        pl.semaphore_signal(barrier, inc=1, device_id=peer, device_id_type=MESH)
    pl.semaphore_wait(barrier, len(peers))


def plan(rows, cols, blocks):
    strips = cols // LANES
    per_block = strips // blocks
    unit = 2 if per_block % 2 == 0 else 1
    units = per_block // unit
    group = 1 if (unit * LANES // PIX) % 16 == 0 else units
    return strips, per_block, unit, units, group


def row_parts(rows):
    parts = 3 if (rows // PIX) % 3 == 0 else 1
    reach = WIND + FOOT + 1 - (rows // parts if parts > 1 else 0)
    return parts, min(HALO, -(-reach // 8) * 8)


def frame_kernel(
    tiles, cores, blocks, stars, weights_in, wind_row_in, wind_col_in, foot_row_in, foot_col_in,
    frac_row_in, frac_col_in, screens, amplitude, valid, matrix, row_table, col_table, gather, spread,
    shifted, slopes, recon,
    weights, wind_row, wind_col, foot_row, foot_col, frac_row, frac_col,
    field, land, outbox, inbox, share, amp, mask, weight, row_tab, col_tab, gath, spre,
    scale, amp_turned, real, stack, sums, total_terms, near, far,
    zsend, zrecv, csend, crecv, xsend, xrecv, local, load, nsend, nrecv, fsend, frecv,
):
    tile, core, layer = (lax.axis_index(n) for n in ("tile", "star", "layer"))
    up, down = lax.rem(tile + 1, tiles), lax.rem(tile + tiles - 1, tiles)
    partners = [lax.rem(core + k, cores) for k in range(1, cores)]
    peers = [lax.rem(layer + k, blocks) for k in range(1, blocks)]
    count = blocks * cores
    me = layer * cores + core
    near_peers = []
    for k in range(1, count):
        rank = lax.rem(me + k, count)
        near_peers.append({"layer": rank // cores, "star": lax.rem(rank, cores)})
    far_peers = [{"tile": lax.rem(tile + k, tiles)} for k in range(1, tiles)]
    lays, rows, cols = screens.shape
    strips, per_block, unit, units, group = plan(rows, cols, blocks)
    chunks = units // group
    width = group * unit * LANES
    subs = rows // PIX
    parts, inner = row_parts(rows)
    part_rows, part_subs = rows // parts, subs // parts
    first = (layer + 1) * per_block + strips - 1
    star_start, layer_start = core * stars, layer * lays
    groups = rows // 8
    many = groups // parts
    block_rows = stars * part_rows
    block_subs = stars * part_subs
    taps = matrix.shape[3] // chunks

    def column(n, size=1):
        start = pl.multiple_of(lax.rem(first + n, strips) * LANES, LANES)
        return pl.ds(start, size * LANES)

    copies = []
    for n in range(strips + 2):
        copy = pltpu.make_async_copy(
            screens.at[:, :, column(n % strips)],
            field.at[:, n, pl.ds(HALO, rows), :],
            local.at[n],
        )
        copy.start()
        copies.append(copy)
    greet(near_peers + far_peers)
    steps = strips // cores
    last = steps - 1
    pieces = [(m, d, 0, HALO) for m in range(last) for d in range(2)]
    near_rows = [(last, 0, HALO - inner, inner), (last, 1, 0, inner)]
    far_rows = [(last, 0, 0, HALO - inner), (last, 1, inner, HALO - inner)]
    far_rows = [p for p in far_rows if p[3]]
    pieces += near_rows + far_rows
    sends = []
    for q, (m, d, low, size) in enumerate(pieces):
        n = m * cores + core
        start, peer = ((rows - HALO, up), (0, down))[d]
        copy = pltpu.make_async_remote_copy(
            src_ref=screens.at[:, pl.ds(start + low, size), column(n)],
            dst_ref=land.at[d, n, :, pl.ds(low, size), :],
            send_sem=zsend.at[q],
            recv_sem=zrecv.at[q],
            device_id={"tile": peer},
            device_id_type=MESH,
        )
        copy.start()
        sends.append(copy)
    loads = []
    for n, (source, target) in enumerate(
        ((amplitude, amp), (valid, mask), (row_table, row_tab), (col_table, col_tab),
         (gather, gath), (spread, spre), (weights_in, weights), (wind_row_in, wind_row),
         (wind_col_in, wind_col), (foot_row_in, foot_row), (foot_col_in, foot_col),
         (frac_row_in, frac_row), (frac_col_in, frac_col))
    ):
        copy = pltpu.make_async_copy(source, target, load.at[n])
        copy.start()
        loads.append(copy)
    matrix_copies = []

    def fetch_matrix():
        for w in range(chunks):
            for p in range(parts):
                for d in range(2):
                    copy = pltpu.make_async_copy(
                        matrix.at[
                            :, d, p * part_subs : (p + 1) * part_subs, w * taps : (w + 1) * taps, :
                        ],
                        weight.at[w, p, d, 0:stars, :, 0:taps, :],
                        load.at[len(loads) + len(matrix_copies)],
                    )
                    copy.start()
                    matrix_copies.append(copy)

    slots, depth = weight.shape[3], weight.shape[5]
    for w in range(chunks):
        for p in range(parts):
            for d in range(2):
                if slots > stars:
                    weight[w, p, d, stars:] = jnp.zeros(
                        (slots - stars,) + weight.shape[4:], weight.dtype
                    )
                if depth > taps:
                    weight[w, p, d, 0:stars, :, taps:, :] = jnp.zeros(
                        (stars, part_subs, depth - taps, weight.shape[6]), weight.dtype
                    )
    scale[...] = jnp.zeros_like(scale)

    def per_sub(values):
        return jnp.sum(values.reshape(-1, PIX, values.shape[1]), axis=1)

    def collect(values):
        high, low = halves(values)
        return product(high, gath[...]) + product(low, gath[...])

    for copy in loads:
        copy.wait()
    amp_turned[...] = -amp[...]
    for w in range(chunks):
        power = amp[:, w * width : (w + 1) * width]
        total = per_sub(power * power)
        lit = product(mask[...].astype(jnp.float32).astype(jnp.bfloat16), spre[w])
        ratio = lit / (collect(total) * PAD)
        for p in range(parts):
            for d in range(2):
                for g in range(stars):
                    at = d * slots * part_subs + g * part_subs
                    scale[w, p, at : at + part_subs, :] = ratio[
                        p * part_subs : (p + 1) * part_subs
                    ]
    for copy in copies:
        copy.wait()
    lane = lax.broadcasted_iota(jnp.int32, (8, LANES), 1)

    def window(j, row, base, n):
        return [field[j, base + n + k, pl.ds(row, 8), :] for k in range(unit + 1)]

    def place(start):
        base = start // LANES
        turn = start - base * LANES
        return base, turn

    def move(u):
        low = u * unit

        def move_step(i, carry):
            for j in range(lays):
                base, turn = place(LANES - wind_col[layer_start + j])
                values = window(j, HALO + i * 8 - wind_row[layer_start + j], base, low)
                rolled = [pltpu.roll(v, (LANES - turn) & (LANES - 1), 1) for v in values]
                keep = lane < LANES - turn
                for k in range(unit):
                    shifted[j, pl.ds(pl.multiple_of(i * 8, 8), 8), column(low + k + 1)] = jnp.where(
                        keep, rolled[k], rolled[k + 1]
                    )
            return carry

        lax.fori_loop(0, groups, move_step, 0, unroll=math.gcd(groups, 3))

    def compute(u, put, chosen, unroll=1):
        low = u * unit

        def pupil_step(g, carry):
            star = star_start + g
            for part in chosen:
                plain = [[None] * unit for _ in range(many)]
                ahead = [[None] * (unit + 1) for _ in range(many)]
                for j in range(lays):
                    lay = layer_start + j
                    top_row = HALO + part * part_rows + foot_row[star, lay] - wind_row[lay]
                    base, turn = place(LANES + foot_col[star, lay] - wind_col[lay])
                    gain = weights[j]
                    a, b = frac_row[star, lay], frac_col[star, lay]
                    top, bottom = gain * (1.0 - a), gain * a
                    keep = lane < LANES - turn
                    back = (LANES - turn) & (LANES - 1)
                    for r in range(many):
                        row = top_row + r * 8
                        rolled = [
                            pltpu.roll(top * x + bottom * y, back, 1)
                            for x, y in zip(
                                window(j, row, base, low), window(j, row + 1, base, low)
                            )
                        ]
                        shift = [
                            jnp.where(keep, rolled[k], rolled[k + 1]) for k in range(unit)
                        ] + [rolled[unit]]
                        for k in range(unit):
                            term = (1.0 - b) * shift[k]
                            plain[r][k] = term if j == 0 else plain[r][k] + term
                        for k in range(unit + 1):
                            term = b * shift[k]
                            ahead[r][k] = term if j == 0 else ahead[r][k] + term
                for r in range(many):
                    beside = [pltpu.roll(v, LANES - 1, 1) for v in ahead[r]]
                    for k in range(unit):
                        value = plain[r][k] + jnp.where(
                            lane < LANES - 1, beside[k], beside[k + 1]
                        )
                        at = pl.ds(part * part_rows + r * 8, 8)
                        put(g, at, k, value)
            return carry

        lax.fori_loop(0, stars, pupil_step, 0, unroll=unroll)

    def to_outbox(u):
        def put(g, at, k, value):
            outbox[u, g, at, k * LANES : (k + 1) * LANES] = value

        return put

    def to_share(w):
        def put(g, at, k, value):
            share[w, g, at, k * LANES : (k + 1) * LANES] = value

        return put

    block = col_tab.shape[1]

    high_half = slots * part_subs

    def fields(slot, w, p):
        left = w * width
        for n in range(block_subs):
            g, i = divmod(n, part_subs)
            at = slice((p * part_subs + i) * PIX, (p * part_subs + i + 1) * PIX)
            strip = []
            for v in range(w * group, (w + 1) * group):
                phase = share[v, g, at, :]
                for k in range(blocks - 1):
                    phase = phase + inbox[k, v, g, at, :]
                strip.append(phase)
            sine, cosine, turns = sine_cosine(jnp.concatenate(strip, axis=1))
            power = jnp.where(
                (turns.astype(jnp.int32) & 1) == 1,
                amp_turned[at, left : left + width],
                amp[at, left : left + width],
            )
            a, b = power * cosine, power * sine
            real[slot, n * PIX : (n + 1) * PIX, :] = a
            for q, value in enumerate(halves(b) + halves(a)):
                low = q * block_rows + n * PIX
                stack[slot, low : low + PIX, :] = value

    def centroids(slot, w, p):
        a = real[slot]
        found = product(row_tab[...], stack[slot])
        turned = found[0:block_rows] + found[block_rows : 2 * block_rows]
        alt_a = found[2 * block_rows : 2 * block_rows + block_subs]
        step = (found.shape[0] - 2 * block_rows) // 2
        alt_b = found[2 * block_rows + step : 2 * block_rows + step + block_subs]
        sums[slot, 0:block_subs, :] = per_sub(a * turned) - PIX * (alt_a * alt_a + alt_b * alt_b)
        if high_half > block_subs:
            fill = jnp.zeros((high_half - block_subs, width), jnp.float32)
            sums[slot, block_subs:high_half, :] = fill
            sums[slot, high_half + block_subs :, :] = fill
        b_high, b_low, a_high, a_low = (
            stack[slot, q * block_rows : (q + 1) * block_rows, :] for q in range(4)
        )
        across = []
        for k in range(width // block):
            cut = slice(k * block, (k + 1) * block)
            turned = product(
                jnp.concatenate([b_high[:, cut], b_low[:, cut], b_high[:, cut]], axis=1),
                col_tab[0 : 3 * block, :],
            )
            alt = product(
                jnp.concatenate([x[:, cut] for x in (a_high, a_low, b_high, b_low)], axis=1),
                col_tab[3 * block :, :],
            )
            across.append(a[:, cut] * turned - alt * alt)
        sums[slot, high_half : high_half + block_subs, :] = per_sub(
            jnp.concatenate(across, axis=1)
        )
        found = collect(sums[slot]) * scale[w, p]
        for d in range(2):
            for g in range(stars):
                at = d * high_half + g * part_subs
                for i in range(part_subs):
                    slopes[g, p * part_subs + i, d : d + 1, w * taps : (w + 1) * taps] = found[
                        at + i : at + i + 1, w * depth : w * depth + taps
                    ]
        mine = (
            lax.broadcasted_iota(jnp.int32, found.shape, 1) // depth
            == lax.broadcasted_iota(jnp.int32, found.shape, 0)
        )
        return jnp.where(mine, found, 0.0).astype(jnp.bfloat16)

    def slope_parts(chosen):
        terms = []
        slots_here = real.shape[0]
        for n, (w, p) in enumerate(chosen):
            if n == 0:
                fields(0, w, p)
            if n + 1 < len(chosen):
                fields((n + 1) % slots_here, *chosen[n + 1])
            terms.append((w, p, centroids(n % slots_here, w, p)))
        return terms

    started = []

    def project(terms):
        for w, p, _ in terms:
            for d in range(2):
                matrix_copies[(w * parts + p) * 2 + d].wait()
        partial = None
        for w, p, left_side in terms:
            right_side = weight[w, p].reshape(left_side.shape[1], weight.shape[6])
            value = jnp.dot(left_side, right_side, preferred_element_type=jnp.float32)
            partial = value if partial is None else partial + value
        partial = jnp.sum(partial, axis=0, keepdims=True)
        if started:
            total_terms[...] = total_terms[...] + partial
        else:
            total_terms[...] = partial
            started.append(True)

    forwards, swaps = [], []

    passing = {}

    def send_on(chosen):
        for q in chosen:
            m, d, low, size = pieces[q]
            mine = land.at[d, m * cores + core, :, pl.ds(low, size), :]
            sends[q].wait_recv()
            passing[q] = []
            for k, p in enumerate(partners):
                forward = pltpu.make_async_remote_copy(
                    src_ref=mine,
                    dst_ref=mine,
                    send_sem=csend.at[q, k],
                    recv_sem=crecv.at[q, k],
                    device_id={"star": p},
                    device_id_type=MESH,
                )
                forward.start()
                passing[q].append(forward)

    def take(chosen):
        for q in chosen:
            for forward in passing[q]:
                forward.wait_recv()
                forwards.append(forward)
            m, d, low, size = pieces[q]
            base = low + d * (HALO + rows)
            for n in range(m * cores, (m + 1) * cores):
                for to in (n, n + strips):
                    if to < strips + 2:
                        for j in range(lays):
                            field[j, to, base : base + size, :] = land[d, n, j, low : low + size, :]

    def own(u, chosen, unroll=1):
        k, w = divmod(u, units)
        compute(u, to_share(w), chosen, unroll)

    def arrived(w):
        for q, copy in enumerate(swaps):
            if q % units == w:
                copy.wait_recv()

    whole = list(range(parts))
    done = 0
    for m in range(last):
        send_on([2 * m, 2 * m + 1])
        take([2 * m, 2 * m + 1])
        if m == 0:
            fetch_matrix()
        have = (m + 1) * cores
        while done < units * blocks and done * unit + unit + 2 <= have:
            k, w = divmod(done, units)
            if k < blocks - 1:
                compute(done, to_outbox(done), whole)
                copy = pltpu.make_async_remote_copy(
                    src_ref=outbox.at[done],
                    dst_ref=inbox.at[k, w],
                    send_sem=xsend.at[done],
                    recv_sem=xrecv.at[done],
                    device_id={"layer": peers[k]},
                    device_id_type=MESH,
                )
                copy.start()
                swaps.append(copy)
            else:
                own(done, whole)
                arrived(w)
                if (w + 1) % group == 0:
                    c = w // group
                    project(slope_parts([(c, p) for p in whole]))
            move(done)
            done += 1
    late = list(range(done, units * blocks))
    late_chunks = sorted({(u % units) // group for u in late})
    split = last * 2 + 2 < len(pieces)
    send_on([2 * last, 2 * last + 1])
    take([2 * last, 2 * last + 1])
    if split:
        outer = [2 * last + 2, 2 * last + 3]
        middle = whole[1:-1]
        for u in late:
            own(u, middle, True)
            arrived(u % units)
        terms = slope_parts([(c, p) for c in late_chunks for p in middle])
        send_on(outer)
        project(terms)
        take(outer)
    rest = [whole[0], whole[-1]] if split else whole
    for u in late:
        own(u, rest, True)
        if not split:
            arrived(u % units)
    project(slope_parts([(c, p) for c in late_chunks for p in rest]))
    near_copies = []
    for k, peer in enumerate(near_peers):
        copy = pltpu.make_async_remote_copy(
            src_ref=total_terms,
            dst_ref=near.at[me],
            send_sem=nsend.at[k],
            recv_sem=nrecv.at[k],
            device_id=peer,
            device_id_type=MESH,
        )
        copy.start()
        near_copies.append(copy)
    near[me] = total_terms[...]
    for u in late:
        move(u)
    for copy in near_copies:
        copy.wait_recv()
    total = near[0]
    for k in range(1, count):
        total = total + near[k]
    far[tile] = total
    far_copies = []
    for k, peer in enumerate(far_peers):
        copy = pltpu.make_async_remote_copy(
            src_ref=far.at[tile],
            dst_ref=far.at[tile],
            send_sem=fsend.at[k],
            recv_sem=frecv.at[k],
            device_id=peer,
            device_id_type=MESH,
        )
        copy.start()
        far_copies.append(copy)
    for copy in sends + forwards + swaps + near_copies:
        copy.wait_send()
    for copy in far_copies:
        copy.wait()
    total = far[0]
    for k in range(1, tiles):
        total = total + far[k]
    recon[...] = total


def tables(block, block_subs, taps, depth, chunks, lanes):
    def block_diagonal(count, piece):
        return np.kron(np.eye(count), piece)

    index = np.arange(PIX)
    gap = index[:, None] - index[None, :]
    angle = np.where(gap == 0, 1, gap) * (math.pi / PAD)
    sign = np.where(gap % 2 == 0, 1.0, -1.0)
    table = np.where(gap == 0, 0.0, PIX * sign * np.cos(angle) / np.sin(angle))
    alternate = np.where(index % 2 == 0, 1.0, -1.0)
    def split(t):
        high = np.asarray(t.astype(jnp.bfloat16), np.float64)
        return high, t - high

    row_high, row_low = split(block_diagonal(block_subs, 2.0 * table))
    row_alt = np.pad(block_diagonal(block_subs, alternate[None, :]), ((0, -block_subs % 16), (0, 0)))
    none, thin = np.zeros_like(row_high), np.zeros_like(row_alt)
    row_all = np.block([
        [row_high, row_high, none, none],
        [row_low, none, none, none],
        [thin, thin, row_alt, row_alt],
        [row_alt, row_alt, thin, thin],
    ])
    ends = np.zeros((2, PIX, PIX))
    for n in range(2):
        ends[n, :, n] = 4.0 * alternate
    count = block // PIX
    col_high, col_low = split(block_diagonal(count, 2.0 * table.T))
    alt_a, alt_b = (block_diagonal(count, end) for end in ends)
    col_all = np.concatenate([col_high, col_high, col_low, alt_a, alt_a, alt_b, alt_b], axis=0)
    fold = np.zeros((taps, lanes // depth, depth))
    for k in range(taps):
        fold[k, :, k] = 1.0
    fold = fold.reshape(taps, lanes)
    gather = np.repeat(fold, PIX, axis=0)
    spread = np.zeros((chunks, chunks * taps, lanes))
    for w in range(chunks):
        spread[w, w * taps : (w + 1) * taps] = fold
    return tuple(jnp.asarray(t.astype(jnp.bfloat16)) for t in (row_all, col_all, gather, spread))


def stay(*arrays):
    return [pltpu.with_memory_space_constraint(x, pltpu.HBM) for x in arrays]


def frame(scalars, screens, amplitude, valid, matrix):
    tiles, blocks, cores = (lax.axis_size(n) for n in ("tile", "layer", "star"))
    lays, rows, cols = screens.shape
    stars, _, subs, sub_cols, commands = matrix.shape
    strips, per_block, unit, units, group = plan(rows, cols, blocks)
    chunks = units // group
    width = group * unit * LANES
    taps = sub_cols // chunks
    depth = -(-taps // 16) * 16
    parts, inner = row_parts(rows)
    part_subs = subs // parts
    slots = stars
    while slots * part_subs % 8:
        slots += 1
    lanes = 2 * slots * part_subs * depth
    pieces = 2 * (strips // cores) + (2 if inner < HALO else 0)
    block = 2 * LANES if width % (2 * LANES) == 0 else LANES
    consts = tables(block, stars * part_subs, taps, depth, chunks, lanes)
    count = blocks * cores
    dma = pltpu.SemaphoreType.DMA
    bf16, f32 = jnp.bfloat16, jnp.float32
    piece = (stars, rows, unit * LANES)
    return pl.pallas_call(
        functools.partial(frame_kernel, tiles, cores, blocks, stars),
        out_shape=(
            pltpu.VMEM((lays, rows, cols), f32),
            pltpu.VMEM((stars, subs, 2, sub_cols), f32),
            pltpu.VMEM((1, commands), f32),
        ),
        in_specs=[HBM] * (len(scalars) + 4 + len(consts)),
        out_specs=(VMEM, VMEM, VMEM),
        scratch_shapes=[pltpu.SMEM(t.shape, t.dtype) for t in scalars]
        + [
            pltpu.VMEM((lays, strips + 2, rows + 2 * HALO, LANES), f32),
            pltpu.VMEM((2, strips, lays, HALO, LANES), f32),
            pltpu.VMEM((units * (blocks - 1),) + piece, f32),
            pltpu.VMEM((blocks - 1, units) + piece, f32),
            pltpu.VMEM((units,) + piece, f32),
            pltpu.VMEM(amplitude.shape, f32),
            pltpu.VMEM(valid.shape, valid.dtype),
            pltpu.VMEM((chunks, parts, 2, slots, part_subs, depth, commands), bf16),
        ]
        + [pltpu.VMEM(t.shape, bf16) for t in consts]
        + [
            pltpu.VMEM((chunks, parts, 2 * slots * part_subs, lanes), f32),
            pltpu.VMEM(amplitude.shape, f32),
            pltpu.VMEM((4, stars * rows // parts, width), f32),
            pltpu.VMEM((4, 4 * stars * rows // parts, width), bf16),
            pltpu.VMEM((4, 2 * slots * part_subs, width), f32),
            pltpu.VMEM((1, commands), f32),
            pltpu.VMEM((count, 1, commands), f32),
            pltpu.VMEM((tiles, 1, commands), f32),
            dma((pieces,)),
            dma((pieces,)),
            dma((pieces, cores - 1)),
            dma((pieces, cores - 1)),
            dma((units * (blocks - 1),)),
            dma((units * (blocks - 1),)),
            dma((strips + 2,)),
            dma((6 + len(scalars) + chunks * parts * 2,)),
            dma((count - 1,)),
            dma((count - 1,)),
            dma((tiles - 1,)),
            dma((tiles - 1,)),
        ],
        compiler_params=pltpu.CompilerParams(
            collective_id=0, has_side_effects=True, vmem_limit_bytes=48 * 2**20
        ),
        name="frame",
    )(*stay(*scalars, screens, amplitude, valid, matrix, *consts))


def horner(z, first, *rest):
    value = first
    for c in rest:
        value = value * z + c
    return value


def sine_cosine(x):
    turns = jnp.floor(x * (1.0 / math.pi) + 0.5)
    r = x - turns * 3.140625
    r = r - turns * 9.67653589793e-4
    z = r * r
    s = r + r * (z * horner(z, 2.63541936e-6, -1.98230239e-4, 8.33324557e-3, -1.66666661e-1))
    c = 1.0 + z * horner(
        z, -2.63066288e-7, 2.47750852e-5, -1.38886609e-3, 4.166666e-2, -0.5
    )
    return s, c, turns


def halves(x):
    high = x.astype(jnp.bfloat16)
    return high, (x - high.astype(jnp.float32)).astype(jnp.bfloat16)


def product(x, y):
    return jnp.dot(x, y, preferred_element_type=jnp.float32)

def finish_kernel(moved, found, recon, previous, shifted, slopes, commands, sems):
    copies = [
        pltpu.make_async_copy(moved.at[j], shifted.at[j], sems.at[j]) for j in range(moved.shape[0])
    ]
    copies.append(pltpu.make_async_copy(found, slopes, sems.at[moved.shape[0]]))
    for copy in copies:
        copy.start()
    commands[...] = 2.0 * recon[0, :] - previous[...]
    for copy in copies:
        copy.wait()


def finish(moved, found, recon, previous):
    shifted, slopes, commands = pl.pallas_call(
        finish_kernel,
        out_shape=tuple(
            jax.ShapeDtypeStruct(x.shape, jnp.float32) for x in (moved, found, previous)
        ),
        in_specs=[ANY, ANY, VMEM, VMEM],
        out_specs=(ANY, ANY, VMEM),
        scratch_shapes=[pltpu.SemaphoreType.DMA((moved.shape[0] + 1,))],
        compiler_params=pltpu.CompilerParams(vmem_limit_bytes=2**20),
        name="finish",
    )(moved, found, recon, previous)
    return shifted, jnp.transpose(slopes, (0, 2, 1, 3)), commands


def body(
    screens,
    layer_weight,
    wind_row,
    wind_col,
    foot_row,
    foot_col,
    frac_row,
    frac_col,
    amplitude,
    valid,
    recon_matrix,
    prev_recon,
):
    scalars = (layer_weight, wind_row, wind_col, foot_row, foot_col, frac_row, frac_col)
    moved, found, recon = frame(scalars, screens, amplitude, valid, recon_matrix)
    return finish(moved, found, recon, prev_recon)


def solution(mesh):
    return jax.shard_map(
        body,
        mesh=mesh,
        in_specs=(
            P(("runs", "layer"), "tile", None),
            P(("runs", "layer")),
            P("runs"),
            P("runs"),
            P(),
            P(),
            P(),
            P(),
            P("tile", "layer"),
            P("tile", "layer"),
            P("star", None, "tile", "layer", None),
            P("runs"),
        ),
        out_specs=(
            P(("runs", "layer"), "tile", None),
            P(("runs", "star"), None, "tile", "layer"),
            P("runs"),
        ),
        check_vma=False,
    )
```

```python
import functools
import math

import jax
import jax.numpy as jnp
import numpy as np
from jax import lax
from jax.experimental import pallas as pl
from jax.experimental.pallas import tpu as pltpu
from jax.sharding import PartitionSpec as P

PIX = 16
PAD = 32
WIND = 4
FOOT = 80
LANES = 128
DEPTH = WIND + FOOT
HALO = -(-DEPTH // 8) * 8
DIRECT = DEPTH // 8 * 8
EXTRA = DEPTH - DIRECT
PACK = 8 // EXTRA
MESH = pl.DeviceIdType.MESH
ANY = pl.BlockSpec(memory_space=pl.ANY)
HBM = pl.BlockSpec(memory_space=pltpu.HBM)
SMEM = pl.BlockSpec(memory_space=pltpu.SMEM)
VMEM = pl.BlockSpec(memory_space=pltpu.VMEM)


def greet(peers):
    barrier = pltpu.get_barrier_semaphore()
    for peer in peers:
        pl.semaphore_signal(barrier, inc=1, device_id=peer, device_id_type=MESH)
    pl.semaphore_wait(barrier, len(peers))


def plan(rows, cols, blocks):
    strips = cols // LANES
    per_block = strips // blocks
    unit = 2 if per_block % 2 == 0 else 1
    units = per_block // unit
    group = 1 if (unit * LANES // PIX) % 16 == 0 else units
    return strips, per_block, unit, units, group


def row_parts(rows):
    parts = 3 if (rows // PIX) % 3 == 0 else 1
    reach = WIND + FOOT + 1 - (rows // parts if parts > 1 else 0)
    return parts, min(DIRECT, -(-reach // 8) * 8)


def frame_kernel(
    tiles, cores, blocks, stars, weights_in, wind_row_in, wind_col_in, foot_row_in, foot_col_in,
    frac_row_in, frac_col_in, screens, amplitude, valid, matrix, row_table, col_table, gather, spread,
    shifted, slopes, recon,
    weights, wind_row, wind_col, foot_row, foot_col, frac_row, frac_col,
    field, land, rim, rim_land, outbox, inbox, share, amp, mask, weight, row_tab, col_tab, gath, spre,
    scale, amp_turned, real, stack, sums, total_terms, near, far,
    zsend, zrecv, csend, crecv, esend, erecv, fesend, ferecv, xsend, xrecv, local, load, nsend, nrecv, fsend, frecv,
):
    tile, core, layer = (lax.axis_index(n) for n in ("tile", "star", "layer"))
    up, down = lax.rem(tile + 1, tiles), lax.rem(tile + tiles - 1, tiles)
    partners = [lax.rem(core + k, cores) for k in range(1, cores)]
    peers = [lax.rem(layer + k, blocks) for k in range(1, blocks)]
    count = blocks * cores
    me = layer * cores + core
    near_peers = []
    for k in range(1, count):
        rank = lax.rem(me + k, count)
        near_peers.append({"layer": rank // cores, "star": lax.rem(rank, cores)})
    far_peers = [{"tile": lax.rem(tile + k, tiles)} for k in range(1, tiles)]
    lays, rows, cols = screens.shape
    strips, per_block, unit, units, group = plan(rows, cols, blocks)
    chunks = units // group
    width = group * unit * LANES
    subs = rows // PIX
    parts, inner = row_parts(rows)
    part_rows, part_subs = rows // parts, subs // parts
    first = (layer + 1) * per_block + strips - 1
    star_start, layer_start = core * stars, layer * lays
    groups = rows // 8
    many = groups // parts
    block_rows = stars * part_rows
    block_subs = stars * part_subs
    taps = matrix.shape[3] // chunks

    def column(n, size=1):
        start = pl.multiple_of(lax.rem(first + n, strips) * LANES, LANES)
        return pl.ds(start, size * LANES)

    copies = []
    for n in range(strips + 2):
        copy = pltpu.make_async_copy(
            screens.at[:, :, column(n % strips)],
            field.at[:, n, pl.ds(HALO, rows), :],
            local.at[n],
        )
        copy.start()
        copies.append(copy)
    greet(near_peers + far_peers)
    steps = strips // cores
    last = steps - 1
    pieces = [(m, d, 0, DIRECT) for m in range(last) for d in range(2)]
    near_rows = [(last, 0, DIRECT - inner, inner), (last, 1, 0, inner)]
    far_rows = [(last, 0, 0, DIRECT - inner), (last, 1, inner, DIRECT - inner)]
    far_rows = [p for p in far_rows if p[3]]
    pieces += near_rows + far_rows
    targets = (up, down)
    sends = []

    def send(q):
        m, d, low, size = pieces[q]
        n = m * cores + core
        copy = pltpu.make_async_remote_copy(
            src_ref=screens.at[:, pl.ds((rows - DIRECT, 0)[d] + low, size), column(n)],
            dst_ref=land.at[d, n, :, pl.ds(low, size), :],
            send_sem=zsend.at[q],
            recv_sem=zrecv.at[q],
            device_id={"tile": targets[d]},
            device_id_type=MESH,
        )
        copy.start()
        sends.append(copy)

    for q in range(2):
        send(q)
    for copy in copies:
        copy.wait()
    for d, start in enumerate((rows - DEPTH, DIRECT)):
        for m in range(steps):
            for j in range(lays):
                e = m * lays + j
                to = slice(e % PACK * EXTRA, (e % PACK + 1) * EXTRA)
                rim[d, e // PACK, to, :] = field[
                    j, m * cores + core, HALO + start : HALO + start + EXTRA, :
                ]
    rims = []
    for d in range(2):
        copy = pltpu.make_async_remote_copy(
            src_ref=rim.at[d],
            dst_ref=rim_land.at[d, core],
            send_sem=esend.at[d],
            recv_sem=erecv.at[d],
            device_id={"tile": targets[d]},
            device_id_type=MESH,
        )
        copy.start()
        rims.append(copy)
    for q in range(2, len(pieces)):
        send(q)
    loads = []
    for n, (source, target) in enumerate(
        ((amplitude, amp), (valid, mask), (row_table, row_tab), (col_table, col_tab),
         (gather, gath), (spread, spre), (weights_in, weights), (wind_row_in, wind_row),
         (wind_col_in, wind_col), (foot_row_in, foot_row), (foot_col_in, foot_col),
         (frac_row_in, frac_row), (frac_col_in, frac_col))
    ):
        copy = pltpu.make_async_copy(source, target, load.at[n])
        copy.start()
        loads.append(copy)
    matrix_copies = []

    def fetch_matrix():
        for w in range(chunks):
            for p in range(parts):
                for d in range(2):
                    copy = pltpu.make_async_copy(
                        matrix.at[
                            :, d, p * part_subs : (p + 1) * part_subs, w * taps : (w + 1) * taps, :
                        ],
                        weight.at[w, p, d, 0:stars, :, 0:taps, :],
                        load.at[len(loads) + len(matrix_copies)],
                    )
                    copy.start()
                    matrix_copies.append(copy)

    slots, depth = weight.shape[3], weight.shape[5]
    for w in range(chunks):
        for p in range(parts):
            for d in range(2):
                if slots > stars:
                    weight[w, p, d, stars:] = jnp.zeros(
                        (slots - stars,) + weight.shape[4:], weight.dtype
                    )
                if depth > taps:
                    weight[w, p, d, 0:stars, :, taps:, :] = jnp.zeros(
                        (stars, part_subs, depth - taps, weight.shape[6]), weight.dtype
                    )
    scale[...] = jnp.zeros_like(scale)

    def per_sub(values):
        return jnp.sum(values.reshape(-1, PIX, values.shape[1]), axis=1)

    def collect(values):
        high, low = halves(values)
        return product(high, gath[...]) + product(low, gath[...])

    for copy in loads:
        copy.wait()
    amp_turned[...] = -amp[...]
    for w in range(chunks):
        power = amp[:, w * width : (w + 1) * width]
        total = per_sub(power * power)
        lit = product(mask[...].astype(jnp.float32).astype(jnp.bfloat16), spre[w])
        ratio = lit / (collect(total) * PAD)
        for p in range(parts):
            for d in range(2):
                for g in range(stars):
                    at = d * slots * part_subs + g * part_subs
                    scale[w, p, at : at + part_subs, :] = ratio[
                        p * part_subs : (p + 1) * part_subs
                    ]
    lane = lax.broadcasted_iota(jnp.int32, (8, LANES), 1)

    def window(j, row, base, n):
        return [field[j, base + n + k, pl.ds(row, 8), :] for k in range(unit + 1)]

    def place(start):
        base = start // LANES
        turn = start - base * LANES
        return base, turn

    def move(u):
        low = u * unit

        def move_step(i, carry):
            for j in range(lays):
                base, turn = place(LANES - wind_col[layer_start + j])
                values = window(j, HALO + i * 8 - wind_row[layer_start + j], base, low)
                rolled = [pltpu.roll(v, (LANES - turn) & (LANES - 1), 1) for v in values]
                keep = lane < LANES - turn
                for k in range(unit):
                    shifted[j, pl.ds(pl.multiple_of(i * 8, 8), 8), column(low + k + 1)] = jnp.where(
                        keep, rolled[k], rolled[k + 1]
                    )
            return carry

        lax.fori_loop(0, groups, move_step, 0, unroll=math.gcd(groups, 3))

    def compute(u, put, chosen, unroll=1):
        low = u * unit

        def pupil_step(g, carry):
            star = star_start + g
            for part in chosen:
                plain = [[None] * unit for _ in range(many)]
                ahead = [[None] * (unit + 1) for _ in range(many)]
                for j in range(lays):
                    lay = layer_start + j
                    top_row = HALO + part * part_rows + foot_row[star, lay] - wind_row[lay]
                    base, turn = place(LANES + foot_col[star, lay] - wind_col[lay])
                    gain = weights[j]
                    a, b = frac_row[star, lay], frac_col[star, lay]
                    top, bottom = gain * (1.0 - a), gain * a
                    keep = lane < LANES - turn
                    back = (LANES - turn) & (LANES - 1)
                    for r in range(many):
                        row = top_row + r * 8
                        rolled = [
                            pltpu.roll(top * x + bottom * y, back, 1)
                            for x, y in zip(
                                window(j, row, base, low), window(j, row + 1, base, low)
                            )
                        ]
                        shift = [
                            jnp.where(keep, rolled[k], rolled[k + 1]) for k in range(unit)
                        ] + [rolled[unit]]
                        for k in range(unit):
                            term = (1.0 - b) * shift[k]
                            plain[r][k] = term if j == 0 else plain[r][k] + term
                        for k in range(unit + 1):
                            term = b * shift[k]
                            ahead[r][k] = term if j == 0 else ahead[r][k] + term
                for r in range(many):
                    beside = [pltpu.roll(v, LANES - 1, 1) for v in ahead[r]]
                    for k in range(unit):
                        value = plain[r][k] + jnp.where(
                            lane < LANES - 1, beside[k], beside[k + 1]
                        )
                        at = pl.ds(part * part_rows + r * 8, 8)
                        put(g, at, k, value)
            return carry

        lax.fori_loop(0, stars, pupil_step, 0, unroll=unroll)

    def to_outbox(u):
        def put(g, at, k, value):
            outbox[u, g, at, k * LANES : (k + 1) * LANES] = value

        return put

    def to_share(w):
        def put(g, at, k, value):
            share[w, g, at, k * LANES : (k + 1) * LANES] = value

        return put

    block = col_tab.shape[1]

    high_half = slots * part_subs

    def fields(slot, w, p):
        left = w * width
        for n in range(block_subs):
            g, i = divmod(n, part_subs)
            at = slice((p * part_subs + i) * PIX, (p * part_subs + i + 1) * PIX)
            strip = []
            for v in range(w * group, (w + 1) * group):
                phase = share[v, g, at, :]
                for k in range(blocks - 1):
                    phase = phase + inbox[k, v, g, at, :]
                strip.append(phase)
            sine, cosine, turns = sine_cosine(jnp.concatenate(strip, axis=1))
            power = jnp.where(
                (turns.astype(jnp.int32) & 1) == 1,
                amp_turned[at, left : left + width],
                amp[at, left : left + width],
            )
            a, b = power * cosine, power * sine
            real[slot, n * PIX : (n + 1) * PIX, :] = a
            for q, value in enumerate(halves(b) + halves(a)):
                low = q * block_rows + n * PIX
                stack[slot, low : low + PIX, :] = value

    def centroids(slot, w, p):
        a = real[slot]
        found = product(row_tab[...], stack[slot])
        turned = found[0:block_rows] + found[block_rows : 2 * block_rows]
        alt_a = found[2 * block_rows : 2 * block_rows + block_subs]
        step = (found.shape[0] - 2 * block_rows) // 2
        alt_b = found[2 * block_rows + step : 2 * block_rows + step + block_subs]
        sums[slot, 0:block_subs, :] = per_sub(a * turned) - PIX * (alt_a * alt_a + alt_b * alt_b)
        if high_half > block_subs:
            fill = jnp.zeros((high_half - block_subs, width), jnp.float32)
            sums[slot, block_subs:high_half, :] = fill
            sums[slot, high_half + block_subs :, :] = fill
        b_high, b_low, a_high, a_low = (
            stack[slot, q * block_rows : (q + 1) * block_rows, :] for q in range(4)
        )
        across = []
        for k in range(width // block):
            cut = slice(k * block, (k + 1) * block)
            turned = product(
                jnp.concatenate([b_high[:, cut], b_low[:, cut], b_high[:, cut]], axis=1),
                col_tab[0 : 3 * block, :],
            )
            alt = product(
                jnp.concatenate([x[:, cut] for x in (a_high, a_low, b_high, b_low)], axis=1),
                col_tab[3 * block :, :],
            )
            across.append(a[:, cut] * turned - alt * alt)
        sums[slot, high_half : high_half + block_subs, :] = per_sub(
            jnp.concatenate(across, axis=1)
        )
        found = collect(sums[slot]) * scale[w, p]
        for d in range(2):
            for g in range(stars):
                at = d * high_half + g * part_subs
                for i in range(part_subs):
                    slopes[g, p * part_subs + i, d : d + 1, w * taps : (w + 1) * taps] = found[
                        at + i : at + i + 1, w * depth : w * depth + taps
                    ]
        mine = (
            lax.broadcasted_iota(jnp.int32, found.shape, 1) // depth
            == lax.broadcasted_iota(jnp.int32, found.shape, 0)
        )
        return jnp.where(mine, found, 0.0).astype(jnp.bfloat16)

    def slope_parts(chosen):
        terms = []
        slots_here = real.shape[0]
        for n, (w, p) in enumerate(chosen):
            if n == 0:
                fields(0, w, p)
            if n + 1 < len(chosen):
                fields((n + 1) % slots_here, *chosen[n + 1])
            terms.append((w, p, centroids(n % slots_here, w, p)))
        return terms

    started = []

    def project(terms):
        for w, p, _ in terms:
            for d in range(2):
                matrix_copies[(w * parts + p) * 2 + d].wait()
        partial = None
        for w, p, left_side in terms:
            right_side = weight[w, p].reshape(left_side.shape[1], weight.shape[6])
            value = jnp.dot(left_side, right_side, preferred_element_type=jnp.float32)
            partial = value if partial is None else partial + value
        partial = jnp.sum(partial, axis=0, keepdims=True)
        if started:
            total_terms[...] = total_terms[...] + partial
        else:
            total_terms[...] = partial
            started.append(True)

    forwards, swaps = [], []

    passing = {}

    def send_on(chosen):
        for q in chosen:
            m, d, low, size = pieces[q]
            mine = land.at[d, m * cores + core, :, pl.ds(low, size), :]
            sends[q].wait_recv()
            passing[q] = []
            for k, p in enumerate(partners):
                forward = pltpu.make_async_remote_copy(
                    src_ref=mine,
                    dst_ref=mine,
                    send_sem=csend.at[q, k],
                    recv_sem=crecv.at[q, k],
                    device_id={"star": p},
                    device_id_type=MESH,
                )
                forward.start()
                passing[q].append(forward)

    def take(chosen):
        for q in chosen:
            for forward in passing[q]:
                forward.wait_recv()
                forwards.append(forward)
            m, d, low, size = pieces[q]
            base = low + (HALO - DIRECT, HALO + rows)[d]
            for n in range(m * cores, (m + 1) * cores):
                for to in (n, n + strips):
                    if to < strips + 2:
                        for j in range(lays):
                            field[j, to, base : base + size, :] = land[d, n, j, low : low + size, :]

    def take_rims():
        for d in range(2):
            rims[d].wait_recv()
            for k, p in enumerate(partners):
                forward = pltpu.make_async_remote_copy(
                    src_ref=rim_land.at[d, core],
                    dst_ref=rim_land.at[d, core],
                    send_sem=fesend.at[d, k],
                    recv_sem=ferecv.at[d, k],
                    device_id={"star": p},
                    device_id_type=MESH,
                )
                forward.start()
                forwards.append(forward)
        for forward in forwards[-2 * len(partners) :]:
            forward.wait_recv()
        for d, base in enumerate((HALO - DEPTH, HALO + rows + DIRECT)):
            for m in range(steps):
                for j in range(lays):
                    e = m * lays + j
                    at = slice(e % PACK * EXTRA, (e % PACK + 1) * EXTRA)
                    for c in range(cores):
                        n = m * cores + c
                        for to in (n, n + strips):
                            if to < strips + 2:
                                field[j, to, base : base + EXTRA, :] = rim_land[d, c, e // PACK, at, :]

    def own(u, chosen, unroll=1):
        k, w = divmod(u, units)
        compute(u, to_share(w), chosen, unroll)

    def arrived(w):
        for q, copy in enumerate(swaps):
            if q % units == w:
                copy.wait_recv()

    whole = list(range(parts))
    done = 0
    for m in range(last):
        send_on([2 * m, 2 * m + 1])
        take([2 * m, 2 * m + 1])
        if m == 0:
            take_rims()
            fetch_matrix()
        have = (m + 1) * cores
        while done < units * blocks and done * unit + unit + 2 <= have:
            k, w = divmod(done, units)
            if k < blocks - 1:
                compute(done, to_outbox(done), whole)
                copy = pltpu.make_async_remote_copy(
                    src_ref=outbox.at[done],
                    dst_ref=inbox.at[k, w],
                    send_sem=xsend.at[done],
                    recv_sem=xrecv.at[done],
                    device_id={"layer": peers[k]},
                    device_id_type=MESH,
                )
                copy.start()
                swaps.append(copy)
            else:
                own(done, whole)
                arrived(w)
                if (w + 1) % group == 0:
                    c = w // group
                    project(slope_parts([(c, p) for p in whole]))
            move(done)
            done += 1
    late = list(range(done, units * blocks))
    late_chunks = sorted({(u % units) // group for u in late})
    split = last * 2 + 2 < len(pieces)
    send_on([2 * last, 2 * last + 1])
    take([2 * last, 2 * last + 1])
    if split:
        outer = [2 * last + 2, 2 * last + 3]
        middle = whole[1:-1]
        for u in late:
            own(u, middle, True)
            arrived(u % units)
        terms = slope_parts([(c, p) for c in late_chunks for p in middle])
        send_on(outer)
        project(terms)
        take(outer)
    rest = [whole[0], whole[-1]] if split else whole
    for u in late:
        own(u, rest, True)
        if not split:
            arrived(u % units)
    project(slope_parts([(c, p) for c in late_chunks for p in rest]))
    near_copies = []
    for k, peer in enumerate(near_peers):
        copy = pltpu.make_async_remote_copy(
            src_ref=total_terms,
            dst_ref=near.at[me],
            send_sem=nsend.at[k],
            recv_sem=nrecv.at[k],
            device_id=peer,
            device_id_type=MESH,
        )
        copy.start()
        near_copies.append(copy)
    near[me] = total_terms[...]
    for u in late:
        move(u)
    for copy in near_copies:
        copy.wait_recv()
    total = near[0]
    for k in range(1, count):
        total = total + near[k]
    far[tile] = total
    far_copies = []
    for k, peer in enumerate(far_peers):
        copy = pltpu.make_async_remote_copy(
            src_ref=far.at[tile],
            dst_ref=far.at[tile],
            send_sem=fsend.at[k],
            recv_sem=frecv.at[k],
            device_id=peer,
            device_id_type=MESH,
        )
        copy.start()
        far_copies.append(copy)
    for copy in sends + rims + forwards + swaps + near_copies:
        copy.wait_send()
    for copy in far_copies:
        copy.wait()
    total = far[0]
    for k in range(1, tiles):
        total = total + far[k]
    recon[...] = total


def tables(block, block_subs, taps, depth, chunks, lanes):
    def block_diagonal(count, piece):
        return np.kron(np.eye(count), piece)

    index = np.arange(PIX)
    gap = index[:, None] - index[None, :]
    angle = np.where(gap == 0, 1, gap) * (math.pi / PAD)
    sign = np.where(gap % 2 == 0, 1.0, -1.0)
    table = np.where(gap == 0, 0.0, PIX * sign * np.cos(angle) / np.sin(angle))
    alternate = np.where(index % 2 == 0, 1.0, -1.0)
    def split(t):
        high = np.asarray(t.astype(jnp.bfloat16), np.float64)
        return high, t - high

    row_high, row_low = split(block_diagonal(block_subs, 2.0 * table))
    row_alt = np.pad(block_diagonal(block_subs, alternate[None, :]), ((0, -block_subs % 16), (0, 0)))
    none, thin = np.zeros_like(row_high), np.zeros_like(row_alt)
    row_all = np.block([
        [row_high, row_high, none, none],
        [row_low, none, none, none],
        [thin, thin, row_alt, row_alt],
        [row_alt, row_alt, thin, thin],
    ])
    ends = np.zeros((2, PIX, PIX))
    for n in range(2):
        ends[n, :, n] = 4.0 * alternate
    count = block // PIX
    col_high, col_low = split(block_diagonal(count, 2.0 * table.T))
    alt_a, alt_b = (block_diagonal(count, end) for end in ends)
    col_all = np.concatenate([col_high, col_high, col_low, alt_a, alt_a, alt_b, alt_b], axis=0)
    fold = np.zeros((taps, lanes // depth, depth))
    for k in range(taps):
        fold[k, :, k] = 1.0
    fold = fold.reshape(taps, lanes)
    gather = np.repeat(fold, PIX, axis=0)
    spread = np.zeros((chunks, chunks * taps, lanes))
    for w in range(chunks):
        spread[w, w * taps : (w + 1) * taps] = fold
    return tuple(jnp.asarray(t.astype(jnp.bfloat16)) for t in (row_all, col_all, gather, spread))


def stay(*arrays):
    return [pltpu.with_memory_space_constraint(x, pltpu.HBM) for x in arrays]


def frame(scalars, screens, amplitude, valid, matrix):
    tiles, blocks, cores = (lax.axis_size(n) for n in ("tile", "layer", "star"))
    lays, rows, cols = screens.shape
    stars, _, subs, sub_cols, commands = matrix.shape
    strips, per_block, unit, units, group = plan(rows, cols, blocks)
    chunks = units // group
    width = group * unit * LANES
    taps = sub_cols // chunks
    depth = -(-taps // 16) * 16
    parts, inner = row_parts(rows)
    part_subs = subs // parts
    slots = stars
    while slots * part_subs % 8:
        slots += 1
    lanes = 2 * slots * part_subs * depth
    pieces = 2 * (strips // cores) + (2 if inner < DIRECT else 0)
    rim_tiles = -(-(strips // cores) * lays // PACK)
    block = 2 * LANES if width % (2 * LANES) == 0 else LANES
    consts = tables(block, stars * part_subs, taps, depth, chunks, lanes)
    count = blocks * cores
    dma = pltpu.SemaphoreType.DMA
    bf16, f32 = jnp.bfloat16, jnp.float32
    piece = (stars, rows, unit * LANES)
    return pl.pallas_call(
        functools.partial(frame_kernel, tiles, cores, blocks, stars),
        out_shape=(
            pltpu.VMEM((lays, rows, cols), f32),
            pltpu.VMEM((stars, subs, 2, sub_cols), f32),
            pltpu.VMEM((1, commands), f32),
        ),
        in_specs=[HBM] * (len(scalars) + 4 + len(consts)),
        out_specs=(VMEM, VMEM, VMEM),
        scratch_shapes=[pltpu.SMEM(t.shape, t.dtype) for t in scalars]
        + [
            pltpu.VMEM((lays, strips + 2, rows + 2 * HALO, LANES), f32),
            pltpu.VMEM((2, strips, lays, DIRECT, LANES), f32),
            pltpu.VMEM((2, rim_tiles, 8, LANES), f32),
            pltpu.VMEM((2, cores, rim_tiles, 8, LANES), f32),
            pltpu.VMEM((units * (blocks - 1),) + piece, f32),
            pltpu.VMEM((blocks - 1, units) + piece, f32),
            pltpu.VMEM((units,) + piece, f32),
            pltpu.VMEM(amplitude.shape, f32),
            pltpu.VMEM(valid.shape, valid.dtype),
            pltpu.VMEM((chunks, parts, 2, slots, part_subs, depth, commands), bf16),
        ]
        + [pltpu.VMEM(t.shape, bf16) for t in consts]
        + [
            pltpu.VMEM((chunks, parts, 2 * slots * part_subs, lanes), f32),
            pltpu.VMEM(amplitude.shape, f32),
            pltpu.VMEM((4, stars * rows // parts, width), f32),
            pltpu.VMEM((4, 4 * stars * rows // parts, width), bf16),
            pltpu.VMEM((4, 2 * slots * part_subs, width), f32),
            pltpu.VMEM((1, commands), f32),
            pltpu.VMEM((count, 1, commands), f32),
            pltpu.VMEM((tiles, 1, commands), f32),
            dma((pieces,)),
            dma((pieces,)),
            dma((pieces, cores - 1)),
            dma((pieces, cores - 1)),
            dma((2,)),
            dma((2,)),
            dma((2, cores - 1)),
            dma((2, cores - 1)),
            dma((units * (blocks - 1),)),
            dma((units * (blocks - 1),)),
            dma((strips + 2,)),
            dma((6 + len(scalars) + chunks * parts * 2,)),
            dma((count - 1,)),
            dma((count - 1,)),
            dma((tiles - 1,)),
            dma((tiles - 1,)),
        ],
        compiler_params=pltpu.CompilerParams(
            collective_id=0, has_side_effects=True, vmem_limit_bytes=48 * 2**20
        ),
        name="frame",
    )(*stay(*scalars, screens, amplitude, valid, matrix, *consts))


def horner(z, first, *rest):
    value = first
    for c in rest:
        value = value * z + c
    return value


def sine_cosine(x):
    turns = jnp.floor(x * (1.0 / math.pi) + 0.5)
    r = x - turns * 3.140625
    r = r - turns * 9.67653589793e-4
    z = r * r
    s = r + r * (z * horner(z, 2.63541936e-6, -1.98230239e-4, 8.33324557e-3, -1.66666661e-1))
    c = 1.0 + z * horner(
        z, -2.63066288e-7, 2.47750852e-5, -1.38886609e-3, 4.166666e-2, -0.5
    )
    return s, c, turns


def halves(x):
    high = x.astype(jnp.bfloat16)
    return high, (x - high.astype(jnp.float32)).astype(jnp.bfloat16)


def product(x, y):
    return jnp.dot(x, y, preferred_element_type=jnp.float32)

def finish_kernel(moved, found, recon, previous, shifted, slopes, commands, sems):
    copies = [
        pltpu.make_async_copy(moved.at[j], shifted.at[j], sems.at[j]) for j in range(moved.shape[0])
    ]
    copies.append(pltpu.make_async_copy(found, slopes, sems.at[moved.shape[0]]))
    for copy in copies:
        copy.start()
    commands[...] = 2.0 * recon[0, :] - previous[...]
    for copy in copies:
        copy.wait()


def finish(moved, found, recon, previous):
    shifted, slopes, commands = pl.pallas_call(
        finish_kernel,
        out_shape=tuple(
            jax.ShapeDtypeStruct(x.shape, jnp.float32) for x in (moved, found, previous)
        ),
        in_specs=[ANY, ANY, VMEM, VMEM],
        out_specs=(ANY, ANY, VMEM),
        scratch_shapes=[pltpu.SemaphoreType.DMA((moved.shape[0] + 1,))],
        compiler_params=pltpu.CompilerParams(vmem_limit_bytes=2**20),
        name="finish",
    )(moved, found, recon, previous)
    return shifted, jnp.transpose(slopes, (0, 2, 1, 3)), commands


def body(
    screens,
    layer_weight,
    wind_row,
    wind_col,
    foot_row,
    foot_col,
    frac_row,
    frac_col,
    amplitude,
    valid,
    recon_matrix,
    prev_recon,
):
    scalars = (layer_weight, wind_row, wind_col, foot_row, foot_col, frac_row, frac_col)
    moved, found, recon = frame(scalars, screens, amplitude, valid, recon_matrix)
    return finish(moved, found, recon, prev_recon)


def solution(mesh):
    return jax.shard_map(
        body,
        mesh=mesh,
        in_specs=(
            P(("runs", "layer"), "tile", None),
            P(("runs", "layer")),
            P("runs"),
            P("runs"),
            P(),
            P(),
            P(),
            P(),
            P("tile", "layer"),
            P("tile", "layer"),
            P("star", None, "tile", "layer", None),
            P("runs"),
        ),
        out_specs=(
            P(("runs", "layer"), "tile", None),
            P(("runs", "star"), None, "tile", "layer"),
            P("runs"),
        ),
        check_vma=False,
    )
```

```python
import functools
import math

import jax
import jax.numpy as jnp
import numpy as np
from jax import lax
from jax.experimental import pallas as pl
from jax.experimental.pallas import tpu as pltpu
from jax.sharding import PartitionSpec as P

PIX = 16
PAD = 32
WIND = 4
FOOT = 80
LANES = 128
DEPTH = WIND + FOOT
HALO = -(-DEPTH // 8) * 8
DIRECT = DEPTH // 8 * 8
EXTRA = DEPTH - DIRECT
PACK = 8 // EXTRA
MESH = pl.DeviceIdType.MESH
ANY = pl.BlockSpec(memory_space=pl.ANY)
HBM = pl.BlockSpec(memory_space=pltpu.HBM)
SMEM = pl.BlockSpec(memory_space=pltpu.SMEM)
VMEM = pl.BlockSpec(memory_space=pltpu.VMEM)


def signal(sem, peer):
    pl.semaphore_signal(sem, inc=1, device_id=peer, device_id_type=MESH)


def greet(peers):
    barrier = pltpu.get_barrier_semaphore()
    for peer in peers:
        signal(barrier, peer)
    return lambda: pl.semaphore_wait(barrier, len(peers))


def plan(rows, cols, blocks):
    strips = cols // LANES
    per_block = strips // blocks
    unit = 2 if per_block % 2 == 0 else 1
    units = per_block // unit
    group = 1 if (unit * LANES // PIX) % 16 == 0 else units
    return strips, per_block, unit, units, group


def row_parts(rows, cols, blocks, cores):
    parts = 3 if (rows // PIX) % 3 == 0 else 1
    inner = min(DIRECT, -(-(DEPTH - rows // parts) // 8) * 8) if parts > 1 else DIRECT
    strips, _, unit, units, group = plan(rows, cols, blocks)
    ready = ((strips // cores - 2) * cores - 2) // unit
    split = 0 < inner < DIRECT and group == 1 and units * (blocks - 1) <= ready
    return parts, inner, split


def frame_kernel(
    tiles, cores, blocks, stars, weights_in, wind_row_in, wind_col_in, foot_row_in, foot_col_in,
    frac_row_in, frac_col_in, screens, amplitude, valid, matrix, row_table, col_table, gather, spread,
    shifted, slopes, recon,
    weights, wind_row, wind_col, foot_row, foot_col, frac_row, frac_col,
    field, land, rim, rim_land, outbox, inbox, share, amp, mask, weight, row_tab, col_tab, gath, spre,
    scale, amp_turned, real, stack, sums, total_terms, near, far,
    zsend, zrecv, csend, crecv, esend, erecv, fesend, ferecv, xsend, xrecv, local, load, nsend, nrecv, fsend, frecv,
):
    tile, core, layer = (lax.axis_index(n) for n in ("tile", "star", "layer"))
    up, down = lax.rem(tile + 1, tiles), lax.rem(tile + tiles - 1, tiles)
    partners = [lax.rem(core + k, cores) for k in range(1, cores)]
    peers = [lax.rem(layer + k, blocks) for k in range(1, blocks)]
    count = blocks * cores
    me = layer * cores + core
    near_peers = []
    for k in range(1, count):
        rank = lax.rem(me + k, count)
        near_peers.append({"layer": rank // cores, "star": lax.rem(rank, cores)})
    far_peers = [{"tile": lax.rem(tile + k, tiles)} for k in range(1, tiles)]
    lays, rows, cols = screens.shape
    strips, per_block, unit, units, group = plan(rows, cols, blocks)
    chunks = units // group
    width = group * unit * LANES
    subs = rows // PIX
    parts, inner, split = row_parts(rows, cols, blocks, cores)
    part_rows, part_subs = rows // parts, subs // parts
    first = (layer + 1) * per_block + strips - 1
    star_start, layer_start = core * stars, layer * lays
    groups = rows // 8
    many = groups // parts
    block_rows = stars * part_rows
    block_subs = stars * part_subs
    taps = matrix.shape[3] // chunks

    def column(n, size=1):
        start = pl.multiple_of(lax.rem(first + n, strips) * LANES, LANES)
        return pl.ds(start, size * LANES)

    greeted = greet(near_peers + far_peers)
    copies = []
    for n in range(strips + 2):
        copy = pltpu.make_async_copy(
            screens.at[:, :, column(n % strips)],
            field.at[:, n, pl.ds(HALO, rows), :],
            local.at[n],
        )
        copy.start()
        copies.append(copy)
    greeted()
    steps = strips // cores
    full = steps - 2 if split else steps
    pieces = [(m, d, 0, DIRECT) for m in range(full) for d in range(2)]
    for m in range(full, steps):
        pieces += [(m, 0, DIRECT - inner, inner), (m, 1, 0, inner)]
        pieces += [(m, 0, 0, DIRECT - inner), (m, 1, inner, DIRECT - inner)]
    targets = (up, down)
    sends = []

    def send(q):
        m, d, low, size = pieces[q]
        n = m * cores + core
        copy = pltpu.make_async_remote_copy(
            src_ref=screens.at[:, pl.ds((rows - DIRECT, 0)[d] + low, size), column(n)],
            dst_ref=land.at[d, n, :, pl.ds(low, size), :],
            send_sem=zsend.at[q],
            recv_sem=zrecv.at[q],
            device_id={"tile": targets[d]},
            device_id_type=MESH,
        )
        sends.append(copy)
        return copy

    for q in range(2):
        send(q).start()
    for copy in copies:
        copy.wait()
    for d, start in enumerate((rows - DEPTH, DIRECT)):
        for m in range(steps):
            for j in range(lays):
                e = m * lays + j
                to = slice(e % PACK * EXTRA, (e % PACK + 1) * EXTRA)
                rim[d, e // PACK, to, :] = field[
                    j, m * cores + core, HALO + start : HALO + start + EXTRA, :
                ]
    rims = []
    for d in range(2):
        copy = pltpu.make_async_remote_copy(
            src_ref=rim.at[d],
            dst_ref=rim_land.at[d, core],
            send_sem=esend.at[d],
            recv_sem=erecv.at[d],
            device_id={"tile": targets[d]},
            device_id_type=MESH,
        )
        copy.start()
        rims.append(copy)
    for q in range(2, len(pieces)):
        send(q).start()
    loads = []
    for n, (source, target) in enumerate(
        ((amplitude, amp), (valid, mask), (row_table, row_tab), (col_table, col_tab),
         (gather, gath), (spread, spre), (weights_in, weights), (wind_row_in, wind_row),
         (wind_col_in, wind_col), (foot_row_in, foot_row), (foot_col_in, foot_col),
         (frac_row_in, frac_row), (frac_col_in, frac_col))
    ):
        copy = pltpu.make_async_copy(source, target, load.at[n])
        copy.start()
        loads.append(copy)
    matrix_copies = []

    def fetch_matrix():
        for w in range(chunks):
            for p in range(parts):
                for d in range(2):
                    copy = pltpu.make_async_copy(
                        matrix.at[
                            :, d, p * part_subs : (p + 1) * part_subs, w * taps : (w + 1) * taps, :
                        ],
                        weight.at[w, p, d, 0:stars, :, 0:taps, :],
                        load.at[len(loads) + len(matrix_copies)],
                    )
                    copy.start()
                    matrix_copies.append(copy)

    slots, depth = weight.shape[3], weight.shape[5]
    for w in range(chunks):
        for p in range(parts):
            for d in range(2):
                if slots > stars:
                    weight[w, p, d, stars:] = jnp.zeros(
                        (slots - stars,) + weight.shape[4:], weight.dtype
                    )
                if depth > taps:
                    weight[w, p, d, 0:stars, :, taps:, :] = jnp.zeros(
                        (stars, part_subs, depth - taps, weight.shape[6]), weight.dtype
                    )
    scale[...] = jnp.zeros_like(scale)

    def per_sub(values):
        return jnp.sum(values.reshape(-1, PIX, values.shape[1]), axis=1)

    def collect(values):
        high, low = halves(values)
        return product(high, gath[...]) + product(low, gath[...])

    for copy in loads:
        copy.wait()
    amp_turned[...] = -amp[...]
    for w in range(chunks):
        power = amp[:, w * width : (w + 1) * width]
        total = per_sub(power * power)
        lit = product(mask[...].astype(jnp.float32).astype(jnp.bfloat16), spre[w])
        ratio = lit / (collect(total) * PAD)
        for p in range(parts):
            for d in range(2):
                for g in range(stars):
                    at = d * slots * part_subs + g * part_subs
                    scale[w, p, at : at + part_subs, :] = ratio[
                        p * part_subs : (p + 1) * part_subs
                    ]
    lane = lax.broadcasted_iota(jnp.int32, (8, LANES), 1)

    def window(j, row, base, n):
        return [field[j, base + n + k, pl.ds(row, 8), :] for k in range(unit + 1)]

    def place(start):
        base = start // LANES
        turn = start - base * LANES
        return base, turn

    def move(u):
        low = u * unit

        def move_step(i, carry):
            for j in range(lays):
                base, turn = place(LANES - wind_col[layer_start + j])
                values = window(j, HALO + i * 8 - wind_row[layer_start + j], base, low)
                rolled = [pltpu.roll(v, (LANES - turn) & (LANES - 1), 1) for v in values]
                keep = lane < LANES - turn
                for k in range(unit):
                    shifted[j, pl.ds(pl.multiple_of(i * 8, 8), 8), column(low + k + 1)] = jnp.where(
                        keep, rolled[k], rolled[k + 1]
                    )
            return carry

        lax.fori_loop(0, groups, move_step, 0, unroll=math.gcd(groups, 3))

    def compute(u, put, chosen, unroll=1):
        low = u * unit

        def pupil_step(g, carry):
            star = star_start + g
            for part in chosen:
                plain = [[None] * unit for _ in range(many)]
                ahead = [[None] * (unit + 1) for _ in range(many)]
                for j in range(lays):
                    lay = layer_start + j
                    top_row = HALO + part * part_rows + foot_row[star, lay] - wind_row[lay]
                    base, turn = place(LANES + foot_col[star, lay] - wind_col[lay])
                    gain = weights[j]
                    a, b = frac_row[star, lay], frac_col[star, lay]
                    top, bottom = gain * (1.0 - a), gain * a
                    keep = lane < LANES - turn
                    back = (LANES - turn) & (LANES - 1)
                    for r in range(many):
                        row = top_row + r * 8
                        rolled = [
                            pltpu.roll(top * x + bottom * y, back, 1)
                            for x, y in zip(
                                window(j, row, base, low), window(j, row + 1, base, low)
                            )
                        ]
                        shift = [
                            jnp.where(keep, rolled[k], rolled[k + 1]) for k in range(unit)
                        ] + [rolled[unit]]
                        for k in range(unit):
                            term = (1.0 - b) * shift[k]
                            plain[r][k] = term if j == 0 else plain[r][k] + term
                        for k in range(unit + 1):
                            term = b * shift[k]
                            ahead[r][k] = term if j == 0 else ahead[r][k] + term
                for r in range(many):
                    beside = [pltpu.roll(v, LANES - 1, 1) for v in ahead[r]]
                    for k in range(unit):
                        value = plain[r][k] + jnp.where(
                            lane < LANES - 1, beside[k], beside[k + 1]
                        )
                        at = pl.ds(part * part_rows + r * 8, 8)
                        put(g, at, k, value)
            return carry

        lax.fori_loop(0, stars, pupil_step, 0, unroll=unroll)

    def to_outbox(u):
        def put(g, at, k, value):
            outbox[u, g, at, k * LANES : (k + 1) * LANES] = value

        return put

    def to_share(w):
        def put(g, at, k, value):
            share[w, g, at, k * LANES : (k + 1) * LANES] = value

        return put

    block = col_tab.shape[1]

    high_half = slots * part_subs

    def fields(slot, w, p):
        left = w * width
        for n in range(block_subs):
            g, i = divmod(n, part_subs)
            at = slice((p * part_subs + i) * PIX, (p * part_subs + i + 1) * PIX)
            strip = []
            for v in range(w * group, (w + 1) * group):
                phase = share[v, g, at, :]
                for k in range(blocks - 1):
                    phase = phase + inbox[k, v, g, at, :]
                strip.append(phase)
            sine, cosine, turns = sine_cosine(jnp.concatenate(strip, axis=1))
            power = jnp.where(
                (turns.astype(jnp.int32) & 1) == 1,
                amp_turned[at, left : left + width],
                amp[at, left : left + width],
            )
            a, b = power * cosine, power * sine
            real[slot, n * PIX : (n + 1) * PIX, :] = a
            for q, value in enumerate(halves(b) + halves(a)):
                low = q * block_rows + n * PIX
                stack[slot, low : low + PIX, :] = value

    def centroids(slot, w, p):
        a = real[slot]
        found = product(row_tab[...], stack[slot])
        turned = found[0:block_rows] + found[block_rows : 2 * block_rows]
        alt_a = found[2 * block_rows : 2 * block_rows + block_subs]
        step = (found.shape[0] - 2 * block_rows) // 2
        alt_b = found[2 * block_rows + step : 2 * block_rows + step + block_subs]
        sums[slot, 0:block_subs, :] = per_sub(a * turned) - PIX * (alt_a * alt_a + alt_b * alt_b)
        if high_half > block_subs:
            fill = jnp.zeros((high_half - block_subs, width), jnp.float32)
            sums[slot, block_subs:high_half, :] = fill
            sums[slot, high_half + block_subs :, :] = fill
        b_high, b_low, a_high, a_low = (
            stack[slot, q * block_rows : (q + 1) * block_rows, :] for q in range(4)
        )
        across = []
        for k in range(width // block):
            cut = slice(k * block, (k + 1) * block)
            turned = product(
                jnp.concatenate([b_high[:, cut], b_low[:, cut], b_high[:, cut]], axis=1),
                col_tab[0 : 3 * block, :],
            )
            alt = product(
                jnp.concatenate([x[:, cut] for x in (a_high, a_low, b_high, b_low)], axis=1),
                col_tab[3 * block :, :],
            )
            across.append(a[:, cut] * turned - alt * alt)
        sums[slot, high_half : high_half + block_subs, :] = per_sub(
            jnp.concatenate(across, axis=1)
        )
        found = collect(sums[slot]) * scale[w, p]
        for d in range(2):
            for g in range(stars):
                at = d * high_half + g * part_subs
                for i in range(part_subs):
                    slopes[g, p * part_subs + i, d : d + 1, w * taps : (w + 1) * taps] = found[
                        at + i : at + i + 1, w * depth : w * depth + taps
                    ]
        mine = (
            lax.broadcasted_iota(jnp.int32, found.shape, 1) // depth
            == lax.broadcasted_iota(jnp.int32, found.shape, 0)
        )
        return jnp.where(mine, found, 0.0).astype(jnp.bfloat16)

    def slope_parts(chosen):
        terms = []
        slots_here = real.shape[0]
        for n, (w, p) in enumerate(chosen):
            if n == 0:
                fields(0, w, p)
            if n + 1 < len(chosen):
                fields((n + 1) % slots_here, *chosen[n + 1])
            terms.append((w, p, centroids(n % slots_here, w, p)))
        return terms

    started = []

    def project(terms):
        for w, p, _ in terms:
            for d in range(2):
                matrix_copies[(w * parts + p) * 2 + d].wait()
        partial = None
        for w, p, left_side in terms:
            right_side = weight[w, p].reshape(left_side.shape[1], weight.shape[6])
            value = jnp.dot(left_side, right_side, preferred_element_type=jnp.float32)
            partial = value if partial is None else partial + value
        partial = jnp.sum(partial, axis=0, keepdims=True)
        if started:
            total_terms[...] = total_terms[...] + partial
        else:
            total_terms[...] = partial
            started.append(True)

    forwards, swaps = [], []

    passing = {}

    def send_on(chosen):
        for q in chosen:
            m, d, low, size = pieces[q]
            mine = land.at[d, m * cores + core, :, pl.ds(low, size), :]
            sends[q].wait_recv()
            passing[q] = []
            for k, p in enumerate(partners):
                forward = pltpu.make_async_remote_copy(
                    src_ref=mine,
                    dst_ref=mine,
                    send_sem=csend.at[q, k],
                    recv_sem=crecv.at[q, k],
                    device_id={"star": p},
                    device_id_type=MESH,
                )
                forward.start()
                passing[q].append(forward)

    def take(chosen):
        for q in chosen:
            for forward in passing[q]:
                forward.wait_recv()
                forwards.append(forward)
            m, d, low, size = pieces[q]
            base = low + (HALO - DIRECT, HALO + rows)[d]
            for n in range(m * cores, (m + 1) * cores):
                for to in (n, n + strips):
                    if to < strips + 2:
                        for j in range(lays):
                            field[j, to, base : base + size, :] = land[d, n, j, low : low + size, :]

    def take_rims():
        for d in range(2):
            rims[d].wait_recv()
            for k, p in enumerate(partners):
                forward = pltpu.make_async_remote_copy(
                    src_ref=rim_land.at[d, core],
                    dst_ref=rim_land.at[d, core],
                    send_sem=fesend.at[d, k],
                    recv_sem=ferecv.at[d, k],
                    device_id={"star": p},
                    device_id_type=MESH,
                )
                forward.start()
                forwards.append(forward)
        for forward in forwards[-2 * len(partners) :]:
            forward.wait_recv()
        for d, base in enumerate((HALO - DEPTH, HALO + rows + DIRECT)):
            for m in range(steps):
                for j in range(lays):
                    e = m * lays + j
                    at = slice(e % PACK * EXTRA, (e % PACK + 1) * EXTRA)
                    for c in range(cores):
                        n = m * cores + c
                        for to in (n, n + strips):
                            if to < strips + 2:
                                field[j, to, base : base + EXTRA, :] = rim_land[d, c, e // PACK, at, :]

    def own(u, chosen, unroll=1):
        k, w = divmod(u, units)
        compute(u, to_share(w), chosen, unroll)

    def arrived(w):
        for q, copy in enumerate(swaps):
            if q % units == w:
                copy.wait_recv()

    whole = list(range(parts))
    done = 0
    def pair(n):
        return [2 * n, 2 * n + 1]

    def finish_unit(u):
        k, w = divmod(u, units)
        if k < blocks - 1:
            compute(u, to_outbox(u), whole)
            copy = pltpu.make_async_remote_copy(
                src_ref=outbox.at[u],
                dst_ref=inbox.at[k, w],
                send_sem=xsend.at[u],
                recv_sem=xrecv.at[u],
                device_id={"layer": peers[k]},
                device_id_type=MESH,
            )
            copy.start()
            swaps.append(copy)
        else:
            own(u, whole)
            arrived(w)
            if (w + 1) % group == 0:
                slope_all([w // group], whole)

    def slope_all(chosen, some):
        project(slope_parts([(c, p) for c in chosen for p in some]))

    late = []
    for m in range(full):
        send_on(pair(m))
        take(pair(m))
        if m == 0:
            take_rims()
            fetch_matrix()
        have = (m + 1) * cores
        while done < units * blocks and (
            have == strips or done * unit + unit + 2 <= have
        ):
            finish_unit(done)
            if have < strips:
                move(done)
            else:
                late.append(done)
            done += 1
    if split:
        middle, rest = whole[1:-1], [whole[0], whole[-1]]
        have = (steps - 1) * cores
        soon = [u for u in range(done, units * blocks) if u * unit + unit + 2 <= have]
        late = [u for u in range(done, units * blocks) if u not in soon]
        soon_chunks, late_chunks = ([u % units for u in some] for some in (soon, late))
        near_soon, far_soon, near_late, far_late = (pair(full + n) for n in range(4))
        send_on(near_soon)
        take(near_soon)
        for u in soon:
            own(u, middle, True)
            arrived(u % units)
        slope_all(soon_chunks, middle)
        send_on(far_soon)
        take(far_soon)
        for u in soon:
            own(u, rest, True)
        slope_all(soon_chunks, rest)
        send_on(near_late)
        for u in soon:
            move(u)
        take(near_late)
        for u in late:
            own(u, middle, True)
            arrived(u % units)
        send_on(far_late)
        slope_all(late_chunks, middle)
        take(far_late)
        for u in late:
            own(u, rest, True)
        slope_all(late_chunks, rest)
    near_copies = []
    for k, peer in enumerate(near_peers):
        copy = pltpu.make_async_remote_copy(
            src_ref=total_terms,
            dst_ref=near.at[me],
            send_sem=nsend.at[k],
            recv_sem=nrecv.at[k],
            device_id=peer,
            device_id_type=MESH,
        )
        copy.start()
        near_copies.append(copy)
    near[me] = total_terms[...]
    for u in late:
        move(u)
    for copy in near_copies:
        copy.wait_recv()
    total = near[0]
    for k in range(1, count):
        total = total + near[k]
    far[tile] = total
    far_copies = []
    toward = jnp.where(2 * tile < tiles, 1, tiles - 1)
    for k in range(tiles - 1, 0, -1):
        copy = pltpu.make_async_remote_copy(
            src_ref=far.at[tile],
            dst_ref=far.at[tile],
            send_sem=fsend.at[k - 1],
            recv_sem=frecv.at[tile],
            device_id={"tile": lax.rem(tile + toward * k, tiles)},
            device_id_type=MESH,
        )
        copy.start()
        far_copies.append(copy)
    for copy in sends + rims + forwards + swaps + near_copies:
        copy.wait_send()
    for copy in far_copies:
        copy.wait_send()
    for k in range(1, tiles):
        source = lax.rem(tile + k, tiles)
        pltpu.make_async_remote_copy(
            src_ref=far.at[source],
            dst_ref=far.at[source],
            send_sem=fsend.at[k - 1],
            recv_sem=frecv.at[source],
            device_id={"tile": source},
            device_id_type=MESH,
        ).wait_recv()
    total = far[0]
    for k in range(1, tiles):
        total = total + far[k]
    recon[...] = total


def tables(block, block_subs, taps, depth, chunks, lanes):
    def block_diagonal(count, piece):
        return np.kron(np.eye(count), piece)

    index = np.arange(PIX)
    gap = index[:, None] - index[None, :]
    angle = np.where(gap == 0, 1, gap) * (math.pi / PAD)
    sign = np.where(gap % 2 == 0, 1.0, -1.0)
    table = np.where(gap == 0, 0.0, PIX * sign * np.cos(angle) / np.sin(angle))
    alternate = np.where(index % 2 == 0, 1.0, -1.0)
    def split(t):
        high = np.asarray(t.astype(jnp.bfloat16), np.float64)
        return high, t - high

    row_high, row_low = split(block_diagonal(block_subs, 2.0 * table))
    row_alt = np.pad(block_diagonal(block_subs, alternate[None, :]), ((0, -block_subs % 16), (0, 0)))
    none, thin = np.zeros_like(row_high), np.zeros_like(row_alt)
    row_all = np.block([
        [row_high, row_high, none, none],
        [row_low, none, none, none],
        [thin, thin, row_alt, row_alt],
        [row_alt, row_alt, thin, thin],
    ])
    ends = np.zeros((2, PIX, PIX))
    for n in range(2):
        ends[n, :, n] = 4.0 * alternate
    count = block // PIX
    col_high, col_low = split(block_diagonal(count, 2.0 * table.T))
    alt_a, alt_b = (block_diagonal(count, end) for end in ends)
    col_all = np.concatenate([col_high, col_high, col_low, alt_a, alt_a, alt_b, alt_b], axis=0)
    fold = np.zeros((taps, lanes // depth, depth))
    for k in range(taps):
        fold[k, :, k] = 1.0
    fold = fold.reshape(taps, lanes)
    gather = np.repeat(fold, PIX, axis=0)
    spread = np.zeros((chunks, chunks * taps, lanes))
    for w in range(chunks):
        spread[w, w * taps : (w + 1) * taps] = fold
    return tuple(jnp.asarray(t.astype(jnp.bfloat16)) for t in (row_all, col_all, gather, spread))


def stay(*arrays):
    return [pltpu.with_memory_space_constraint(x, pltpu.HBM) for x in arrays]


def frame(scalars, screens, amplitude, valid, matrix):
    tiles, blocks, cores = (lax.axis_size(n) for n in ("tile", "layer", "star"))
    lays, rows, cols = screens.shape
    stars, _, subs, sub_cols, commands = matrix.shape
    strips, per_block, unit, units, group = plan(rows, cols, blocks)
    chunks = units // group
    width = group * unit * LANES
    taps = sub_cols // chunks
    depth = -(-taps // 16) * 16
    parts, inner, split = row_parts(rows, cols, blocks, cores)
    part_subs = subs // parts
    slots = stars
    while slots * part_subs % 8:
        slots += 1
    lanes = 2 * slots * part_subs * depth
    pieces = 2 * (strips // cores) + (4 if split else 0)
    rim_tiles = -(-(strips // cores) * lays // PACK)
    block = 2 * LANES if width % (2 * LANES) == 0 else LANES
    consts = tables(block, stars * part_subs, taps, depth, chunks, lanes)
    count = blocks * cores
    dma = pltpu.SemaphoreType.DMA
    bf16, f32 = jnp.bfloat16, jnp.float32
    piece = (stars, rows, unit * LANES)
    return pl.pallas_call(
        functools.partial(frame_kernel, tiles, cores, blocks, stars),
        out_shape=(
            pltpu.VMEM((lays, rows, cols), f32),
            pltpu.VMEM((stars, subs, 2, sub_cols), f32),
            pltpu.VMEM((1, commands), f32),
        ),
        in_specs=[HBM] * (len(scalars) + 4 + len(consts)),
        out_specs=(VMEM, VMEM, VMEM),
        scratch_shapes=[pltpu.SMEM(t.shape, t.dtype) for t in scalars]
        + [
            pltpu.VMEM((lays, strips + 2, rows + 2 * HALO, LANES), f32),
            pltpu.VMEM((2, strips, lays, DIRECT, LANES), f32),
            pltpu.VMEM((2, rim_tiles, 8, LANES), f32),
            pltpu.VMEM((2, cores, rim_tiles, 8, LANES), f32),
            pltpu.VMEM((units * (blocks - 1),) + piece, f32),
            pltpu.VMEM((blocks - 1, units) + piece, f32),
            pltpu.VMEM((units,) + piece, f32),
            pltpu.VMEM(amplitude.shape, f32),
            pltpu.VMEM(valid.shape, valid.dtype),
            pltpu.VMEM((chunks, parts, 2, slots, part_subs, depth, commands), bf16),
        ]
        + [pltpu.VMEM(t.shape, bf16) for t in consts]
        + [
            pltpu.VMEM((chunks, parts, 2 * slots * part_subs, lanes), f32),
            pltpu.VMEM(amplitude.shape, f32),
            pltpu.VMEM((4, stars * rows // parts, width), f32),
            pltpu.VMEM((4, 4 * stars * rows // parts, width), bf16),
            pltpu.VMEM((4, 2 * slots * part_subs, width), f32),
            pltpu.VMEM((1, commands), f32),
            pltpu.VMEM((count, 1, commands), f32),
            pltpu.VMEM((tiles, 1, commands), f32),
            dma((pieces,)),
            dma((pieces,)),
            dma((pieces, cores - 1)),
            dma((pieces, cores - 1)),
            dma((2,)),
            dma((2,)),
            dma((2, cores - 1)),
            dma((2, cores - 1)),
            dma((units * (blocks - 1),)),
            dma((units * (blocks - 1),)),
            dma((strips + 2,)),
            dma((6 + len(scalars) + chunks * parts * 2,)),
            dma((count - 1,)),
            dma((count - 1,)),
            dma((tiles - 1,)),
            dma((tiles,)),
        ],
        compiler_params=pltpu.CompilerParams(
            collective_id=0, has_side_effects=True, vmem_limit_bytes=48 * 2**20
        ),
        name="frame",
    )(*stay(*scalars, screens, amplitude, valid, matrix, *consts))


def horner(z, first, *rest):
    value = first
    for c in rest:
        value = value * z + c
    return value


def sine_cosine(x):
    turns = jnp.floor(x * (1.0 / math.pi) + 0.5)
    r = x - turns * 3.140625
    r = r - turns * 9.67653589793e-4
    z = r * r
    s = r + r * (z * horner(z, 2.63541936e-6, -1.98230239e-4, 8.33324557e-3, -1.66666661e-1))
    c = 1.0 + z * horner(
        z, -2.63066288e-7, 2.47750852e-5, -1.38886609e-3, 4.166666e-2, -0.5
    )
    return s, c, turns


def halves(x):
    high = x.astype(jnp.bfloat16)
    return high, (x - high.astype(jnp.float32)).astype(jnp.bfloat16)


def product(x, y):
    return jnp.dot(x, y, preferred_element_type=jnp.float32)

def finish_kernel(moved, found, recon, previous, shifted, slopes, commands, sems):
    copies = [
        pltpu.make_async_copy(moved.at[j], shifted.at[j], sems.at[j]) for j in range(moved.shape[0])
    ]
    copies.append(pltpu.make_async_copy(found, slopes, sems.at[moved.shape[0]]))
    for copy in copies:
        copy.start()
    commands[...] = 2.0 * recon[0, :] - previous[...]
    for copy in copies:
        copy.wait()


def finish(moved, found, recon, previous):
    shifted, slopes, commands = pl.pallas_call(
        finish_kernel,
        out_shape=tuple(
            jax.ShapeDtypeStruct(x.shape, jnp.float32) for x in (moved, found, previous)
        ),
        in_specs=[ANY, ANY, VMEM, VMEM],
        out_specs=(ANY, ANY, VMEM),
        scratch_shapes=[pltpu.SemaphoreType.DMA((moved.shape[0] + 1,))],
        compiler_params=pltpu.CompilerParams(vmem_limit_bytes=2**20),
        name="finish",
    )(moved, found, recon, previous)
    return shifted, jnp.transpose(slopes, (0, 2, 1, 3)), commands


def body(
    screens,
    layer_weight,
    wind_row,
    wind_col,
    foot_row,
    foot_col,
    frac_row,
    frac_col,
    amplitude,
    valid,
    recon_matrix,
    prev_recon,
):
    scalars = (layer_weight, wind_row, wind_col, foot_row, foot_col, frac_row, frac_col)
    moved, found, recon = frame(scalars, screens, amplitude, valid, recon_matrix)
    return finish(moved, found, recon, prev_recon)


def solution(mesh):
    return jax.shard_map(
        body,
        mesh=mesh,
        in_specs=(
            P(("runs", "layer"), "tile", None),
            P(("runs", "layer")),
            P("runs"),
            P("runs"),
            P(),
            P(),
            P(),
            P(),
            P("tile", "layer"),
            P("tile", "layer"),
            P("star", None, "tile", "layer", None),
            P("runs"),
        ),
        out_specs=(
            P(("runs", "layer"), "tile", None),
            P(("runs", "star"), None, "tile", "layer"),
            P("runs"),
        ),
        check_vma=False,
    )
```

```python
import functools
import math

import jax
import jax.numpy as jnp
import numpy as np
from jax import lax
from jax.experimental import pallas as pl
from jax.experimental.pallas import tpu as pltpu
from jax.sharding import PartitionSpec as P

PIX = 16
PAD = 32
WIND = 4
FOOT = 80
LANES = 128
DEPTH = WIND + FOOT
HALO = -(-DEPTH // 8) * 8
DIRECT = DEPTH // 8 * 8
EXTRA = DEPTH - DIRECT
PACK = 8 // EXTRA
MESH = pl.DeviceIdType.MESH
ANY = pl.BlockSpec(memory_space=pl.ANY)
HBM = pl.BlockSpec(memory_space=pltpu.HBM)
SMEM = pl.BlockSpec(memory_space=pltpu.SMEM)
VMEM = pl.BlockSpec(memory_space=pltpu.VMEM)


def signal(sem, peer):
    pl.semaphore_signal(sem, inc=1, device_id=peer, device_id_type=MESH)


def greet(peers):
    barrier = pltpu.get_barrier_semaphore()
    for peer in peers:
        signal(barrier, peer)
    return lambda: pl.semaphore_wait(barrier, len(peers))


def plan(rows, cols, blocks):
    strips = cols // LANES
    per_block = strips // blocks
    unit = 2 if per_block % 2 == 0 else 1
    units = per_block // unit
    group = 1 if (unit * LANES // PIX) % 16 == 0 else units
    return strips, per_block, unit, units, group


def row_parts(rows, cols, blocks, cores):
    parts = 3 if (rows // PIX) % 3 == 0 else 1
    inner = min(DIRECT, -(-(DEPTH - rows // parts) // 8) * 8) if parts > 1 else DIRECT
    strips, _, unit, units, group = plan(rows, cols, blocks)
    ready = ((strips // cores - 2) * cores - 2) // unit
    split = 0 < inner < DIRECT and group == 1 and units * (blocks - 1) <= ready
    return parts, inner, split


def frame_kernel(
    tiles, cores, blocks, stars, weights_in, wind_row_in, wind_col_in, foot_row_in, foot_col_in,
    frac_row_in, frac_col_in, screens, amplitude, valid, previous, matrix, row_table, col_table, gather, spread,
    shifted, slopes, commands,
    weights, wind_row, wind_col, foot_row, foot_col, frac_row, frac_col,
    field, land, rim, rim_land, outbox, inbox, share, amp, mask, before, weight, row_tab, col_tab, gath, spre,
    scale, amp_turned, real, stack, sums, total_terms, near, far,
    zsend, zrecv, csend, crecv, esend, erecv, fesend, ferecv, xsend, xrecv, local, load, nsend, nrecv, fsend, frecv,
):
    tile, core, layer = (lax.axis_index(n) for n in ("tile", "star", "layer"))
    up, down = lax.rem(tile + 1, tiles), lax.rem(tile + tiles - 1, tiles)
    partners = [lax.rem(core + k, cores) for k in range(1, cores)]
    peers = [lax.rem(layer + k, blocks) for k in range(1, blocks)]
    count = blocks * cores
    me = layer * cores + core
    near_peers = []
    for k in range(1, count):
        rank = lax.rem(me + k, count)
        near_peers.append({"layer": rank // cores, "star": lax.rem(rank, cores)})
    far_peers = [{"tile": lax.rem(tile + k, tiles)} for k in range(1, tiles)]
    lays, rows, cols = screens.shape
    strips, per_block, unit, units, group = plan(rows, cols, blocks)
    chunks = units // group
    width = group * unit * LANES
    subs = rows // PIX
    parts, inner, split = row_parts(rows, cols, blocks, cores)
    part_rows, part_subs = rows // parts, subs // parts
    first = (layer + 1) * per_block + strips - 1
    star_start, layer_start = core * stars, layer * lays
    groups = rows // 8
    many = groups // parts
    block_rows = stars * part_rows
    block_subs = stars * part_subs
    taps = matrix.shape[3] // chunks

    def column(n, size=1):
        start = pl.multiple_of(lax.rem(first + n, strips) * LANES, LANES)
        return pl.ds(start, size * LANES)

    greeted = greet(near_peers + far_peers)
    copies = []
    for n in range(strips + 2):
        copy = pltpu.make_async_copy(
            screens.at[:, :, column(n % strips)],
            field.at[:, n, pl.ds(HALO, rows), :],
            local.at[n],
        )
        copy.start()
        copies.append(copy)
    greeted()
    steps = strips // cores
    full = steps - 2 if split else steps
    pieces = [(m, d, 0, DIRECT) for m in range(full) for d in range(2)]
    for m in range(full, steps):
        pieces += [(m, 0, DIRECT - inner, inner), (m, 1, 0, inner)]
        pieces += [(m, 0, 0, DIRECT - inner), (m, 1, inner, DIRECT - inner)]
    targets = (up, down)
    sends = []

    def send(q):
        m, d, low, size = pieces[q]
        n = m * cores + core
        copy = pltpu.make_async_remote_copy(
            src_ref=screens.at[:, pl.ds((rows - DIRECT, 0)[d] + low, size), column(n)],
            dst_ref=land.at[d, n, :, pl.ds(low, size), :],
            send_sem=zsend.at[q],
            recv_sem=zrecv.at[q],
            device_id={"tile": targets[d]},
            device_id_type=MESH,
        )
        sends.append(copy)
        return copy

    for q in range(2):
        send(q).start()
    for copy in copies:
        copy.wait()
    for d, start in enumerate((rows - DEPTH, DIRECT)):
        for m in range(steps):
            for j in range(lays):
                e = m * lays + j
                to = slice(e % PACK * EXTRA, (e % PACK + 1) * EXTRA)
                rim[d, e // PACK, to, :] = field[
                    j, m * cores + core, HALO + start : HALO + start + EXTRA, :
                ]
    rims = []
    for d in range(2):
        copy = pltpu.make_async_remote_copy(
            src_ref=rim.at[d],
            dst_ref=rim_land.at[d, core],
            send_sem=esend.at[d],
            recv_sem=erecv.at[d],
            device_id={"tile": targets[d]},
            device_id_type=MESH,
        )
        copy.start()
        rims.append(copy)
    for q in range(2, len(pieces)):
        send(q).start()
    loads = []
    for n, (source, target) in enumerate(
        ((amplitude, amp), (valid, mask), (row_table, row_tab), (col_table, col_tab),
         (gather, gath), (spread, spre), (previous, before), (weights_in, weights), (wind_row_in, wind_row),
         (wind_col_in, wind_col), (foot_row_in, foot_row), (foot_col_in, foot_col),
         (frac_row_in, frac_row), (frac_col_in, frac_col))
    ):
        copy = pltpu.make_async_copy(source, target, load.at[n])
        copy.start()
        loads.append(copy)
    matrix_copies = []

    def fetch_matrix():
        for w in range(chunks):
            for p in range(parts):
                for d in range(2):
                    copy = pltpu.make_async_copy(
                        matrix.at[
                            :, d, p * part_subs : (p + 1) * part_subs, w * taps : (w + 1) * taps, :
                        ],
                        weight.at[w, p, d, 0:stars, :, 0:taps, :],
                        load.at[len(loads) + len(matrix_copies)],
                    )
                    copy.start()
                    matrix_copies.append(copy)

    slots, depth = weight.shape[3], weight.shape[5]
    for w in range(chunks):
        for p in range(parts):
            for d in range(2):
                if slots > stars:
                    weight[w, p, d, stars:] = jnp.zeros(
                        (slots - stars,) + weight.shape[4:], weight.dtype
                    )
                if depth > taps:
                    weight[w, p, d, 0:stars, :, taps:, :] = jnp.zeros(
                        (stars, part_subs, depth - taps, weight.shape[6]), weight.dtype
                    )
    scale[...] = jnp.zeros_like(scale)

    def per_sub(values):
        return jnp.sum(values.reshape(-1, PIX, values.shape[1]), axis=1)

    def collect(values):
        high, low = halves(values)
        return product(high, gath[...]) + product(low, gath[...])

    for copy in loads:
        copy.wait()
    amp_turned[...] = -amp[...]
    for w in range(chunks):
        power = amp[:, w * width : (w + 1) * width]
        total = per_sub(power * power)
        lit = product(mask[...].astype(jnp.float32).astype(jnp.bfloat16), spre[w])
        ratio = lit / (collect(total) * PAD)
        for p in range(parts):
            for d in range(2):
                for g in range(stars):
                    at = d * slots * part_subs + g * part_subs
                    scale[w, p, at : at + part_subs, :] = ratio[
                        p * part_subs : (p + 1) * part_subs
                    ]
    lane = lax.broadcasted_iota(jnp.int32, (8, LANES), 1)

    def window(j, row, base, n):
        return [field[j, base + n + k, pl.ds(row, 8), :] for k in range(unit + 1)]

    def place(start):
        base = start // LANES
        turn = start - base * LANES
        return base, turn

    def move(u):
        low = u * unit

        def move_step(i, carry):
            for j in range(lays):
                base, turn = place(LANES - wind_col[layer_start + j])
                values = window(j, HALO + i * 8 - wind_row[layer_start + j], base, low)
                rolled = [pltpu.roll(v, (LANES - turn) & (LANES - 1), 1) for v in values]
                keep = lane < LANES - turn
                for k in range(unit):
                    shifted[j, pl.ds(pl.multiple_of(i * 8, 8), 8), column(low + k + 1)] = jnp.where(
                        keep, rolled[k], rolled[k + 1]
                    )
            return carry

        lax.fori_loop(0, groups, move_step, 0, unroll=math.gcd(groups, 3))

    def compute(u, put, chosen, unroll=1):
        low = u * unit

        def pupil_step(g, carry):
            star = star_start + g
            for part in chosen:
                plain = [[None] * unit for _ in range(many)]
                ahead = [[None] * (unit + 1) for _ in range(many)]
                for j in range(lays):
                    lay = layer_start + j
                    top_row = HALO + part * part_rows + foot_row[star, lay] - wind_row[lay]
                    base, turn = place(LANES + foot_col[star, lay] - wind_col[lay])
                    gain = weights[j]
                    a, b = frac_row[star, lay], frac_col[star, lay]
                    top, bottom = gain * (1.0 - a), gain * a
                    keep = lane < LANES - turn
                    back = (LANES - turn) & (LANES - 1)
                    for r in range(many):
                        row = top_row + r * 8
                        rolled = [
                            pltpu.roll(top * x + bottom * y, back, 1)
                            for x, y in zip(
                                window(j, row, base, low), window(j, row + 1, base, low)
                            )
                        ]
                        shift = [
                            jnp.where(keep, rolled[k], rolled[k + 1]) for k in range(unit)
                        ] + [rolled[unit]]
                        for k in range(unit):
                            term = (1.0 - b) * shift[k]
                            plain[r][k] = term if j == 0 else plain[r][k] + term
                        for k in range(unit + 1):
                            term = b * shift[k]
                            ahead[r][k] = term if j == 0 else ahead[r][k] + term
                for r in range(many):
                    beside = [pltpu.roll(v, LANES - 1, 1) for v in ahead[r]]
                    for k in range(unit):
                        value = plain[r][k] + jnp.where(
                            lane < LANES - 1, beside[k], beside[k + 1]
                        )
                        at = pl.ds(part * part_rows + r * 8, 8)
                        put(g, at, k, value)
            return carry

        lax.fori_loop(0, stars, pupil_step, 0, unroll=unroll)

    def to_outbox(u):
        def put(g, at, k, value):
            outbox[u, g, at, k * LANES : (k + 1) * LANES] = value

        return put

    def to_share(w):
        def put(g, at, k, value):
            share[w, g, at, k * LANES : (k + 1) * LANES] = value

        return put

    block = col_tab.shape[1]

    high_half = slots * part_subs

    def fields(slot, w, p):
        left = w * width
        for n in range(block_subs):
            g, i = divmod(n, part_subs)
            at = slice((p * part_subs + i) * PIX, (p * part_subs + i + 1) * PIX)
            strip = []
            for v in range(w * group, (w + 1) * group):
                phase = share[v, g, at, :]
                for k in range(blocks - 1):
                    phase = phase + inbox[k, v, g, at, :]
                strip.append(phase)
            sine, cosine, turns = sine_cosine(jnp.concatenate(strip, axis=1))
            power = jnp.where(
                (turns.astype(jnp.int32) & 1) == 1,
                amp_turned[at, left : left + width],
                amp[at, left : left + width],
            )
            a, b = power * cosine, power * sine
            real[slot, n * PIX : (n + 1) * PIX, :] = a
            for q, value in enumerate(halves(b) + halves(a)):
                low = q * block_rows + n * PIX
                stack[slot, low : low + PIX, :] = value

    def centroids(slot, w, p):
        a = real[slot]
        found = product(row_tab[...], stack[slot])
        turned = found[0:block_rows] + found[block_rows : 2 * block_rows]
        alt_a = found[2 * block_rows : 2 * block_rows + block_subs]
        step = (found.shape[0] - 2 * block_rows) // 2
        alt_b = found[2 * block_rows + step : 2 * block_rows + step + block_subs]
        sums[slot, 0:block_subs, :] = per_sub(a * turned) - PIX * (alt_a * alt_a + alt_b * alt_b)
        if high_half > block_subs:
            fill = jnp.zeros((high_half - block_subs, width), jnp.float32)
            sums[slot, block_subs:high_half, :] = fill
            sums[slot, high_half + block_subs :, :] = fill
        b_high, b_low, a_high, a_low = (
            stack[slot, q * block_rows : (q + 1) * block_rows, :] for q in range(4)
        )
        across = []
        for k in range(width // block):
            cut = slice(k * block, (k + 1) * block)
            turned = product(
                jnp.concatenate([b_high[:, cut], b_low[:, cut], b_high[:, cut]], axis=1),
                col_tab[0 : 3 * block, :],
            )
            alt = product(
                jnp.concatenate([x[:, cut] for x in (a_high, a_low, b_high, b_low)], axis=1),
                col_tab[3 * block :, :],
            )
            across.append(a[:, cut] * turned - alt * alt)
        sums[slot, high_half : high_half + block_subs, :] = per_sub(
            jnp.concatenate(across, axis=1)
        )
        found = collect(sums[slot]) * scale[w, p]
        for d in range(2):
            for g in range(stars):
                at = d * high_half + g * part_subs
                for i in range(part_subs):
                    slopes[g, p * part_subs + i, d : d + 1, w * taps : (w + 1) * taps] = found[
                        at + i : at + i + 1, w * depth : w * depth + taps
                    ]
        mine = (
            lax.broadcasted_iota(jnp.int32, found.shape, 1) // depth
            == lax.broadcasted_iota(jnp.int32, found.shape, 0)
        )
        return jnp.where(mine, found, 0.0).astype(jnp.bfloat16)

    def slope_parts(chosen):
        terms = []
        slots_here = real.shape[0]
        for n, (w, p) in enumerate(chosen):
            if n == 0:
                fields(0, w, p)
            if n + 1 < len(chosen):
                fields((n + 1) % slots_here, *chosen[n + 1])
            terms.append((w, p, centroids(n % slots_here, w, p)))
        return terms

    started = []

    def project(terms):
        for w, p, _ in terms:
            for d in range(2):
                matrix_copies[(w * parts + p) * 2 + d].wait()
        partial = None
        for w, p, left_side in terms:
            right_side = weight[w, p].reshape(left_side.shape[1], weight.shape[6])
            value = jnp.dot(left_side, right_side, preferred_element_type=jnp.float32)
            partial = value if partial is None else partial + value
        partial = jnp.sum(partial, axis=0, keepdims=True)
        if started:
            total_terms[...] = total_terms[...] + partial
        else:
            total_terms[...] = partial
            started.append(True)

    forwards, swaps = [], []

    passing = {}

    def send_on(chosen):
        for q in chosen:
            m, d, low, size = pieces[q]
            mine = land.at[d, m * cores + core, :, pl.ds(low, size), :]
            sends[q].wait_recv()
            passing[q] = []
            for k, p in enumerate(partners):
                forward = pltpu.make_async_remote_copy(
                    src_ref=mine,
                    dst_ref=mine,
                    send_sem=csend.at[q, k],
                    recv_sem=crecv.at[q, k],
                    device_id={"star": p},
                    device_id_type=MESH,
                )
                forward.start()
                passing[q].append(forward)

    def take(chosen):
        for q in chosen:
            for forward in passing[q]:
                forward.wait_recv()
                forwards.append(forward)
            m, d, low, size = pieces[q]
            base = low + (HALO - DIRECT, HALO + rows)[d]
            for n in range(m * cores, (m + 1) * cores):
                for to in (n, n + strips):
                    if to < strips + 2:
                        for j in range(lays):
                            field[j, to, base : base + size, :] = land[d, n, j, low : low + size, :]

    def take_rims():
        for d in range(2):
            rims[d].wait_recv()
            for k, p in enumerate(partners):
                forward = pltpu.make_async_remote_copy(
                    src_ref=rim_land.at[d, core],
                    dst_ref=rim_land.at[d, core],
                    send_sem=fesend.at[d, k],
                    recv_sem=ferecv.at[d, k],
                    device_id={"star": p},
                    device_id_type=MESH,
                )
                forward.start()
                forwards.append(forward)
        for forward in forwards[-2 * len(partners) :]:
            forward.wait_recv()
        for d, base in enumerate((HALO - DEPTH, HALO + rows + DIRECT)):
            for m in range(steps):
                for j in range(lays):
                    e = m * lays + j
                    at = slice(e % PACK * EXTRA, (e % PACK + 1) * EXTRA)
                    for c in range(cores):
                        n = m * cores + c
                        for to in (n, n + strips):
                            if to < strips + 2:
                                field[j, to, base : base + EXTRA, :] = rim_land[d, c, e // PACK, at, :]

    def own(u, chosen, unroll=1):
        k, w = divmod(u, units)
        compute(u, to_share(w), chosen, unroll)

    def arrived(w):
        for q, copy in enumerate(swaps):
            if q % units == w:
                copy.wait_recv()

    whole = list(range(parts))
    done = 0
    def pair(n):
        return [2 * n, 2 * n + 1]

    def finish_unit(u):
        k, w = divmod(u, units)
        if k < blocks - 1:
            compute(u, to_outbox(u), whole)
            copy = pltpu.make_async_remote_copy(
                src_ref=outbox.at[u],
                dst_ref=inbox.at[k, w],
                send_sem=xsend.at[u],
                recv_sem=xrecv.at[u],
                device_id={"layer": peers[k]},
                device_id_type=MESH,
            )
            copy.start()
            swaps.append(copy)
        else:
            own(u, whole)
            arrived(w)
            if (w + 1) % group == 0:
                slope_all([w // group], whole)

    def slope_all(chosen, some):
        project(slope_parts([(c, p) for c in chosen for p in some]))

    late = []
    for m in range(full):
        send_on(pair(m))
        take(pair(m))
        if m == 0:
            take_rims()
            fetch_matrix()
        have = (m + 1) * cores
        while done < units * blocks and (
            have == strips or done * unit + unit + 2 <= have
        ):
            finish_unit(done)
            if have < strips:
                move(done)
            else:
                late.append(done)
            done += 1
    if split:
        middle, rest = whole[1:-1], [whole[0], whole[-1]]
        have = (steps - 1) * cores
        soon = [u for u in range(done, units * blocks) if u * unit + unit + 2 <= have]
        late = [u for u in range(done, units * blocks) if u not in soon]
        soon_chunks, late_chunks = ([u % units for u in some] for some in (soon, late))
        near_soon, far_soon, near_late, far_late = (pair(full + n) for n in range(4))
        send_on(near_soon)
        take(near_soon)
        for u in soon:
            own(u, middle, True)
            arrived(u % units)
        slope_all(soon_chunks, middle)
        send_on(far_soon)
        take(far_soon)
        for u in soon:
            own(u, rest, True)
        slope_all(soon_chunks, rest)
        send_on(near_late)
        for u in soon:
            move(u)
        take(near_late)
        for u in late:
            own(u, middle, True)
            arrived(u % units)
        send_on(far_late)
        slope_all(late_chunks, middle)
        take(far_late)
        for u in late:
            own(u, rest, True)
        slope_all(late_chunks, rest)
    near_copies = []
    for k, peer in enumerate(near_peers):
        copy = pltpu.make_async_remote_copy(
            src_ref=total_terms,
            dst_ref=near.at[me],
            send_sem=nsend.at[k],
            recv_sem=nrecv.at[k],
            device_id=peer,
            device_id_type=MESH,
        )
        copy.start()
        near_copies.append(copy)
    near[me] = total_terms[...]
    for u in late:
        move(u)
    for copy in near_copies:
        copy.wait_recv()
    total = near[0]
    for k in range(1, count):
        total = total + near[k]
    far[tile] = total
    far_copies = []
    toward = jnp.where(2 * tile < tiles, 1, tiles - 1)
    for k in range(tiles - 1, 0, -1):
        copy = pltpu.make_async_remote_copy(
            src_ref=far.at[tile],
            dst_ref=far.at[tile],
            send_sem=fsend.at[k - 1],
            recv_sem=frecv.at[tile],
            device_id={"tile": lax.rem(tile + toward * k, tiles)},
            device_id_type=MESH,
        )
        copy.start()
        far_copies.append(copy)
    for copy in sends + rims + forwards + swaps + near_copies:
        copy.wait_send()
    for copy in far_copies:
        copy.wait_send()
    for k in range(1, tiles):
        source = lax.rem(tile + k, tiles)
        pltpu.make_async_remote_copy(
            src_ref=far.at[source],
            dst_ref=far.at[source],
            send_sem=fsend.at[k - 1],
            recv_sem=frecv.at[source],
            device_id={"tile": source},
            device_id_type=MESH,
        ).wait_recv()
    total = far[0]
    for k in range(1, tiles):
        total = total + far[k]
    commands[...] = 2.0 * total[0, :] - before[...]


def tables(block, block_subs, taps, depth, chunks, lanes):
    def block_diagonal(count, piece):
        return np.kron(np.eye(count), piece)

    index = np.arange(PIX)
    gap = index[:, None] - index[None, :]
    angle = np.where(gap == 0, 1, gap) * (math.pi / PAD)
    sign = np.where(gap % 2 == 0, 1.0, -1.0)
    table = np.where(gap == 0, 0.0, PIX * sign * np.cos(angle) / np.sin(angle))
    alternate = np.where(index % 2 == 0, 1.0, -1.0)
    def split(t):
        high = np.asarray(t.astype(jnp.bfloat16), np.float64)
        return high, t - high

    row_high, row_low = split(block_diagonal(block_subs, 2.0 * table))
    row_alt = np.pad(block_diagonal(block_subs, alternate[None, :]), ((0, -block_subs % 16), (0, 0)))
    none, thin = np.zeros_like(row_high), np.zeros_like(row_alt)
    row_all = np.block([
        [row_high, row_high, none, none],
        [row_low, none, none, none],
        [thin, thin, row_alt, row_alt],
        [row_alt, row_alt, thin, thin],
    ])
    ends = np.zeros((2, PIX, PIX))
    for n in range(2):
        ends[n, :, n] = 4.0 * alternate
    count = block // PIX
    col_high, col_low = split(block_diagonal(count, 2.0 * table.T))
    alt_a, alt_b = (block_diagonal(count, end) for end in ends)
    col_all = np.concatenate([col_high, col_high, col_low, alt_a, alt_a, alt_b, alt_b], axis=0)
    fold = np.zeros((taps, lanes // depth, depth))
    for k in range(taps):
        fold[k, :, k] = 1.0
    fold = fold.reshape(taps, lanes)
    gather = np.repeat(fold, PIX, axis=0)
    spread = np.zeros((chunks, chunks * taps, lanes))
    for w in range(chunks):
        spread[w, w * taps : (w + 1) * taps] = fold
    return tuple(jnp.asarray(t.astype(jnp.bfloat16)) for t in (row_all, col_all, gather, spread))


def stay(*arrays):
    return [pltpu.with_memory_space_constraint(x, pltpu.HBM) for x in arrays]


def frame(scalars, screens, amplitude, valid, previous, matrix):
    tiles, blocks, cores = (lax.axis_size(n) for n in ("tile", "layer", "star"))
    lays, rows, cols = screens.shape
    stars, _, subs, sub_cols, commands = matrix.shape
    strips, per_block, unit, units, group = plan(rows, cols, blocks)
    chunks = units // group
    width = group * unit * LANES
    taps = sub_cols // chunks
    depth = -(-taps // 16) * 16
    parts, inner, split = row_parts(rows, cols, blocks, cores)
    part_subs = subs // parts
    slots = stars
    while slots * part_subs % 8:
        slots += 1
    lanes = 2 * slots * part_subs * depth
    pieces = 2 * (strips // cores) + (4 if split else 0)
    rim_tiles = -(-(strips // cores) * lays // PACK)
    block = 2 * LANES if width % (2 * LANES) == 0 else LANES
    consts = tables(block, stars * part_subs, taps, depth, chunks, lanes)
    count = blocks * cores
    dma = pltpu.SemaphoreType.DMA
    bf16, f32 = jnp.bfloat16, jnp.float32
    piece = (stars, rows, unit * LANES)
    return pl.pallas_call(
        functools.partial(frame_kernel, tiles, cores, blocks, stars),
        out_shape=(
            pltpu.VMEM((lays, rows, cols), f32),
            pltpu.VMEM((stars, subs, 2, sub_cols), f32),
            pltpu.VMEM((commands,), f32),
        ),
        in_specs=[HBM] * (len(scalars) + 5 + len(consts)),
        out_specs=(VMEM, VMEM, VMEM),
        scratch_shapes=[pltpu.SMEM(t.shape, t.dtype) for t in scalars]
        + [
            pltpu.VMEM((lays, strips + 2, rows + 2 * HALO, LANES), f32),
            pltpu.VMEM((2, strips, lays, DIRECT, LANES), f32),
            pltpu.VMEM((2, rim_tiles, 8, LANES), f32),
            pltpu.VMEM((2, cores, rim_tiles, 8, LANES), f32),
            pltpu.VMEM((units * (blocks - 1),) + piece, f32),
            pltpu.VMEM((blocks - 1, units) + piece, f32),
            pltpu.VMEM((units,) + piece, f32),
            pltpu.VMEM(amplitude.shape, f32),
            pltpu.VMEM(valid.shape, valid.dtype),
            pltpu.VMEM(previous.shape, f32),
            pltpu.VMEM((chunks, parts, 2, slots, part_subs, depth, commands), bf16),
        ]
        + [pltpu.VMEM(t.shape, bf16) for t in consts]
        + [
            pltpu.VMEM((chunks, parts, 2 * slots * part_subs, lanes), f32),
            pltpu.VMEM(amplitude.shape, f32),
            pltpu.VMEM((4, stars * rows // parts, width), f32),
            pltpu.VMEM((4, 4 * stars * rows // parts, width), bf16),
            pltpu.VMEM((4, 2 * slots * part_subs, width), f32),
            pltpu.VMEM((1, commands), f32),
            pltpu.VMEM((count, 1, commands), f32),
            pltpu.VMEM((tiles, 1, commands), f32),
            dma((pieces,)),
            dma((pieces,)),
            dma((pieces, cores - 1)),
            dma((pieces, cores - 1)),
            dma((2,)),
            dma((2,)),
            dma((2, cores - 1)),
            dma((2, cores - 1)),
            dma((units * (blocks - 1),)),
            dma((units * (blocks - 1),)),
            dma((strips + 2,)),
            dma((7 + len(scalars) + chunks * parts * 2,)),
            dma((count - 1,)),
            dma((count - 1,)),
            dma((tiles - 1,)),
            dma((tiles,)),
        ],
        compiler_params=pltpu.CompilerParams(
            collective_id=0, has_side_effects=True, vmem_limit_bytes=48 * 2**20
        ),
        name="frame",
    )(*stay(*scalars, screens, amplitude, valid, previous, matrix, *consts))


def horner(z, first, *rest):
    value = first
    for c in rest:
        value = value * z + c
    return value


def sine_cosine(x):
    turns = jnp.floor(x * (1.0 / math.pi) + 0.5)
    r = x - turns * 3.140625
    r = r - turns * 9.67653589793e-4
    z = r * r
    s = r + r * (z * horner(z, 2.63541936e-6, -1.98230239e-4, 8.33324557e-3, -1.66666661e-1))
    c = 1.0 + z * horner(
        z, -2.63066288e-7, 2.47750852e-5, -1.38886609e-3, 4.166666e-2, -0.5
    )
    return s, c, turns


def halves(x):
    high = x.astype(jnp.bfloat16)
    return high, (x - high.astype(jnp.float32)).astype(jnp.bfloat16)


def product(x, y):
    return jnp.dot(x, y, preferred_element_type=jnp.float32)

def finish_kernel(*refs):
    sems, count = refs[-1], len(refs) // 2
    copies = []
    for n in range(count):
        copies.append(pltpu.make_async_copy(refs[n], refs[count + n], sems.at[n]))
        copies[-1].start()
    for copy in copies:
        copy.wait()


def finish(*arrays):
    return pl.pallas_call(
        finish_kernel,
        out_shape=[jax.ShapeDtypeStruct(x.shape, x.dtype) for x in arrays],
        in_specs=[ANY] * len(arrays),
        out_specs=[ANY] * len(arrays),
        scratch_shapes=[pltpu.SemaphoreType.DMA((len(arrays),))],
        compiler_params=pltpu.CompilerParams(vmem_limit_bytes=2**20),
        name="finish",
    )(*arrays)


def body(
    screens,
    layer_weight,
    wind_row,
    wind_col,
    foot_row,
    foot_col,
    frac_row,
    frac_col,
    amplitude,
    valid,
    recon_matrix,
    prev_recon,
):
    scalars = (layer_weight, wind_row, wind_col, foot_row, foot_col, frac_row, frac_col)
    shifted, slopes, commands = finish(
        *frame(scalars, screens, amplitude, valid, prev_recon, recon_matrix)
    )
    return shifted, jnp.transpose(slopes, (0, 2, 1, 3)), commands


def solution(mesh):
    return jax.shard_map(
        body,
        mesh=mesh,
        in_specs=(
            P(("runs", "layer"), "tile", None),
            P(("runs", "layer")),
            P("runs"),
            P("runs"),
            P(),
            P(),
            P(),
            P(),
            P("tile", "layer"),
            P("tile", "layer"),
            P("star", None, "tile", "layer", None),
            P("runs"),
        ),
        out_specs=(
            P(("runs", "layer"), "tile", None),
            P(("runs", "star"), None, "tile", "layer"),
            P("runs"),
        ),
        check_vma=False,
    )
```

```python
import functools
import math

import jax
import jax.numpy as jnp
import numpy as np
from jax import lax
from jax.experimental import pallas as pl
from jax.experimental.pallas import tpu as pltpu
from jax.sharding import PartitionSpec as P

PIX = 16
PAD = 32
WIND = 4
FOOT = 80
LANES = 128
DEPTH = WIND + FOOT
HALO = -(-DEPTH // 8) * 8
DIRECT = DEPTH // 8 * 8
EXTRA = DEPTH - DIRECT
PACK = 8 // EXTRA
MESH = pl.DeviceIdType.MESH
ANY = pl.BlockSpec(memory_space=pl.ANY)
HBM = pl.BlockSpec(memory_space=pltpu.HBM)
SMEM = pl.BlockSpec(memory_space=pltpu.SMEM)
VMEM = pl.BlockSpec(memory_space=pltpu.VMEM)


def signal(sem, peer):
    pl.semaphore_signal(sem, inc=1, device_id=peer, device_id_type=MESH)


def greet(peers):
    barrier = pltpu.get_barrier_semaphore()
    for peer in peers:
        signal(barrier, peer)
    return lambda: pl.semaphore_wait(barrier, len(peers))


def plan(rows, cols, blocks):
    strips = cols // LANES
    per_block = strips // blocks
    unit = 2 if per_block % 2 == 0 else 1
    units = per_block // unit
    group = 1 if (unit * LANES // PIX) % 16 == 0 else units
    return strips, per_block, unit, units, group


def row_parts(rows, cols, blocks, cores):
    parts = 3 if (rows // PIX) % 3 == 0 else 1
    inner = min(DIRECT, -(-(DEPTH - rows // parts) // 8) * 8) if parts > 1 else DIRECT
    strips, _, unit, units, group = plan(rows, cols, blocks)
    ready = ((strips // cores - 2) * cores - 2) // unit
    split = 0 < inner < DIRECT and group == 1 and units * (blocks - 1) <= ready
    return parts, inner, split


def frame_kernel(
    tiles, cores, blocks, stars, weights_in, wind_row_in, wind_col_in, foot_row_in, foot_col_in,
    frac_row_in, frac_col_in, screens, amplitude, valid, previous, matrix, row_table, col_table, gather, spread,
    shifted, slopes, commands,
    weights, wind_row, wind_col, foot_row, foot_col, frac_row, frac_col,
    field, land, rim, rim_land, outbox, inbox, share, amp, mask, before, weight, row_tab, col_tab, gath, spre,
    scale, amp_turned, real, stack, sums, total_terms, near, far,
    zsend, zrecv, csend, crecv, esend, erecv, fesend, ferecv, xsend, xrecv, local, load, nsend, nrecv, fsend, frecv,
):
    tile, core, layer = (lax.axis_index(n) for n in ("tile", "star", "layer"))
    up, down = lax.rem(tile + 1, tiles), lax.rem(tile + tiles - 1, tiles)
    partners = [lax.rem(core + k, cores) for k in range(1, cores)]
    peers = [lax.rem(layer + k, blocks) for k in range(1, blocks)]
    count = blocks * cores
    me = layer * cores + core
    near_peers = []
    for k in range(1, count):
        rank = lax.rem(me + k, count)
        near_peers.append({"layer": rank // cores, "star": lax.rem(rank, cores)})
    far_peers = [{"tile": lax.rem(tile + k, tiles)} for k in range(1, tiles)]
    lays, rows, cols = screens.shape
    strips, per_block, unit, units, group = plan(rows, cols, blocks)
    chunks = units // group
    width = group * unit * LANES
    subs = rows // PIX
    parts, inner, split = row_parts(rows, cols, blocks, cores)
    part_rows, part_subs = rows // parts, subs // parts
    first = (layer + 1) * per_block + strips - 1
    star_start, layer_start = core * stars, layer * lays
    groups = rows // 8
    many = groups // parts
    block_rows = stars * part_rows
    block_subs = stars * part_subs
    taps = matrix.shape[3] // chunks

    def column(n, size=1):
        start = pl.multiple_of(lax.rem(first + n, strips) * LANES, LANES)
        return pl.ds(start, size * LANES)

    greeted = greet(near_peers + far_peers)
    copies = []
    for n in range(strips + 2):
        copy = pltpu.make_async_copy(
            screens.at[:, :, column(n % strips)],
            field.at[:, n, pl.ds(HALO, rows), :],
            local.at[n],
        )
        copy.start()
        copies.append(copy)
    greeted()
    steps = strips // cores
    full = steps - 2 if split else steps
    pieces = [(m, d, 0, DIRECT) for m in range(full) for d in range(2)]
    for m in range(full, steps):
        pieces += [(m, 0, DIRECT - inner, inner), (m, 1, 0, inner)]
        pieces += [(m, 0, 0, DIRECT - inner), (m, 1, inner, DIRECT - inner)]
    targets = (up, down)
    sends = []

    def send(q):
        m, d, low, size = pieces[q]
        n = m * cores + core
        copy = pltpu.make_async_remote_copy(
            src_ref=screens.at[:, pl.ds((rows - DIRECT, 0)[d] + low, size), column(n)],
            dst_ref=land.at[d, n, :, pl.ds(low, size), :],
            send_sem=zsend.at[q],
            recv_sem=zrecv.at[q],
            device_id={"tile": targets[d]},
            device_id_type=MESH,
        )
        sends.append(copy)
        return copy

    for q in range(2):
        send(q).start()
    for copy in copies:
        copy.wait()
    for d, start in enumerate((rows - DEPTH, DIRECT)):
        for m in range(steps):
            for j in range(lays):
                e = m * lays + j
                to = slice(e % PACK * EXTRA, (e % PACK + 1) * EXTRA)
                rim[d, e // PACK, to, :] = field[
                    j, m * cores + core, HALO + start : HALO + start + EXTRA, :
                ]
    rims = []
    for d in range(2):
        copy = pltpu.make_async_remote_copy(
            src_ref=rim.at[d],
            dst_ref=rim_land.at[d, core],
            send_sem=esend.at[d],
            recv_sem=erecv.at[d],
            device_id={"tile": targets[d]},
            device_id_type=MESH,
        )
        copy.start()
        rims.append(copy)
    for q in range(2, len(pieces)):
        send(q).start()
    loads = []
    for n, (source, target) in enumerate(
        ((amplitude, amp), (valid, mask), (row_table, row_tab), (col_table, col_tab),
         (gather, gath), (spread, spre), (previous, before), (weights_in, weights), (wind_row_in, wind_row),
         (wind_col_in, wind_col), (foot_row_in, foot_row), (foot_col_in, foot_col),
         (frac_row_in, frac_row), (frac_col_in, frac_col))
    ):
        copy = pltpu.make_async_copy(source, target, load.at[n])
        copy.start()
        loads.append(copy)
    matrix_copies = []

    def fetch_matrix():
        for w in range(chunks):
            for p in range(parts):
                for d in range(2):
                    copy = pltpu.make_async_copy(
                        matrix.at[
                            :, d, p * part_subs : (p + 1) * part_subs, w * taps : (w + 1) * taps, :
                        ],
                        weight.at[w, p, d, 0:stars, :, 0:taps, :],
                        load.at[len(loads) + len(matrix_copies)],
                    )
                    copy.start()
                    matrix_copies.append(copy)

    slots, depth = weight.shape[3], weight.shape[5]
    for w in range(chunks):
        for p in range(parts):
            for d in range(2):
                if slots > stars:
                    weight[w, p, d, stars:] = jnp.zeros(
                        (slots - stars,) + weight.shape[4:], weight.dtype
                    )
                if depth > taps:
                    weight[w, p, d, 0:stars, :, taps:, :] = jnp.zeros(
                        (stars, part_subs, depth - taps, weight.shape[6]), weight.dtype
                    )
    scale[...] = jnp.zeros_like(scale)

    def per_sub(values):
        return jnp.sum(values.reshape(-1, PIX, values.shape[1]), axis=1)

    def collect(values):
        high, low = halves(values)
        return product(high, gath[...]) + product(low, gath[...])

    for copy in loads:
        copy.wait()
    amp_turned[...] = -amp[...]
    for w in range(chunks):
        power = amp[:, w * width : (w + 1) * width]
        total = per_sub(power * power)
        lit = product(mask[...].astype(jnp.float32).astype(jnp.bfloat16), spre[w])
        ratio = lit / (collect(total) * PAD)
        for p in range(parts):
            for d in range(2):
                for g in range(stars):
                    at = d * slots * part_subs + g * part_subs
                    scale[w, p, at : at + part_subs, :] = ratio[
                        p * part_subs : (p + 1) * part_subs
                    ]
    lane = lax.broadcasted_iota(jnp.int32, (8, LANES), 1)

    def window(j, row, base, n):
        return [field[j, base + n + k, pl.ds(row, 8), :] for k in range(unit + 1)]

    def place(start):
        base = start // LANES
        turn = start - base * LANES
        return base, turn

    def move(u):
        low = u * unit

        def move_step(i, carry):
            for j in range(lays):
                base, turn = place(LANES - wind_col[layer_start + j])
                values = window(j, HALO + i * 8 - wind_row[layer_start + j], base, low)
                rolled = [pltpu.roll(v, (LANES - turn) & (LANES - 1), 1) for v in values]
                keep = lane < LANES - turn
                for k in range(unit):
                    shifted[j, pl.ds(pl.multiple_of(i * 8, 8), 8), column(low + k + 1)] = jnp.where(
                        keep, rolled[k], rolled[k + 1]
                    )
            return carry

        lax.fori_loop(0, groups, move_step, 0, unroll=math.gcd(groups, 3))

    def compute(u, put, chosen, unroll=1):
        low = u * unit

        def pupil_step(g, carry):
            star = star_start + g
            for part in chosen:
                plain = [[None] * unit for _ in range(many)]
                ahead = [[None] * (unit + 1) for _ in range(many)]
                for j in range(lays):
                    lay = layer_start + j
                    top_row = HALO + part * part_rows + foot_row[star, lay] - wind_row[lay]
                    base, turn = place(LANES + foot_col[star, lay] - wind_col[lay])
                    gain = weights[j]
                    a, b = frac_row[star, lay], frac_col[star, lay]
                    top, bottom = gain * (1.0 - a), gain * a
                    keep = lane < LANES - turn
                    back = (LANES - turn) & (LANES - 1)
                    for r in range(many):
                        row = top_row + r * 8
                        rolled = [
                            pltpu.roll(top * x + bottom * y, back, 1)
                            for x, y in zip(
                                window(j, row, base, low), window(j, row + 1, base, low)
                            )
                        ]
                        shift = [
                            jnp.where(keep, rolled[k], rolled[k + 1]) for k in range(unit)
                        ] + [rolled[unit]]
                        for k in range(unit):
                            term = (1.0 - b) * shift[k]
                            plain[r][k] = term if j == 0 else plain[r][k] + term
                        for k in range(unit + 1):
                            term = b * shift[k]
                            ahead[r][k] = term if j == 0 else ahead[r][k] + term
                for r in range(many):
                    beside = [pltpu.roll(v, LANES - 1, 1) for v in ahead[r]]
                    for k in range(unit):
                        value = plain[r][k] + jnp.where(
                            lane < LANES - 1, beside[k], beside[k + 1]
                        )
                        at = pl.ds(part * part_rows + r * 8, 8)
                        put(g, at, k, value)
            return carry

        lax.fori_loop(0, stars, pupil_step, 0, unroll=unroll)

    def to_outbox(u):
        def put(g, at, k, value):
            outbox[u, g, at, k * LANES : (k + 1) * LANES] = value

        return put

    def to_share(w):
        def put(g, at, k, value):
            share[w, g, at, k * LANES : (k + 1) * LANES] = value

        return put

    block = col_tab.shape[1]

    high_half = slots * part_subs

    def fields(slot, w, p):
        left = w * width
        for n in range(block_subs):
            g, i = divmod(n, part_subs)
            at = slice((p * part_subs + i) * PIX, (p * part_subs + i + 1) * PIX)
            strip = []
            for v in range(w * group, (w + 1) * group):
                phase = share[v, g, at, :]
                for k in range(blocks - 1):
                    phase = phase + inbox[k, v, g, at, :]
                strip.append(phase)
            sine, cosine, turns = sine_cosine(jnp.concatenate(strip, axis=1))
            power = jnp.where(
                (turns.astype(jnp.int32) & 1) == 1,
                amp_turned[at, left : left + width],
                amp[at, left : left + width],
            )
            a, b = power * cosine, power * sine
            real[slot, n * PIX : (n + 1) * PIX, :] = a
            for q, value in enumerate(halves(b) + halves(a)):
                low = q * block_rows + n * PIX
                stack[slot, low : low + PIX, :] = value

    def centroids(slot, w, p):
        a = real[slot]
        found = product(row_tab[...], stack[slot])
        turned = found[0:block_rows] + found[block_rows : 2 * block_rows]
        alt_a = found[2 * block_rows : 2 * block_rows + block_subs]
        step = (found.shape[0] - 2 * block_rows) // 2
        alt_b = found[2 * block_rows + step : 2 * block_rows + step + block_subs]
        sums[slot, 0:block_subs, :] = per_sub(a * turned) - PIX * (alt_a * alt_a + alt_b * alt_b)
        if high_half > block_subs:
            fill = jnp.zeros((high_half - block_subs, width), jnp.float32)
            sums[slot, block_subs:high_half, :] = fill
            sums[slot, high_half + block_subs :, :] = fill
        b_high, b_low, a_high, a_low = (
            stack[slot, q * block_rows : (q + 1) * block_rows, :] for q in range(4)
        )
        across = []
        for k in range(width // block):
            cut = slice(k * block, (k + 1) * block)
            turned = product(
                jnp.concatenate([b_high[:, cut], b_low[:, cut], b_high[:, cut]], axis=1),
                col_tab[0 : 3 * block, :],
            )
            alt = product(
                jnp.concatenate([x[:, cut] for x in (a_high, a_low, b_high, b_low)], axis=1),
                col_tab[3 * block :, :],
            )
            across.append(a[:, cut] * turned - alt * alt)
        sums[slot, high_half : high_half + block_subs, :] = per_sub(
            jnp.concatenate(across, axis=1)
        )
        found = collect(sums[slot]) * scale[w, p]
        for d in range(2):
            for g in range(stars):
                at = d * high_half + g * part_subs
                for i in range(part_subs):
                    slopes[g, p * part_subs + i, d : d + 1, w * taps : (w + 1) * taps] = found[
                        at + i : at + i + 1, w * depth : w * depth + taps
                    ]
        mine = (
            lax.broadcasted_iota(jnp.int32, found.shape, 1) // depth
            == lax.broadcasted_iota(jnp.int32, found.shape, 0)
        )
        return jnp.where(mine, found, 0.0).astype(jnp.bfloat16)

    def slope_parts(chosen):
        terms = []
        slots_here = real.shape[0]
        for n, (w, p) in enumerate(chosen):
            if n == 0:
                fields(0, w, p)
            if n + 1 < len(chosen):
                fields((n + 1) % slots_here, *chosen[n + 1])
            terms.append((w, p, centroids(n % slots_here, w, p)))
        return terms

    started = []

    def project(terms):
        for w, p, _ in terms:
            for d in range(2):
                matrix_copies[(w * parts + p) * 2 + d].wait()
        partial = None
        for w, p, left_side in terms:
            right_side = weight[w, p].reshape(left_side.shape[1], weight.shape[6])
            value = jnp.dot(left_side, right_side, preferred_element_type=jnp.float32)
            partial = value if partial is None else partial + value
        partial = jnp.sum(partial, axis=0, keepdims=True)
        if started:
            total_terms[...] = total_terms[...] + partial
        else:
            total_terms[...] = partial
            started.append(True)

    forwards, swaps = [], []

    passing = {}

    def send_on(chosen):
        for q in chosen:
            m, d, low, size = pieces[q]
            mine = land.at[d, m * cores + core, :, pl.ds(low, size), :]
            sends[q].wait_recv()
            passing[q] = []
            for k, p in enumerate(partners):
                forward = pltpu.make_async_remote_copy(
                    src_ref=mine,
                    dst_ref=mine,
                    send_sem=csend.at[q, k],
                    recv_sem=crecv.at[q, k],
                    device_id={"star": p},
                    device_id_type=MESH,
                )
                forward.start()
                passing[q].append(forward)

    def take(chosen):
        for q in chosen:
            for forward in passing[q]:
                forward.wait_recv()
                forwards.append(forward)
            m, d, low, size = pieces[q]
            base = low + (HALO - DIRECT, HALO + rows)[d]
            for n in range(m * cores, (m + 1) * cores):
                for to in (n, n + strips):
                    if to < strips + 2:
                        for j in range(lays):
                            field[j, to, base : base + size, :] = land[d, n, j, low : low + size, :]

    def take_rims():
        for d in range(2):
            rims[d].wait_recv()
            for k, p in enumerate(partners):
                forward = pltpu.make_async_remote_copy(
                    src_ref=rim_land.at[d, core],
                    dst_ref=rim_land.at[d, core],
                    send_sem=fesend.at[d, k],
                    recv_sem=ferecv.at[d, k],
                    device_id={"star": p},
                    device_id_type=MESH,
                )
                forward.start()
                forwards.append(forward)
        for forward in forwards[-2 * len(partners) :]:
            forward.wait_recv()
        for d, base in enumerate((HALO - DEPTH, HALO + rows + DIRECT)):
            for m in range(steps):
                for j in range(lays):
                    e = m * lays + j
                    at = slice(e % PACK * EXTRA, (e % PACK + 1) * EXTRA)
                    for c in range(cores):
                        n = m * cores + c
                        for to in (n, n + strips):
                            if to < strips + 2:
                                field[j, to, base : base + EXTRA, :] = rim_land[d, c, e // PACK, at, :]

    def own(u, chosen, unroll=1):
        k, w = divmod(u, units)
        compute(u, to_share(w), chosen, unroll)

    def arrived(w):
        for q, copy in enumerate(swaps):
            if q % units == w:
                copy.wait_recv()

    whole = list(range(parts))
    done = 0
    def pair(n):
        return [2 * n, 2 * n + 1]

    def finish_unit(u):
        k, w = divmod(u, units)
        if k < blocks - 1:
            compute(u, to_outbox(u), whole)
            copy = pltpu.make_async_remote_copy(
                src_ref=outbox.at[u],
                dst_ref=inbox.at[k, w],
                send_sem=xsend.at[u],
                recv_sem=xrecv.at[u],
                device_id={"layer": peers[k]},
                device_id_type=MESH,
            )
            copy.start()
            swaps.append(copy)
        else:
            own(u, whole)
            arrived(w)
            if (w + 1) % group == 0:
                slope_all([w // group], whole)

    def slope_all(chosen, some):
        project(slope_parts([(c, p) for c in chosen for p in some]))

    late = []
    for m in range(full):
        send_on(pair(m))
        take(pair(m))
        if m == 0:
            take_rims()
            fetch_matrix()
        have = (m + 1) * cores
        while done < units * blocks and (
            have == strips or done * unit + unit + 2 <= have
        ):
            finish_unit(done)
            if have < strips:
                move(done)
            else:
                late.append(done)
            done += 1
    if split:
        middle, rest = whole[1:-1], [whole[0], whole[-1]]
        have = (steps - 1) * cores
        soon = [u for u in range(done, units * blocks) if u * unit + unit + 2 <= have]
        late = [u for u in range(done, units * blocks) if u not in soon]
        soon_chunks, late_chunks = ([u % units for u in some] for some in (soon, late))
        near_soon, far_soon, near_late, far_late = (pair(full + n) for n in range(4))
        send_on(near_soon)
        take(near_soon)
        for u in soon:
            own(u, middle, True)
            arrived(u % units)
        slope_all(soon_chunks, middle)
        send_on(far_soon)
        take(far_soon)
        for u in soon:
            own(u, rest, True)
        slope_all(soon_chunks, rest)
        send_on(near_late)
        for u in soon:
            move(u)
        take(near_late)
        for u in late:
            own(u, middle, True)
            arrived(u % units)
        send_on(far_late)
        slope_all(late_chunks, middle)
        take(far_late)
        for u in late:
            own(u, rest, True)
        slope_all(late_chunks, rest)
    near_copies = []
    for k, peer in enumerate(near_peers):
        copy = pltpu.make_async_remote_copy(
            src_ref=total_terms,
            dst_ref=near.at[me],
            send_sem=nsend.at[k],
            recv_sem=nrecv.at[k],
            device_id=peer,
            device_id_type=MESH,
        )
        copy.start()
        near_copies.append(copy)
    near[me] = total_terms[...]
    for u in late:
        move(u)
    for copy in near_copies:
        copy.wait_recv()
    total = near[0]
    for k in range(1, count):
        total = total + near[k]
    far[tile] = total
    far_copies = []
    toward = jnp.where(2 * tile < tiles, 1, tiles - 1)
    for k in range(tiles - 1, 0, -1):
        copy = pltpu.make_async_remote_copy(
            src_ref=far.at[tile],
            dst_ref=far.at[tile],
            send_sem=fsend.at[k - 1],
            recv_sem=frecv.at[tile],
            device_id={"tile": lax.rem(tile + toward * k, tiles)},
            device_id_type=MESH,
        )
        copy.start()
        far_copies.append(copy)
    for copy in sends + rims + forwards + swaps + near_copies:
        copy.wait_send()
    for copy in far_copies:
        copy.wait_send()
    for k in range(1, tiles):
        source = lax.rem(tile + k, tiles)
        pltpu.make_async_remote_copy(
            src_ref=far.at[source],
            dst_ref=far.at[source],
            send_sem=fsend.at[k - 1],
            recv_sem=frecv.at[source],
            device_id={"tile": source},
            device_id_type=MESH,
        ).wait_recv()
    total = far[0]
    for k in range(1, tiles):
        total = total + far[k]
    commands[...] = 2.0 * total[0, :] - before[...]


def tables(block, block_subs, taps, depth, chunks, lanes):
    def block_diagonal(count, piece):
        return np.kron(np.eye(count), piece)

    index = np.arange(PIX)
    gap = index[:, None] - index[None, :]
    angle = np.where(gap == 0, 1, gap) * (math.pi / PAD)
    sign = np.where(gap % 2 == 0, 1.0, -1.0)
    table = np.where(gap == 0, 0.0, PIX * sign * np.cos(angle) / np.sin(angle))
    alternate = np.where(index % 2 == 0, 1.0, -1.0)
    def split(t):
        high = np.asarray(t.astype(jnp.bfloat16), np.float64)
        return high, t - high

    row_high, row_low = split(block_diagonal(block_subs, 2.0 * table))
    row_alt = np.pad(block_diagonal(block_subs, alternate[None, :]), ((0, -block_subs % 16), (0, 0)))
    none, thin = np.zeros_like(row_high), np.zeros_like(row_alt)
    row_all = np.block([
        [row_high, row_high, none, none],
        [row_low, none, none, none],
        [thin, thin, row_alt, row_alt],
        [row_alt, row_alt, thin, thin],
    ])
    ends = np.zeros((2, PIX, PIX))
    for n in range(2):
        ends[n, :, n] = 4.0 * alternate
    count = block // PIX
    col_high, col_low = split(block_diagonal(count, 2.0 * table.T))
    alt_a, alt_b = (block_diagonal(count, end) for end in ends)
    col_all = np.concatenate([col_high, col_high, col_low, alt_a, alt_a, alt_b, alt_b], axis=0)
    fold = np.zeros((taps, lanes // depth, depth))
    for k in range(taps):
        fold[k, :, k] = 1.0
    fold = fold.reshape(taps, lanes)
    gather = np.repeat(fold, PIX, axis=0)
    spread = np.zeros((chunks, chunks * taps, lanes))
    for w in range(chunks):
        spread[w, w * taps : (w + 1) * taps] = fold
    return tuple(jnp.asarray(t.astype(jnp.bfloat16)) for t in (row_all, col_all, gather, spread))


def stay(*arrays):
    return [pltpu.with_memory_space_constraint(x, pltpu.HBM) for x in arrays]


def frame(scalars, screens, amplitude, valid, previous, matrix):
    tiles, blocks, cores = (lax.axis_size(n) for n in ("tile", "layer", "star"))
    lays, rows, cols = screens.shape
    stars, _, subs, sub_cols, commands = matrix.shape
    strips, per_block, unit, units, group = plan(rows, cols, blocks)
    chunks = units // group
    width = group * unit * LANES
    taps = sub_cols // chunks
    depth = -(-taps // 16) * 16
    parts, inner, split = row_parts(rows, cols, blocks, cores)
    part_subs = subs // parts
    slots = stars
    while slots * part_subs % 8:
        slots += 1
    lanes = 2 * slots * part_subs * depth
    pieces = 2 * (strips // cores) + (4 if split else 0)
    rim_tiles = -(-(strips // cores) * lays // PACK)
    block = 2 * LANES if width % (2 * LANES) == 0 else LANES
    consts = tables(block, stars * part_subs, taps, depth, chunks, lanes)
    count = blocks * cores
    dma = pltpu.SemaphoreType.DMA
    bf16, f32 = jnp.bfloat16, jnp.float32
    piece = (stars, rows, unit * LANES)
    return pl.pallas_call(
        functools.partial(frame_kernel, tiles, cores, blocks, stars),
        out_shape=(
            pltpu.VMEM((lays, rows, cols), f32),
            pltpu.VMEM((stars, subs, 2, sub_cols), f32),
            pltpu.VMEM((commands,), f32),
        ),
        in_specs=[HBM] * (len(scalars) + 5 + len(consts)),
        out_specs=(VMEM, VMEM, VMEM),
        scratch_shapes=[pltpu.SMEM(t.shape, t.dtype) for t in scalars]
        + [
            pltpu.VMEM((lays, strips + 2, rows + 2 * HALO, LANES), f32),
            pltpu.VMEM((2, strips, lays, DIRECT, LANES), f32),
            pltpu.VMEM((2, rim_tiles, 8, LANES), f32),
            pltpu.VMEM((2, cores, rim_tiles, 8, LANES), f32),
            pltpu.VMEM((units * (blocks - 1),) + piece, f32),
            pltpu.VMEM((blocks - 1, units) + piece, f32),
            pltpu.VMEM((units,) + piece, f32),
            pltpu.VMEM(amplitude.shape, f32),
            pltpu.VMEM(valid.shape, valid.dtype),
            pltpu.VMEM(previous.shape, f32),
            pltpu.VMEM((chunks, parts, 2, slots, part_subs, depth, commands), bf16),
        ]
        + [pltpu.VMEM(t.shape, bf16) for t in consts]
        + [
            pltpu.VMEM((chunks, parts, 2 * slots * part_subs, lanes), f32),
            pltpu.VMEM(amplitude.shape, f32),
            pltpu.VMEM((4, stars * rows // parts, width), f32),
            pltpu.VMEM((4, 4 * stars * rows // parts, width), bf16),
            pltpu.VMEM((4, 2 * slots * part_subs, width), f32),
            pltpu.VMEM((1, commands), f32),
            pltpu.VMEM((count, 1, commands), f32),
            pltpu.VMEM((tiles, 1, commands), f32),
            dma((pieces,)),
            dma((pieces,)),
            dma((pieces, cores - 1)),
            dma((pieces, cores - 1)),
            dma((2,)),
            dma((2,)),
            dma((2, cores - 1)),
            dma((2, cores - 1)),
            dma((units * (blocks - 1),)),
            dma((units * (blocks - 1),)),
            dma((strips + 2,)),
            dma((7 + len(scalars) + chunks * parts * 2,)),
            dma((count - 1,)),
            dma((count - 1,)),
            dma((tiles - 1,)),
            dma((tiles,)),
        ],
        compiler_params=pltpu.CompilerParams(
            collective_id=0, has_side_effects=True, vmem_limit_bytes=48 * 2**20
        ),
        name="frame",
    )(*stay(*scalars, screens, amplitude, valid, previous, matrix, *consts))


def horner(z, first, *rest):
    value = first
    for c in rest:
        value = value * z + c
    return value


def sine_cosine(x):
    turns = jnp.floor(x * (1.0 / math.pi) + 0.5)
    r = x - turns * 3.140625
    r = r - turns * 9.67653589793e-4
    z = r * r
    s = r + r * (z * horner(z, 2.63541936e-6, -1.98230239e-4, 8.33324557e-3, -1.66666661e-1))
    c = 1.0 + z * horner(
        z, -2.63066288e-7, 2.47750852e-5, -1.38886609e-3, 4.166666e-2, -0.5
    )
    return s, c, turns


def halves(x):
    high = x.astype(jnp.bfloat16)
    return high, (x - high.astype(jnp.float32)).astype(jnp.bfloat16)


def product(x, y):
    return jnp.dot(x, y, preferred_element_type=jnp.float32)

def finish_kernel(*refs):
    sems, count = refs[-1], len(refs) // 2
    copies = []
    for n in range(count):
        source, target = refs[n], refs[count + n]
        whole = n > 0
        half = 0 if whole else source.shape[1] // 2
        cuts = [None] if whole else [
            (j, pl.ds(i * half, half)) for j in range(source.shape[0]) for i in range(2)
        ]
        for cut in cuts:
            pair = (source, target) if whole else (source.at[cut], target.at[cut])
            copies.append(pltpu.make_async_copy(*pair, sems.at[len(copies)]))
            copies[-1].start()
    for copy in copies:
        copy.wait()


def finish(*arrays):
    return pl.pallas_call(
        finish_kernel,
        out_shape=[jax.ShapeDtypeStruct(x.shape, x.dtype) for x in arrays],
        in_specs=[ANY] * len(arrays),
        out_specs=[ANY] * len(arrays),
        scratch_shapes=[pltpu.SemaphoreType.DMA((2 * arrays[0].shape[0] + len(arrays) - 1,))],
        compiler_params=pltpu.CompilerParams(vmem_limit_bytes=2**20),
        name="finish",
    )(*arrays)


def body(
    screens,
    layer_weight,
    wind_row,
    wind_col,
    foot_row,
    foot_col,
    frac_row,
    frac_col,
    amplitude,
    valid,
    recon_matrix,
    prev_recon,
):
    scalars = (layer_weight, wind_row, wind_col, foot_row, foot_col, frac_row, frac_col)
    shifted, slopes, commands = finish(
        *frame(scalars, screens, amplitude, valid, prev_recon, recon_matrix)
    )
    return shifted, jnp.transpose(slopes, (0, 2, 1, 3)), commands


def solution(mesh):
    return jax.shard_map(
        body,
        mesh=mesh,
        in_specs=(
            P(("runs", "layer"), "tile", None),
            P(("runs", "layer")),
            P("runs"),
            P("runs"),
            P(),
            P(),
            P(),
            P(),
            P("tile", "layer"),
            P("tile", "layer"),
            P("star", None, "tile", "layer", None),
            P("runs"),
        ),
        out_specs=(
            P(("runs", "layer"), "tile", None),
            P(("runs", "star"), None, "tile", "layer"),
            P("runs"),
        ),
        check_vma=False,
    )
```
